32 devices in a mesh: groups: 2 (over y), space: 4 (over z), chan: 2 (over x), rep: 2 (over core).
Axes of the slice: x: 2, y: 2, z: 4, core: 2. Of those that a mesh axis runs over, the one named last changes fastest.
Arguments:
- volume: bfloat16 [4, 8, 32, 8, 128], P(('groups', 'rep'), 'space', 'chan'), parts along dimension 0, may hold values from -6 to 6
- early_weight: bfloat16 [3, 3, 3, 128, 128], replicated, may hold values from -0.109375 to 0.109375
- late_weight: bfloat16 [3, 3, 3, 128, 512], P(None, None, None, None, 'chan'), may hold values from -0.109375 to 0.109375
- cotangent: bfloat16 [4, 4, 16, 4, 512], P(('groups', 'rep'), 'space', None, None, 'chan'), parts along dimension 0, may hold values from -6 to 6
Outputs:
- grad_early: bfloat16 [6, 3, 3, 128, 128], P('groups'), parts along dimension 0
- grad_late: bfloat16 [6, 3, 3, 128, 512], P('groups', None, None, None, 'chan'), parts along dimension 0
- grad_volume: bfloat16 [4, 8, 32, 8, 128], P(('groups', 'rep'), 'space', 'chan'), parts along dimension 0
The draws below stay inside these ranges and needn't reach their ends.
There are 2 independent parts, one for each index of `groups`. The reference program is written for one: setup_inputs(seed, part) draws one part's arguments, and reference() takes and returns one part's arrays. A program takes and returns all parts, laid end to end along the dimension named above; an argument that names none is the same for every part. Nothing has to cross between parts.
All inputs are finite; a program needn't handle non-finite values.
Results may differ from the reference program's by a relative error of at most 0.0065.
Values may be sent and summed in bfloat16 or wider, within the bound.
No kernel may reach another device: no remote copies, remote signals or barrier semaphores. Data moves between devices by JAX's collectives and lax.ppermute only.
A program may use at most 64 MiB of HBM per device.

```python
import jax
import jax.numpy as jnp
from jax import lax

CE = 128
CL = 512
ZLEN = 8
NS = 2
GX = 8
GY = 32
LX = 4
LY = 16
LZ = 4


def levels(own_key, dims, pieces, least, largest):
    factor_of, own = 1.0, jax.random.fold_in(own_key, 6)
    for dim, parts in pieces:
        heights = jnp.exp(jax.random.uniform(jax.random.fold_in(own, dim), (parts,), jnp.float32, least / len(pieces), largest / len(pieces)))
        factor_of = factor_of * jnp.repeat(heights, dims[dim] // parts).reshape([-1 if axis == dim else 1 for axis in range(len(dims))])
    return factor_of


def centred(own_key, dims, width, bound, pieces=(), held_as=jnp.bfloat16):
    loudness = levels(own_key, dims, pieces, -0.22, 0.18) if pieces else 1.0
    result = jax.random.normal(own_key, dims, jnp.float32) * width * loudness
    return jnp.minimum(jnp.maximum(result, -bound), bound).astype(held_as)


def setup_inputs(seed: int = 0, part: int = 0) -> dict:
    keys = jax.random.split(jax.random.key(seed), 5)
    part_splits = jax.random.split(jax.random.fold_in(keys[4], part), 5)
    return {
        "volume": centred(part_splits[0], (NS, GX, GY, ZLEN, CE), 1.0, 6.0, ((0, 2), (1, 4), (2, 2))),
        "early_weight": centred(keys[1], (3, 3, 3, CE, CE), (27 * CE) ** -0.5, 0.109375),
        "late_weight": centred(keys[2], (3, 3, 3, CE, CL), (27 * CE) ** -0.5, 0.109375, ((4, 2),)),
        "cotangent": centred(part_splits[3], (NS, LX, LY, LZ, CL), 1.0, 6.0, ((0, 2), (1, 4), (4, 2))),
    }


def gelu_tanh(value):
    return jax.nn.gelu(value, approximate=True)

def conv_same(field, weight):
    return lax.conv_general_dilated(field, weight, (1, 1, 1), 'SAME', dimension_numbers=('NDHWC', 'DHWIO', 'NDHWC'), precision=lax.Precision.HIGHEST)

def pool_cells(field):
    s, x, y, z, c = field.shape
    return lax.optimization_barrier(jnp.mean(field.reshape(s, x // 2, 2, y // 2, 2, z // 2, 2, c), axis=(2, 4, 6)))

def spread_cells(field):
    s, x, y, z, c = field.shape
    wide = jnp.broadcast_to(field[:, :, None, :, None, :, None, :], (s, x, 2, y, 2, z, 2, c))
    return wide.reshape(s, 2 * x, 2 * y, 2 * z, c) * 0.125

def reference(volume, early_weight, late_weight, cotangent):
    volume_f = volume.astype(jnp.float32)
    early_f = early_weight.astype(jnp.float32)
    late_f = late_weight.astype(jnp.float32)
    pre_early = conv_same(volume_f, early_f)
    pooled = pool_cells(gelu_tanh(pre_early)).astype(jnp.bfloat16)
    pooled_f = pooled.astype(jnp.float32)
    pre_late = conv_same(pooled_f, late_f)
    gelu_late = jax.vjp(gelu_tanh, pre_late)[1]
    delta_late = gelu_late(cotangent.astype(jnp.float32))[0].astype(jnp.bfloat16)
    late_pull = jax.vjp(conv_same, pooled_f, late_f)[1]
    back_pooled, late_sum = late_pull(delta_late.astype(jnp.float32))
    gelu_early = jax.vjp(gelu_tanh, pre_early)[1]
    delta_early = gelu_early(spread_cells(back_pooled))[0].astype(jnp.bfloat16)
    early_pull = jax.vjp(conv_same, volume_f, early_f)[1]
    volume_grad, early_sum = early_pull(delta_early.astype(jnp.float32))
    scale = (NS * LX * LY * LZ) ** (-0.5)
    return ((early_sum * scale).astype(jnp.bfloat16), (late_sum * scale).astype(jnp.bfloat16), volume_grad.astype(jnp.bfloat16))
```

```python
import functools
import math

import jax
import jax.numpy as jnp
from jax import lax
from jax.experimental import pallas as pl
from jax.experimental.pallas import tpu as pltpu
from jax.sharding import PartitionSpec as P

BF = jnp.bfloat16
F32 = jnp.float32
VMEM_BYTES = 56 * 2**20
GATHER_BLOCKS = 8


def padded_2(block, sides, width):
    for axis, dim in sides:
        count = lax.axis_size(axis)
        forward = [(i, i + 1) for i in range(count - 1)]
        backward = [(target, source) for source, target in forward]
        low = lax.ppermute(
            lax.slice_in_dim(block, block.shape[dim] - width, None, axis=dim), axis, forward
        )
        high = lax.ppermute(lax.slice_in_dim(block, 0, width, axis=dim), axis, backward)
        block = jnp.concatenate([low, block, high], axis=dim)
    return block


def gelu_tanh(value):
    return jax.nn.gelu(value, approximate=True)


def conv_padded(padded, weight):
    depth = padded.shape[1] - 2
    height = padded.shape[2] - 2
    length = padded.shape[3] - 2
    total = None
    for first in range(3):
        for second in range(3):
            for third in range(3):
                window = padded[
                    :, first : first + depth, second : second + height, third : third + length
                ]
                term = jnp.einsum(
                    "sxyzc,co->sxyzo",
                    window,
                    weight[first, second, third],
                    preferred_element_type=jnp.float32,
                )
                total = term if total is None else total + term
    return total


def kernel_grad(padded, delta):
    depth = delta.shape[1]
    height = delta.shape[2]
    length = delta.shape[3]
    planes = []
    for first in range(3):
        for second in range(3):
            for third in range(3):
                window = padded[
                    :, first : first + depth, second : second + height, third : third + length
                ]
                planes.append(
                    jnp.einsum("sxyzc,sxyzo->co", window, delta, preferred_element_type=jnp.float32)
                )
    stacked = jnp.stack(planes, axis=0)
    return stacked.reshape((3, 3, 3) + stacked.shape[1:])


def flipped(weight):
    return jnp.swapaxes(weight[::-1, ::-1, ::-1], 3, 4)


def pad_dims(field, dims):
    widths = [(1, 1) if place in dims else (0, 0) for place in range(field.ndim)]
    return jnp.pad(field, widths)


def pool_cells(field):
    s, x, y, z, c = field.shape
    return jnp.mean(field.reshape(s, x // 2, 2, y // 2, 2, z // 2, 2, c), axis=(2, 4, 6))


def spread_cells(field):
    s, x, y, z, c = field.shape
    wide = jnp.broadcast_to(field[:, :, None, :, None, :, None, :], (s, x, 2, y, 2, z, 2, c))
    return wide.reshape(s, 2 * x, 2 * y, 2 * z, c) * 0.125


def late_layer(joined, late_weight, cotangent):
    rim = padded_2(joined, (("space", 1),), 1)
    late_pad = pad_dims(rim, (2, 3))
    pre_late = conv_padded(late_pad, late_weight)
    delta_late = jax.vjp(gelu_tanh, pre_late)[1](cotangent.astype(jnp.float32))[0].astype(
        jnp.bfloat16
    )
    late_part = kernel_grad(late_pad, delta_late)
    delta_rim = padded_2(delta_late, (("space", 1),), 1)
    back_partial = conv_padded(pad_dims(delta_rim, (2, 3)), flipped(late_weight))
    return (back_partial, late_part)


def per_device(volume, early_weight, late_weight, cotangent):
    count = (
        cotangent.shape[0]
        * lax.axis_size("rep")
        * cotangent.shape[1]
        * lax.axis_size("space")
        * cotangent.shape[2]
        * cotangent.shape[3]
    )
    scale = 1.0 / math.sqrt(count)
    haloed = padded_2(volume, (("space", 1), ("chan", 2)), 1)
    padded_in = pad_dims(haloed, (3,))
    pre_early = conv_padded(padded_in, early_weight)
    pooled = pool_cells(gelu_tanh(pre_early)).astype(jnp.bfloat16)
    joined = lax.all_gather(pooled, "chan", axis=2, tiled=True)
    back_partial, late_part = late_layer(joined, late_weight, cotangent)
    back_rows = lax.psum_scatter(back_partial, "chan", scatter_dimension=2, tiled=True)
    delta_early = jax.vjp(gelu_tanh, pre_early)[1](spread_cells(back_rows))[0].astype(jnp.bfloat16)
    early_part = kernel_grad(padded_in, delta_early)
    delta_halo = padded_2(delta_early, (("space", 1), ("chan", 2)), 1)
    grad_volume = conv_padded(pad_dims(delta_halo, (3,)), flipped(early_weight)).astype(
        jnp.bfloat16
    )
    early_total = lax.psum(early_part, ("space", "chan", "rep"))
    grad_early = (early_total * scale).astype(jnp.bfloat16)
    late_total = lax.psum(late_part, ("space", "rep"))
    grad_late = (late_total * scale).astype(jnp.bfloat16)
    return (grad_early, grad_late, grad_volume)


NT = (((1,), (1,)), ((), ()))


def gelu_and_slope(v):
    k = 0.7978845608028654
    sq = v * v
    t = jnp.tanh(k * (v + 0.044715 * (v * sq)))
    half = 0.5 * (1.0 + t)
    return v * half, half + 0.5 * v * (1.0 - t * t) * (k * (1.0 + 0.134145 * sq))


def depth_of(rows, period):
    return lax.broadcasted_iota(jnp.int32, (rows, 128), 0) % period


def shifted(ref, lead, start, rows, cell, period, step):
    dy, dz = step
    got = ref[lead + (pl.ds(start + dy * period + dz, rows), slice(None))]
    if dz == 0:
        return got
    lanes = got.shape[1] // 128
    edge = (cell == 0) if dz < 0 else (cell == period - 1)
    edge = jnp.concatenate([edge] * lanes, axis=1) if lanes > 1 else edge
    return jnp.where(edge, 0.0, got)


STEPS = [(b, c) for b in (-1, 0, 1) for c in (-1, 0, 1)]


def prep_kernel(we_ref, wcat_ref, wt_ref):
    for n in range(9):
        b, c = divmod(n, 3)
        for a in range(3):
            w = we_ref[a, b, c]
            wcat_ref[pl.ds(n * 128, 128), pl.ds(a * 128, 128)] = w
            wt_ref[a, pl.ds(n * 128, 128), :] = w.astype(F32).T.astype(BF)


def forward_kernel(
    pos_ref, *refs, nk, nj, dims
):
    gx, gy, gz, lx, ly, lz, bx, by = dims
    blocks = refs[: nk * nj]
    wcat_ref, wl_ref = refs[nk * nj : nk * nj + 2]
    col_ref, slope_ref, pd_ref, back_ref = refs[nk * nj + 2 : nk * nj + 6]
    vol_ref, p_ref, h_ref, pool_ref, lcol_ref, dl_ref = refs[nk * nj + 6 :]
    k, j = pos_ref[0], pos_ref[1]
    plane, lplane = gy * gz, ly * lz
    brows = by * gz
    cl = wl_ref.shape[-1]
    crow = bx // 2 * lplane

    vol_ref[:, pl.ds(0, 16), :] = jnp.zeros((gx, 16, 128), F32)
    vol_ref[:, pl.ds(16 + plane, 16), :] = jnp.zeros((gx, 16, 128), F32)
    for dj in range(nj):
        for dk in range(nk):
            src = blocks[dj * nk + dk]
            kk = lax.rem(k + nk - dk, nk)
            jj = lax.rem(j + nj - dj, nj)
            row = pl.multiple_of(16 + jj * brows, 8)
            for q in range(bx):
                vol_ref[kk * bx + q, pl.ds(row, brows), :] = src[pl.ds(q * brows, brows), :].astype(F32)

    cell = depth_of(plane, gz)
    for x in range(gx):
        for n, step in enumerate(STEPS):
            col_ref[pl.ds(x * plane, plane), pl.ds(n * 128, 128)] = shifted(
                vol_ref, (x,), 16, plane, cell, gz, step
            ).astype(BF)

    p_ref[...] = jnp.dot(col_ref[...], wcat_ref[...], preferred_element_type=F32)

    for lq in range(lx):
        pair = None
        for x in (2 * lq, 2 * lq + 1):
            pre = p_ref[pl.ds(x * plane, plane), pl.ds(128, 128)]
            if x > 0:
                pre = pre + p_ref[pl.ds((x - 1) * plane, plane), pl.ds(0, 128)]
            if x < gx - 1:
                pre = pre + p_ref[pl.ds((x + 1) * plane, plane), pl.ds(256, 128)]
            h, slope = gelu_and_slope(pre)
            slope_ref[pl.ds(x * plane, plane), :] = slope
            pair = h if pair is None else pair + h
        wide = pair.reshape(ly, 2, gz, 128)
        h_ref[...] = (wide[:, 0] + wide[:, 1]).reshape(ly * gz, 128)
        pooled = (h_ref[pl.ds(0, lplane, stride=2), :] + h_ref[pl.ds(1, lplane, stride=2), :]) * 0.125
        pooled = pooled.astype(BF)
        pd_ref[pl.ds(lq * lplane, lplane), pl.ds(0, 128)] = pooled
        pool_ref[lq, pl.ds(0, 8), :] = jnp.zeros((8, 128), F32)
        pool_ref[lq, pl.ds(8 + lplane, 8), :] = jnp.zeros((8, 128), F32)
        pool_ref[lq, pl.ds(8, lplane), :] = pooled.astype(F32)

    lcell = depth_of(lplane, lz)
    for x in range(lx):
        for n, step in enumerate(STEPS):
            lcol_ref[pl.ds(x * lplane, lplane), pl.ds(n * 128, 128)] = shifted(
                pool_ref, (x,), 8, lplane, lcell, lz, step
            ).astype(BF)
    lcol = lcol_ref[...]
    parts = [
        jnp.dot(lcol, wl_ref[a].reshape(9 * 128, cl), preferred_element_type=F32) for a in range(3)
    ]
    for x in range(lx):
        dl_ref[x, pl.ds(0, 8), :] = jnp.zeros((8, cl), F32)
        dl_ref[x, pl.ds(8 + lplane, 8), :] = jnp.zeros((8, cl), F32)
    zero = jnp.zeros((lplane, cl), F32)
    pre = parts[1]
    pre = pre + jnp.concatenate([zero, parts[0][:-lplane]], axis=0)
    pre = pre + jnp.concatenate([parts[2][lplane:], zero], axis=0)
    slope = gelu_and_slope(pre)[1]
    for dk in range(nk):
        src = blocks[dk]
        kk = lax.rem(k + nk - dk, nk)
        start = pl.multiple_of(kk * crow, 8)
        for g in range(cl // 128):
            h_ref2 = src[pl.ds(bx * brows + g * crow, crow), :].astype(F32)
            p_ref[pl.ds(start, crow), pl.ds(g * 128, 128)] = h_ref2
    cot = p_ref[pl.ds(0, lx * lplane), pl.ds(0, cl)]
    delta = (cot * slope).astype(BF)
    pd_ref[:, pl.ds(128, cl)] = delta
    wide = delta.astype(F32)
    for x in range(lx):
        dl_ref[x, pl.ds(8, lplane), :] = wide[x * lplane : (x + 1) * lplane]
    total = None
    for n, (b, c) in enumerate(STEPS):
        part = jnp.concatenate(
            [shifted(dl_ref, (x,), 8, lplane, lcell, lz, (-b, -c)) for x in range(lx)], axis=0
        ).astype(BF)
        w = wl_ref[:, b + 1, c + 1].reshape(3 * 128, cl)
        term = lax.dot_general(part, w, NT, preferred_element_type=F32)
        total = term if total is None else total + term
    zero = jnp.zeros((lplane, 128), F32)
    back = total[:, 128:256]
    back = back + jnp.concatenate([total[lplane:, 0:128], zero], axis=0)
    back = back + jnp.concatenate([zero, total[:-lplane, 256:384]], axis=0)
    back_ref[...] = back


def late_grad_kernel(mine_ref, other_ref, out_ref, pool_ref, lcol_ref, *, dims, scale):
    lx, ly, lz = dims
    lplane = ly * lz
    rows = lx * lplane
    lcell = depth_of(lplane, lz)
    pool_ref[...] = jnp.zeros(pool_ref.shape, F32)
    for s, ref in enumerate((mine_ref, other_ref)):
        for x in range(lx):
            pool_ref[s, x + 1, pl.ds(8, lplane), :] = ref[pl.ds(x * lplane, lplane), pl.ds(0, 128)].astype(F32)
        for x in range(lx + 2):
            for n, step in enumerate(STEPS):
                lcol_ref[s, pl.ds(x * lplane, lplane), pl.ds(n * 128, 128)] = shifted(
                    pool_ref, (s, x), 8, lplane, lcell, lz, step
                ).astype(BF)
    cl = mine_ref.shape[1] - 128
    delta = jnp.concatenate([mine_ref[:, pl.ds(128, cl)], other_ref[:, pl.ds(128, cl)]], axis=0)
    for a in range(3):
        left = jnp.concatenate([lcol_ref[s, pl.ds(a * lplane, rows), :] for s in (0, 1)], axis=0)
        got = lax.dot_general(left, delta, (((0,), (0,)), ((), ())), preferred_element_type=F32)
        out_ref[pl.ds(a * 9 * 128, 9 * 128), :] = (got * scale).astype(BF)


def early_back_kernel(
    pos_ref, mine_ref, other_ref, slope_ref, col_ref, wt_ref, grad_ref, gv_ref,
    wide_ref, d_ref, dt_ref, win_ref, vcol_ref, *, dims
):
    gx, gy, gz, lx, ly, lz, bx, by = dims
    plane, lplane = gy * gz, ly * lz
    k, j = pos_ref[0], pos_ref[1]
    brows = by * gz
    for q in (0, gx + 1):
        d_ref[q] = jnp.zeros(d_ref.shape[1:], F32)
    d_ref[:, pl.ds(0, 16), :] = jnp.zeros((gx + 2, 16, 128), F32)
    d_ref[:, pl.ds(16 + plane, 16), :] = jnp.zeros((gx + 2, 16, 128), F32)
    dt_ref[:, pl.ds(0, plane)] = jnp.zeros((128, plane), BF)
    dt_ref[:, pl.ds((gx + 1) * plane, plane)] = jnp.zeros((128, plane), BF)
    back = (mine_ref[...] + other_ref[...].astype(F32)) * 0.125
    wide_ref[pl.ds(0, lx * lplane, stride=2), :] = back
    wide_ref[pl.ds(1, lx * lplane, stride=2), :] = back
    for lq in range(lx):
        rows = wide_ref[pl.ds(lq * ly * gz, ly * gz), :].reshape(ly, 1, gz, 128)
        rows = jnp.broadcast_to(rows, (ly, 2, gz, 128)).reshape(plane, 128)
        for x in (2 * lq, 2 * lq + 1):
            delta = (rows * slope_ref[pl.ds(x * plane, plane), :]).astype(BF).astype(F32)
            d_ref[x + 1, pl.ds(16, plane), :] = delta
            dt_ref[:, pl.ds((x + 1) * plane, plane)] = delta.T.astype(BF)
    left = jnp.concatenate([dt_ref[:, pl.ds((2 - a) * plane, gx * plane)] for a in range(3)], axis=0)
    got = jnp.dot(left, col_ref[...], preferred_element_type=F32)
    for a in range(3):
        for n in range(9):
            grad_ref[pl.ds((a * 9 + n) * 128, 128), :] = got[
                a * 128 : (a + 1) * 128, n * 128 : (n + 1) * 128
            ].T.astype(grad_ref.dtype)
    cell = depth_of(brows, gz)
    row = pl.multiple_of(j * brows, 8)
    for q in range(bx + 2):
        win_ref[q] = d_ref[k * bx + q, pl.ds(row, brows + 32), :]
    for q in range(bx + 2):
        for n, (b, c) in enumerate(STEPS):
            vcol_ref[pl.ds(q * brows, brows), pl.ds(n * 128, 128)] = shifted(
                win_ref, (q,), 16, brows, cell, gz, (-b, -c)
            ).astype(BF)
    total = None
    for a in range(3):
        term = jnp.dot(vcol_ref[pl.ds((2 - a) * brows, bx * brows), :], wt_ref[a], preferred_element_type=F32)
        total = term if total is None else total + term
    gv_ref[...] = total.astype(BF)


def finish_kernel(mine_ref, other_ref, out_ref, *, scale):
    out_ref[...] = ((mine_ref[...].astype(F32) + other_ref[...].astype(F32)) * scale).astype(BF)


def turned(value, axis, by):
    count = lax.axis_size(axis)
    return lax.ppermute(value, axis, [(i, (i + by) % count) for i in range(count)])


def call(kernel, outs, scratch, args, name, smem=0):
    specs = [pl.BlockSpec(memory_space=pltpu.SMEM)] * smem
    specs += [pl.BlockSpec(memory_space=pltpu.VMEM)] * (len(args) - smem)
    return pl.pallas_call(
        kernel,
        out_shape=outs,
        in_specs=specs,
        out_specs=[pl.BlockSpec(memory_space=pltpu.VMEM)] * len(outs),
        scratch_shapes=scratch,
        compiler_params=pltpu.CompilerParams(vmem_limit_bytes=VMEM_BYTES),
        name=name,
    )(*args)


def whole_sample(volume, early_weight, late_weight, cotangent):
    nk, nj, nr = (lax.axis_size(axis) for axis in ("space", "chan", "rep"))
    _, bx, by, gz, _ = volume.shape
    _, cx, ly, lz, cl = cotangent.shape
    gx, gy, lx = bx * nk, by * nj, cx * nk
    plane, lplane, brows = gy * gz, ly * lz, by * gz
    rows, lrows = gx * plane, lx * lplane
    scale = 1.0 / math.sqrt(nr * lrows)
    pos = jnp.stack([lax.axis_index("space"), lax.axis_index("chan")]).astype(jnp.int32)
    sds = jax.ShapeDtypeStruct

    cot = cotangent.reshape(cx * lplane, cl)
    payload = jnp.concatenate(
        [volume.reshape(bx * brows, 128)] + [cot[:, g : g + 128] for g in range(0, cl, 128)], axis=0
    )
    line = [payload] + [turned(payload, "space", dk) for dk in range(1, nk)]
    blocks = list(line)
    for dj in range(1, nj):
        blocks += [turned(block, "chan", dj) for block in line]

    wcat, wt = call(
        prep_kernel, [sds((9 * 128, 3 * 128), BF), sds((3, 9 * 128, 128), BF)], [], [early_weight], "prep"
    )
    dims = (gx, gy, gz, lx, ly, lz, bx, by)
    col, slope, pooled_delta, back = call(
        functools.partial(forward_kernel, nk=nk, nj=nj, dims=dims),
        [sds((rows, 9 * 128), BF), sds((rows, 128), F32), sds((lrows, 128 + cl), BF), sds((lrows, 128), F32)],
        [
            pltpu.VMEM((gx, plane + 32, 128), F32),
            pltpu.VMEM((rows, 3 * 128), F32),
            pltpu.VMEM((ly * gz, 128), F32),
            pltpu.VMEM((lx, lplane + 16, 128), F32),
            pltpu.VMEM((lrows, 9 * 128), BF),
            pltpu.VMEM((lx, lplane + 16, cl), F32),
        ],
        [pos] + blocks + [wcat, late_weight],
        "forward",
        smem=1,
    )
    back_other = turned(back.astype(BF), "chan", 1)
    pd_other = turned(pooled_delta, "rep", 1)
    (late,) = call(
        functools.partial(late_grad_kernel, dims=(lx, ly, lz), scale=scale),
        [sds((27 * 128, cl), BF)],
        [pltpu.VMEM((2, lx + 2, lplane + 16, 128), F32), pltpu.VMEM((2, (lx + 2) * lplane, 9 * 128), BF)],
        [pooled_delta, pd_other],
        "late_grad",
    )
    part, gv = call(
        functools.partial(early_back_kernel, dims=dims),
        [sds((27 * 128, 128), BF), sds((bx * brows, 128), BF)],
        [
            pltpu.VMEM((lx * ly * gz, 128), F32),
            pltpu.VMEM((gx + 2, plane + 32, 128), F32),
            pltpu.VMEM((128, (gx + 2) * plane), BF),
            pltpu.VMEM((bx + 2, brows + 32, 128), F32),
            pltpu.VMEM(((bx + 2) * brows, 9 * 128), BF),
        ],
        [pos, back, back_other, slope, col, wt],
        "early_back",
        smem=1,
    )
    part_other = turned(part, "rep", 1)
    (early,) = call(
        functools.partial(finish_kernel, scale=scale), [sds((27 * 128, 128), BF)], [], [part, part_other], "finish"
    )
    return (
        early.reshape(3, 3, 3, 128, 128),
        late.reshape(3, 3, 3, 128, cl),
        gv.reshape(1, bx, by, gz, 128),
    )


def solution(mesh):
    few = mesh.shape["space"] * mesh.shape["chan"] <= GATHER_BLOCKS
    alone = mesh.shape["rep"] == 2 and mesh.shape["chan"] == 2
    return jax.shard_map(
        whole_sample if few and alone else per_device,
        mesh=mesh,
        in_specs=(
            P(("groups", "rep"), "space", "chan", None, None),
            P(),
            P(None, None, None, None, "chan"),
            P(("groups", "rep"), "space", None, None, "chan"),
        ),
        out_specs=(
            P("groups", None, None, None, None),
            P("groups", None, None, None, "chan"),
            P(("groups", "rep"), "space", "chan", None, None),
        ),
        check_vma=False,
    )
```

```python
import functools
import math

import jax
import jax.numpy as jnp
from jax import lax
from jax.experimental import pallas as pl
from jax.experimental.pallas import tpu as pltpu
from jax.sharding import PartitionSpec as P

BF = jnp.bfloat16
F32 = jnp.float32
VMEM_BYTES = 24 * 2**20
GATHER_BLOCKS = 8


def padded_2(block, sides, width):
    for axis, dim in sides:
        count = lax.axis_size(axis)
        forward = [(i, i + 1) for i in range(count - 1)]
        backward = [(target, source) for source, target in forward]
        low = lax.ppermute(
            lax.slice_in_dim(block, block.shape[dim] - width, None, axis=dim), axis, forward
        )
        high = lax.ppermute(lax.slice_in_dim(block, 0, width, axis=dim), axis, backward)
        block = jnp.concatenate([low, block, high], axis=dim)
    return block


def gelu_tanh(value):
    return jax.nn.gelu(value, approximate=True)


def conv_padded(padded, weight):
    depth = padded.shape[1] - 2
    height = padded.shape[2] - 2
    length = padded.shape[3] - 2
    total = None
    for first in range(3):
        for second in range(3):
            for third in range(3):
                window = padded[
                    :, first : first + depth, second : second + height, third : third + length
                ]
                term = jnp.einsum(
                    "sxyzc,co->sxyzo",
                    window,
                    weight[first, second, third],
                    preferred_element_type=jnp.float32,
                )
                total = term if total is None else total + term
    return total


def kernel_grad(padded, delta):
    depth = delta.shape[1]
    height = delta.shape[2]
    length = delta.shape[3]
    planes = []
    for first in range(3):
        for second in range(3):
            for third in range(3):
                window = padded[
                    :, first : first + depth, second : second + height, third : third + length
                ]
                planes.append(
                    jnp.einsum("sxyzc,sxyzo->co", window, delta, preferred_element_type=jnp.float32)
                )
    stacked = jnp.stack(planes, axis=0)
    return stacked.reshape((3, 3, 3) + stacked.shape[1:])


def flipped(weight):
    return jnp.swapaxes(weight[::-1, ::-1, ::-1], 3, 4)


def pad_dims(field, dims):
    widths = [(1, 1) if place in dims else (0, 0) for place in range(field.ndim)]
    return jnp.pad(field, widths)


def pool_cells(field):
    s, x, y, z, c = field.shape
    return jnp.mean(field.reshape(s, x // 2, 2, y // 2, 2, z // 2, 2, c), axis=(2, 4, 6))


def spread_cells(field):
    s, x, y, z, c = field.shape
    wide = jnp.broadcast_to(field[:, :, None, :, None, :, None, :], (s, x, 2, y, 2, z, 2, c))
    return wide.reshape(s, 2 * x, 2 * y, 2 * z, c) * 0.125


def late_layer(joined, late_weight, cotangent):
    rim = padded_2(joined, (("space", 1),), 1)
    late_pad = pad_dims(rim, (2, 3))
    pre_late = conv_padded(late_pad, late_weight)
    delta_late = jax.vjp(gelu_tanh, pre_late)[1](cotangent.astype(jnp.float32))[0].astype(
        jnp.bfloat16
    )
    late_part = kernel_grad(late_pad, delta_late)
    delta_rim = padded_2(delta_late, (("space", 1),), 1)
    back_partial = conv_padded(pad_dims(delta_rim, (2, 3)), flipped(late_weight))
    return (back_partial, late_part)


def per_device(volume, early_weight, late_weight, cotangent):
    count = (
        cotangent.shape[0]
        * lax.axis_size("rep")
        * cotangent.shape[1]
        * lax.axis_size("space")
        * cotangent.shape[2]
        * cotangent.shape[3]
    )
    scale = 1.0 / math.sqrt(count)
    haloed = padded_2(volume, (("space", 1), ("chan", 2)), 1)
    padded_in = pad_dims(haloed, (3,))
    pre_early = conv_padded(padded_in, early_weight)
    pooled = pool_cells(gelu_tanh(pre_early)).astype(jnp.bfloat16)
    joined = lax.all_gather(pooled, "chan", axis=2, tiled=True)
    back_partial, late_part = late_layer(joined, late_weight, cotangent)
    back_rows = lax.psum_scatter(back_partial, "chan", scatter_dimension=2, tiled=True)
    delta_early = jax.vjp(gelu_tanh, pre_early)[1](spread_cells(back_rows))[0].astype(jnp.bfloat16)
    early_part = kernel_grad(padded_in, delta_early)
    delta_halo = padded_2(delta_early, (("space", 1), ("chan", 2)), 1)
    grad_volume = conv_padded(pad_dims(delta_halo, (3,)), flipped(early_weight)).astype(
        jnp.bfloat16
    )
    early_total = lax.psum(early_part, ("space", "chan", "rep"))
    grad_early = (early_total * scale).astype(jnp.bfloat16)
    late_total = lax.psum(late_part, ("space", "rep"))
    grad_late = (late_total * scale).astype(jnp.bfloat16)
    return (grad_early, grad_late, grad_volume)


NT = (((1,), (1,)), ((), ()))


def gelu_and_slope(v):
    k = 0.7978845608028654
    sq = v * v
    t = jnp.tanh(k * (v + 0.044715 * (v * sq)))
    half = 0.5 * (1.0 + t)
    return v * half, half + 0.5 * v * (1.0 - t * t) * (k * (1.0 + 0.134145 * sq))


def depth_of(rows, period):
    return lax.broadcasted_iota(jnp.int32, (rows, 128), 0) % period


def shifted(ref, lead, start, rows, cell, period, step):
    dy, dz = step
    got = ref[lead + (pl.ds(start + dy * period + dz, rows), slice(None))]
    if dz == 0:
        return got
    lanes = got.shape[1] // 128
    edge = (cell == 0) if dz < 0 else (cell == period - 1)
    edge = jnp.concatenate([edge] * lanes, axis=1) if lanes > 1 else edge
    return jnp.where(edge, 0.0, got)


STEPS = [(b, c) for b in (-1, 0, 1) for c in (-1, 0, 1)]


def prep_kernel(we_ref, wcat_ref, wt_ref):
    for n in range(9):
        b, c = divmod(n, 3)
        for a in range(3):
            w = we_ref[a, b, c]
            wcat_ref[pl.ds(n * 128, 128), pl.ds(a * 128, 128)] = w
            wt_ref[a, pl.ds(n * 128, 128), :] = w.astype(F32).T.astype(BF)


def forward_kernel(*refs, nk, nj, dims):
    gx, gy, gz, lx, ly, lz, bx, by = dims
    blocks, refs = refs[: nk * nj], refs[nk * nj :]
    cots, refs = refs[:nk], refs[nk:]
    wcat_ref, wl_ref, col_ref, slope_ref, pd_ref, back_ref, mine_ref = refs[:7]
    vol_ref, p_ref, h_ref, pool_ref, lcol_ref, dl_ref = refs[7:]
    k, j = lax.axis_index("space"), lax.axis_index("chan")
    plane, lplane = gy * gz, ly * lz
    brows = by * gz
    cl = wl_ref.shape[-1]
    crow = bx // 2 * lplane

    vol_ref[:, pl.ds(0, 16), :] = jnp.zeros((gx, 16, 128), F32)
    vol_ref[:, pl.ds(16 + plane, 16), :] = jnp.zeros((gx, 16, 128), F32)
    for dj in range(nj):
        for dk in range(nk):
            src = blocks[dj * nk + dk]
            kk = lax.rem(k + nk - dk, nk)
            jj = lax.rem(j + nj - dj, nj)
            row = pl.multiple_of(16 + jj * brows, 8)
            for q in range(bx):
                vol_ref[kk * bx + q, pl.ds(row, brows), :] = src[pl.ds(q * brows, brows), :].astype(F32)

    cell = depth_of(plane, gz)
    for x in range(gx):
        for n, step in enumerate(STEPS):
            col_ref[pl.ds(x * plane, plane), pl.ds(n * 128, 128)] = shifted(
                vol_ref, (x,), 16, plane, cell, gz, step
            ).astype(BF)

    p_ref[...] = jnp.dot(col_ref[...], wcat_ref[...], preferred_element_type=F32)

    for lq in range(lx):
        pair = None
        for x in (2 * lq, 2 * lq + 1):
            pre = p_ref[pl.ds(x * plane, plane), pl.ds(128, 128)]
            if x > 0:
                pre = pre + p_ref[pl.ds((x - 1) * plane, plane), pl.ds(0, 128)]
            if x < gx - 1:
                pre = pre + p_ref[pl.ds((x + 1) * plane, plane), pl.ds(256, 128)]
            h, slope = gelu_and_slope(pre)
            slope_ref[pl.ds(x * plane, plane), :] = slope
            pair = h if pair is None else pair + h
        wide = pair.reshape(ly, 2, gz, 128)
        h_ref[...] = (wide[:, 0] + wide[:, 1]).reshape(ly * gz, 128)
        pooled = (h_ref[pl.ds(0, lplane, stride=2), :] + h_ref[pl.ds(1, lplane, stride=2), :]) * 0.125
        pooled = pooled.astype(BF)
        pd_ref[pl.ds(lq * lplane, lplane), pl.ds(0, 128)] = pooled
        pool_ref[lq, pl.ds(0, 8), :] = jnp.zeros((8, 128), F32)
        pool_ref[lq, pl.ds(8 + lplane, 8), :] = jnp.zeros((8, 128), F32)
        pool_ref[lq, pl.ds(8, lplane), :] = pooled.astype(F32)

    lcell = depth_of(lplane, lz)
    for x in range(lx):
        for n, step in enumerate(STEPS):
            lcol_ref[pl.ds(x * lplane, lplane), pl.ds(n * 128, 128)] = shifted(
                pool_ref, (x,), 8, lplane, lcell, lz, step
            ).astype(BF)
    lcol = lcol_ref[...]
    parts = [
        jnp.dot(lcol, wl_ref[a].reshape(9 * 128, cl), preferred_element_type=F32) for a in range(3)
    ]
    for x in range(lx):
        dl_ref[x, pl.ds(0, 8), :] = jnp.zeros((8, cl), F32)
        dl_ref[x, pl.ds(8 + lplane, 8), :] = jnp.zeros((8, cl), F32)
    zero = jnp.zeros((lplane, cl), F32)
    pre = parts[1]
    pre = pre + jnp.concatenate([zero, parts[0][:-lplane]], axis=0)
    pre = pre + jnp.concatenate([parts[2][lplane:], zero], axis=0)
    slope = gelu_and_slope(pre)[1]
    for dk in range(nk):
        kk = lax.rem(k + nk - dk, nk)
        start = pl.multiple_of(kk * crow, 8)
        p_ref[pl.ds(start, crow), pl.ds(0, cl)] = cots[dk][...].astype(F32)
    cot = p_ref[pl.ds(0, lx * lplane), pl.ds(0, cl)]
    delta = (cot * slope).astype(BF)
    pd_ref[:, pl.ds(128, cl)] = delta
    wide = delta.astype(F32)
    for x in range(lx):
        dl_ref[x, pl.ds(8, lplane), :] = wide[x * lplane : (x + 1) * lplane]
    total = None
    for n, (b, c) in enumerate(STEPS):
        part = jnp.concatenate(
            [shifted(dl_ref, (x,), 8, lplane, lcell, lz, (-b, -c)) for x in range(lx)], axis=0
        ).astype(BF)
        w = wl_ref[:, b + 1, c + 1].reshape(3 * 128, cl)
        term = lax.dot_general(part, w, NT, preferred_element_type=F32)
        total = term if total is None else total + term
    zero = jnp.zeros((lplane, 128), F32)
    back = total[:, 128:256]
    back = back + jnp.concatenate([total[lplane:, 0:128], zero], axis=0)
    back = back + jnp.concatenate([zero, total[:-lplane, 256:384]], axis=0)
    back_ref[...] = back.astype(BF)
    mine_ref[...] = back


def late_grad_kernel(mine_ref, other_ref, out_ref, pool_ref, lcol_ref, *, dims, scale):
    lx, ly, lz = dims
    lplane = ly * lz
    rows = lx * lplane
    lcell = depth_of(lplane, lz)
    pool_ref[...] = jnp.zeros(pool_ref.shape, F32)
    for s, ref in enumerate((mine_ref, other_ref)):
        for x in range(lx):
            pool_ref[s, x + 1, pl.ds(8, lplane), :] = ref[pl.ds(x * lplane, lplane), pl.ds(0, 128)].astype(F32)
        for x in range(lx + 2):
            for n, step in enumerate(STEPS):
                lcol_ref[s, pl.ds(x * lplane, lplane), pl.ds(n * 128, 128)] = shifted(
                    pool_ref, (s, x), 8, lplane, lcell, lz, step
                ).astype(BF)
    cl = mine_ref.shape[1] - 128
    delta = jnp.concatenate([mine_ref[:, pl.ds(128, cl)], other_ref[:, pl.ds(128, cl)]], axis=0)
    for a in range(3):
        left = jnp.concatenate([lcol_ref[s, pl.ds(a * lplane, rows), :] for s in (0, 1)], axis=0)
        got = lax.dot_general(left, delta, (((0,), (0,)), ((), ())), preferred_element_type=F32)
        out_ref[pl.ds(a * 9 * 128, 9 * 128), :] = (got * scale).astype(BF)


def early_grad_kernel(
    mine_ref, other_ref, slope_ref, col_ref, part_ref, win_ref, wide_ref, d_ref, dt_ref, *, dims
):
    gx, gy, gz, lx, ly, lz, bx, by = dims
    plane, lplane = gy * gz, ly * lz
    k, j = lax.axis_index("space"), lax.axis_index("chan")
    brows = by * gz
    for q in (0, gx + 1):
        d_ref[q] = jnp.zeros(d_ref.shape[1:], F32)
    d_ref[:, pl.ds(0, 16), :] = jnp.zeros((gx + 2, 16, 128), F32)
    d_ref[:, pl.ds(16 + plane, 16), :] = jnp.zeros((gx + 2, 16, 128), F32)
    dt_ref[:, pl.ds(0, plane)] = jnp.zeros((128, plane), BF)
    dt_ref[:, pl.ds((gx + 1) * plane, plane)] = jnp.zeros((128, plane), BF)
    back = (mine_ref[...] + other_ref[...].astype(F32)) * 0.125
    wide_ref[pl.ds(0, lx * lplane, stride=2), :] = back
    wide_ref[pl.ds(1, lx * lplane, stride=2), :] = back
    for lq in range(lx):
        rows = wide_ref[pl.ds(lq * ly * gz, ly * gz), :].reshape(ly, 1, gz, 128)
        rows = jnp.broadcast_to(rows, (ly, 2, gz, 128)).reshape(plane, 128)
        for x in (2 * lq, 2 * lq + 1):
            delta = (rows * slope_ref[pl.ds(x * plane, plane), :]).astype(BF).astype(F32)
            d_ref[x + 1, pl.ds(16, plane), :] = delta
            dt_ref[:, pl.ds((x + 1) * plane, plane)] = delta.T.astype(BF)
    left = jnp.concatenate([dt_ref[:, pl.ds((2 - a) * plane, gx * plane)] for a in range(3)], axis=0)
    got = jnp.dot(left, col_ref[...], preferred_element_type=F32)
    for a in range(3):
        for n in range(9):
            part_ref[pl.ds((a * 9 + n) * 128, 128), :] = got[
                a * 128 : (a + 1) * 128, n * 128 : (n + 1) * 128
            ].T.astype(part_ref.dtype)
    row = pl.multiple_of(j * brows, 8)
    for q in range(bx + 2):
        win_ref[q] = d_ref[k * bx + q, pl.ds(row, brows + 32), :]


def grad_volume_kernel(win_ref, wt_ref, gv_ref, vcol_ref, *, bx, brows, gz):
    cell = depth_of(brows, gz)
    for q in range(bx + 2):
        for n, (b, c) in enumerate(STEPS):
            vcol_ref[pl.ds(q * brows, brows), pl.ds(n * 128, 128)] = shifted(
                win_ref, (q,), 16, brows, cell, gz, (-b, -c)
            ).astype(BF)
    total = None
    for a in range(3):
        term = jnp.dot(vcol_ref[pl.ds((2 - a) * brows, bx * brows), :], wt_ref[a], preferred_element_type=F32)
        total = term if total is None else total + term
    gv_ref[...] = total.astype(BF)


def turned(value, axis, by):
    count = lax.axis_size(axis)
    return lax.ppermute(value, axis, [(i, (i + by) % count) for i in range(count)])


def call(kernel, outs, scratch, args, name, far=()):
    args = [pltpu.with_memory_space_constraint(arg, pltpu.VMEM) for arg in args]
    outs = [out if n in far else pltpu.VMEM(out.shape, out.dtype) for n, out in enumerate(outs)]
    return pl.pallas_call(
        kernel,
        out_shape=outs,
        in_specs=[pl.BlockSpec(memory_space=pltpu.VMEM)] * len(args),
        out_specs=[pl.BlockSpec(memory_space=pltpu.VMEM)] * len(outs),
        scratch_shapes=scratch,
        compiler_params=pltpu.CompilerParams(vmem_limit_bytes=VMEM_BYTES),
        name=name,
    )(*args)


def whole_sample(volume, early_weight, late_weight, cotangent):
    nk, nj, nr = (lax.axis_size(axis) for axis in ("space", "chan", "rep"))
    _, bx, by, gz, _ = volume.shape
    _, cx, ly, lz, cl = cotangent.shape
    gx, gy, lx = bx * nk, by * nj, cx * nk
    plane, lplane, brows = gy * gz, ly * lz, by * gz
    rows, lrows = gx * plane, lx * lplane
    scale = 1.0 / math.sqrt(nr * lrows)
    sds = jax.ShapeDtypeStruct

    mine = volume.reshape(bx * brows, 128)
    line = [mine] + [turned(mine, "space", dk) for dk in range(1, nk)]
    blocks = list(line)
    for dj in range(1, nj):
        blocks += [turned(block, "chan", dj) for block in line]
    cot = cotangent.reshape(cx * lplane, cl)
    cots = [cot] + [turned(cot, "space", dk) for dk in range(1, nk)]

    wcat, wt = call(
        prep_kernel, [sds((9 * 128, 3 * 128), BF), sds((3, 9 * 128, 128), BF)], [], [early_weight], "prep"
    )
    dims = (gx, gy, gz, lx, ly, lz, bx, by)
    col, slope, pooled_delta, back, back_mine = call(
        functools.partial(forward_kernel, nk=nk, nj=nj, dims=dims),
        [
            sds((rows, 9 * 128), BF),
            sds((rows, 128), F32),
            sds((lrows, 128 + cl), BF),
            sds((lrows, 128), BF),
            sds((lrows, 128), F32),
        ],
        [
            pltpu.VMEM((gx, plane + 32, 128), F32),
            pltpu.VMEM((rows, 3 * 128), F32),
            pltpu.VMEM((ly * gz, 128), F32),
            pltpu.VMEM((lx, lplane + 16, 128), F32),
            pltpu.VMEM((lrows, 9 * 128), BF),
            pltpu.VMEM((lx, lplane + 16, cl), F32),
        ],
        blocks + cots + [wcat, late_weight],
        "forward",
    )
    pd_other = turned(pooled_delta, "rep", 1)
    back_other = turned(back, "chan", 1)
    (late,) = call(
        functools.partial(late_grad_kernel, dims=(lx, ly, lz), scale=scale),
        [sds((27 * 128, cl), BF)],
        [pltpu.VMEM((2, lx + 2, lplane + 16, 128), F32), pltpu.VMEM((2, (lx + 2) * lplane, 9 * 128), BF)],
        [pooled_delta, pd_other],
        "late_grad",
        far=(0,),
    )
    back_mine, late = lax.optimization_barrier((back_mine, late))
    part, win = call(
        functools.partial(early_grad_kernel, dims=dims),
        [sds((27 * 128, 128), BF), sds((bx + 2, brows + 32, 128), F32)],
        [
            pltpu.VMEM((lx * ly * gz, 128), F32),
            pltpu.VMEM((gx + 2, plane + 32, 128), F32),
            pltpu.VMEM((128, (gx + 2) * plane), BF),
        ],
        [back_mine, back_other, slope, col],
        "early_grad",
    )
    part_other = turned(part, "rep", 1)
    (gv,) = call(
        functools.partial(grad_volume_kernel, bx=bx, brows=brows, gz=gz),
        [sds((bx * brows, 128), BF)],
        [pltpu.VMEM(((bx + 2) * brows, 9 * 128), BF)],
        [win, wt],
        "grad_volume",
        far=(0,),
    )
    early = ((part.astype(F32) + part_other.astype(F32)) * scale).astype(BF)
    return (
        early.reshape(3, 3, 3, 128, 128),
        late.reshape(3, 3, 3, 128, cl),
        gv.reshape(1, bx, by, gz, 128),
    )


def solution(mesh):
    few = mesh.shape["space"] * mesh.shape["chan"] <= GATHER_BLOCKS
    alone = mesh.shape["rep"] == 2 and mesh.shape["chan"] == 2
    return jax.shard_map(
        whole_sample if few and alone else per_device,
        mesh=mesh,
        in_specs=(
            P(("groups", "rep"), "space", "chan", None, None),
            P(),
            P(None, None, None, None, "chan"),
            P(("groups", "rep"), "space", None, None, "chan"),
        ),
        out_specs=(
            P("groups", None, None, None, None),
            P("groups", None, None, None, "chan"),
            P(("groups", "rep"), "space", "chan", None, None),
        ),
        check_vma=False,
    )
```

```python
import functools
import math

import jax
import jax.numpy as jnp
from jax import lax
from jax.experimental import pallas as pl
from jax.experimental.pallas import tpu as pltpu
from jax.sharding import PartitionSpec as P

BF = jnp.bfloat16
F32 = jnp.float32
VMEM_BYTES = 24 * 2**20
GATHER_BLOCKS = 8


def padded_2(block, sides, width):
    for axis, dim in sides:
        count = lax.axis_size(axis)
        forward = [(i, i + 1) for i in range(count - 1)]
        backward = [(target, source) for source, target in forward]
        low = lax.ppermute(
            lax.slice_in_dim(block, block.shape[dim] - width, None, axis=dim), axis, forward
        )
        high = lax.ppermute(lax.slice_in_dim(block, 0, width, axis=dim), axis, backward)
        block = jnp.concatenate([low, block, high], axis=dim)
    return block


def gelu_tanh(value):
    return jax.nn.gelu(value, approximate=True)


def conv_padded(padded, weight):
    depth = padded.shape[1] - 2
    height = padded.shape[2] - 2
    length = padded.shape[3] - 2
    total = None
    for first in range(3):
        for second in range(3):
            for third in range(3):
                window = padded[
                    :, first : first + depth, second : second + height, third : third + length
                ]
                term = jnp.einsum(
                    "sxyzc,co->sxyzo",
                    window,
                    weight[first, second, third],
                    preferred_element_type=jnp.float32,
                )
                total = term if total is None else total + term
    return total


def kernel_grad(padded, delta):
    depth = delta.shape[1]
    height = delta.shape[2]
    length = delta.shape[3]
    planes = []
    for first in range(3):
        for second in range(3):
            for third in range(3):
                window = padded[
                    :, first : first + depth, second : second + height, third : third + length
                ]
                planes.append(
                    jnp.einsum("sxyzc,sxyzo->co", window, delta, preferred_element_type=jnp.float32)
                )
    stacked = jnp.stack(planes, axis=0)
    return stacked.reshape((3, 3, 3) + stacked.shape[1:])


def flipped(weight):
    return jnp.swapaxes(weight[::-1, ::-1, ::-1], 3, 4)


def pad_dims(field, dims):
    widths = [(1, 1) if place in dims else (0, 0) for place in range(field.ndim)]
    return jnp.pad(field, widths)


def pool_cells(field):
    s, x, y, z, c = field.shape
    return jnp.mean(field.reshape(s, x // 2, 2, y // 2, 2, z // 2, 2, c), axis=(2, 4, 6))


def spread_cells(field):
    s, x, y, z, c = field.shape
    wide = jnp.broadcast_to(field[:, :, None, :, None, :, None, :], (s, x, 2, y, 2, z, 2, c))
    return wide.reshape(s, 2 * x, 2 * y, 2 * z, c) * 0.125


def late_layer(joined, late_weight, cotangent):
    rim = padded_2(joined, (("space", 1),), 1)
    late_pad = pad_dims(rim, (2, 3))
    pre_late = conv_padded(late_pad, late_weight)
    delta_late = jax.vjp(gelu_tanh, pre_late)[1](cotangent.astype(jnp.float32))[0].astype(
        jnp.bfloat16
    )
    late_part = kernel_grad(late_pad, delta_late)
    delta_rim = padded_2(delta_late, (("space", 1),), 1)
    back_partial = conv_padded(pad_dims(delta_rim, (2, 3)), flipped(late_weight))
    return (back_partial, late_part)


def per_device(volume, early_weight, late_weight, cotangent):
    count = (
        cotangent.shape[0]
        * lax.axis_size("rep")
        * cotangent.shape[1]
        * lax.axis_size("space")
        * cotangent.shape[2]
        * cotangent.shape[3]
    )
    scale = 1.0 / math.sqrt(count)
    haloed = padded_2(volume, (("space", 1), ("chan", 2)), 1)
    padded_in = pad_dims(haloed, (3,))
    pre_early = conv_padded(padded_in, early_weight)
    pooled = pool_cells(gelu_tanh(pre_early)).astype(jnp.bfloat16)
    joined = lax.all_gather(pooled, "chan", axis=2, tiled=True)
    back_partial, late_part = late_layer(joined, late_weight, cotangent)
    back_rows = lax.psum_scatter(back_partial, "chan", scatter_dimension=2, tiled=True)
    delta_early = jax.vjp(gelu_tanh, pre_early)[1](spread_cells(back_rows))[0].astype(jnp.bfloat16)
    early_part = kernel_grad(padded_in, delta_early)
    delta_halo = padded_2(delta_early, (("space", 1), ("chan", 2)), 1)
    grad_volume = conv_padded(pad_dims(delta_halo, (3,)), flipped(early_weight)).astype(
        jnp.bfloat16
    )
    early_total = lax.psum(early_part, ("space", "chan", "rep"))
    grad_early = (early_total * scale).astype(jnp.bfloat16)
    late_total = lax.psum(late_part, ("space", "rep"))
    grad_late = (late_total * scale).astype(jnp.bfloat16)
    return (grad_early, grad_late, grad_volume)


NT = (((1,), (1,)), ((), ()))


def gelu_and_slope(v):
    k = 0.7978845608028654
    sq = v * v
    t = jnp.tanh(k * (v + 0.044715 * (v * sq)))
    half = 0.5 * (1.0 + t)
    return v * half, half + 0.5 * v * (1.0 - t * t) * (k * (1.0 + 0.134145 * sq))


def depth_of(rows, period):
    return lax.broadcasted_iota(jnp.int32, (rows, 128), 0) % period


def shifted(ref, lead, start, rows, cell, period, step):
    dy, dz = step
    got = ref[lead + (pl.ds(start + dy * period + dz, rows), slice(None))]
    if dz == 0:
        return got
    lanes = got.shape[1] // 128
    edge = (cell == 0) if dz < 0 else (cell == period - 1)
    edge = jnp.concatenate([edge] * lanes, axis=1) if lanes > 1 else edge
    return jnp.where(edge, 0.0, got)


STEPS = [(b, c) for b in (-1, 0, 1) for c in (-1, 0, 1)]


def early_kernel(*refs, nk, nj, dims):
    gx, gy, gz, lx, ly, lz, bx, by = dims
    blocks, refs = refs[: nk * nj], refs[nk * nj :]
    we_hbm, wl_hbm, we_ref, wl_ref, col_ref, slope_ref, pooled_ref = refs[:7]
    vol_ref, own_ref, wcat_ref, p_ref, h_ref, sems = refs[7:]
    k, j = lax.axis_index("space"), lax.axis_index("chan")
    plane, lplane = gy * gz, ly * lz
    brows = by * gz
    own_copy = pltpu.make_async_copy(blocks[0], own_ref, sems.at[0])
    we_copy = pltpu.make_async_copy(we_hbm, we_ref, sems.at[1])
    wl_copy = pltpu.make_async_copy(wl_hbm, wl_ref, sems.at[2])
    own_copy.start()
    we_copy.start()
    wl_copy.start()

    vol_ref[:, pl.ds(0, 16), :] = jnp.zeros((gx, 16, 128), F32)
    vol_ref[:, pl.ds(16 + plane, 16), :] = jnp.zeros((gx, 16, 128), F32)
    for n in [*range(1, nk * nj), 0]:
        dj, dk = divmod(n, nk)
        if n == 0:
            own_copy.wait()
        src = blocks[n] if n else own_ref
        kk = lax.rem(k + nk - dk, nk)
        jj = lax.rem(j + nj - dj, nj)
        row = pl.multiple_of(16 + jj * brows, 8)
        for q in range(bx):
            vol_ref[kk * bx + q, pl.ds(row, brows), :] = src[pl.ds(q * brows, brows), :].astype(F32)

    cell = depth_of(plane, gz)
    for x in range(gx):
        for n, step in enumerate(STEPS):
            col_ref[pl.ds(x * plane, plane), pl.ds(n * 128, 128)] = shifted(
                vol_ref, (x,), 16, plane, cell, gz, step
            ).astype(BF)

    we_copy.wait()
    for n in range(9):
        b, c = divmod(n, 3)
        for a in range(3):
            wcat_ref[pl.ds(n * 128, 128), pl.ds(a * 128, 128)] = we_ref[a, b, c]
    p_ref[...] = jnp.dot(col_ref[...], wcat_ref[...], preferred_element_type=F32)

    for lq in range(lx):
        pair = None
        for x in (2 * lq, 2 * lq + 1):
            pre = p_ref[pl.ds(x * plane, plane), pl.ds(128, 128)]
            if x > 0:
                pre = pre + p_ref[pl.ds((x - 1) * plane, plane), pl.ds(0, 128)]
            if x < gx - 1:
                pre = pre + p_ref[pl.ds((x + 1) * plane, plane), pl.ds(256, 128)]
            h, slope = gelu_and_slope(pre)
            slope_ref[pl.ds(x * plane, plane), :] = slope
            pair = h if pair is None else pair + h
        wide = pair.reshape(ly, 2, gz, 128)
        h_ref[...] = (wide[:, 0] + wide[:, 1]).reshape(ly * gz, 128)
        pooled = (h_ref[pl.ds(0, lplane, stride=2), :] + h_ref[pl.ds(1, lplane, stride=2), :]) * 0.125
        pooled_ref[pl.ds(lq * lplane, lplane), :] = pooled.astype(BF)
    wl_copy.wait()


def late_kernel(*refs, nk, dims):
    lx, ly, lz, cx = dims
    pooled_ref, cots, refs = refs[0], refs[1 : nk + 1], refs[nk + 1 :]
    wl_ref, pd_ref, back_ref, mine_ref, pool_ref, lcol_ref, dl_ref, cot_ref = refs
    lplane = ly * lz
    cl = wl_ref.shape[-1]
    crow = cx * lplane
    k = lax.axis_index("space")
    for x in range(lx):
        pool_ref[x, pl.ds(0, 8), :] = jnp.zeros((8, 128), F32)
        pool_ref[x, pl.ds(8 + lplane, 8), :] = jnp.zeros((8, 128), F32)
        pool_ref[x, pl.ds(8, lplane), :] = pooled_ref[pl.ds(x * lplane, lplane), :].astype(F32)
    pd_ref[:, pl.ds(0, 128)] = pooled_ref[...]

    lcell = depth_of(lplane, lz)
    for x in range(lx):
        for n, step in enumerate(STEPS):
            lcol_ref[pl.ds(x * lplane, lplane), pl.ds(n * 128, 128)] = shifted(
                pool_ref, (x,), 8, lplane, lcell, lz, step
            ).astype(BF)
    lcol = lcol_ref[...]
    parts = [
        jnp.dot(lcol, wl_ref[a].reshape(9 * 128, cl), preferred_element_type=F32) for a in range(3)
    ]
    for x in range(lx):
        dl_ref[x, pl.ds(0, 8), :] = jnp.zeros((8, cl), F32)
        dl_ref[x, pl.ds(8 + lplane, 8), :] = jnp.zeros((8, cl), F32)
    zero = jnp.zeros((lplane, cl), F32)
    pre = parts[1]
    pre = pre + jnp.concatenate([zero, parts[0][:-lplane]], axis=0)
    pre = pre + jnp.concatenate([parts[2][lplane:], zero], axis=0)
    slope = gelu_and_slope(pre)[1]
    for dk in range(nk):
        kk = lax.rem(k + nk - dk, nk)
        start = pl.multiple_of(kk * crow, 8)
        cot_ref[pl.ds(start, crow), :] = cots[dk][...].astype(F32)
    delta = (cot_ref[...] * slope).astype(BF)
    pd_ref[:, pl.ds(128, cl)] = delta
    wide = delta.astype(F32)
    for x in range(lx):
        dl_ref[x, pl.ds(8, lplane), :] = wide[x * lplane : (x + 1) * lplane]
    total = None
    for n, (b, c) in enumerate(STEPS):
        part = jnp.concatenate(
            [shifted(dl_ref, (x,), 8, lplane, lcell, lz, (-b, -c)) for x in range(lx)], axis=0
        ).astype(BF)
        w = wl_ref[:, b + 1, c + 1].reshape(3 * 128, cl)
        term = lax.dot_general(part, w, NT, preferred_element_type=F32)
        total = term if total is None else total + term
    zero = jnp.zeros((lplane, 128), F32)
    back = total[:, 128:256]
    back = back + jnp.concatenate([total[lplane:, 0:128], zero], axis=0)
    back = back + jnp.concatenate([zero, total[:-lplane, 256:384]], axis=0)
    back_ref[...] = back.astype(BF)
    mine_ref[...] = back


def late_grad_kernel(mine_ref, other_ref, out_ref, pool_ref, lcol_ref, *, dims, scale):
    lx, ly, lz = dims
    lplane = ly * lz
    rows = lx * lplane
    lcell = depth_of(lplane, lz)
    pool_ref[...] = jnp.zeros(pool_ref.shape, F32)
    for s, ref in enumerate((mine_ref, other_ref)):
        for x in range(lx):
            pool_ref[s, x + 1, pl.ds(8, lplane), :] = ref[pl.ds(x * lplane, lplane), pl.ds(0, 128)].astype(F32)
        for x in range(lx + 2):
            for n, step in enumerate(STEPS):
                lcol_ref[s, pl.ds(x * lplane, lplane), pl.ds(n * 128, 128)] = shifted(
                    pool_ref, (s, x), 8, lplane, lcell, lz, step
                ).astype(BF)
    cl = mine_ref.shape[1] - 128
    delta = jnp.concatenate([mine_ref[:, pl.ds(128, cl)], other_ref[:, pl.ds(128, cl)]], axis=0)
    for a in range(3):
        left = jnp.concatenate([lcol_ref[s, pl.ds(a * lplane, rows), :] for s in (0, 1)], axis=0)
        got = lax.dot_general(left, delta, (((0,), (0,)), ((), ())), preferred_element_type=F32)
        out_ref[pl.ds(a * 9 * 128, 9 * 128), :] = (got * scale).astype(BF)


def early_grad_kernel(
    mine_ref, other_ref, slope_ref, col_ref, part_ref, win_ref, wide_ref, d_ref, dt_ref, *, dims
):
    gx, gy, gz, lx, ly, lz, bx, by = dims
    plane, lplane = gy * gz, ly * lz
    k, j = lax.axis_index("space"), lax.axis_index("chan")
    brows = by * gz
    for q in (0, gx + 1):
        d_ref[q] = jnp.zeros(d_ref.shape[1:], F32)
    d_ref[:, pl.ds(0, 16), :] = jnp.zeros((gx + 2, 16, 128), F32)
    d_ref[:, pl.ds(16 + plane, 16), :] = jnp.zeros((gx + 2, 16, 128), F32)
    dt_ref[:, pl.ds(0, plane)] = jnp.zeros((128, plane), BF)
    dt_ref[:, pl.ds((gx + 1) * plane, plane)] = jnp.zeros((128, plane), BF)
    back = (mine_ref[...] + other_ref[...].astype(F32)) * 0.125
    wide_ref[pl.ds(0, lx * lplane, stride=2), :] = back
    wide_ref[pl.ds(1, lx * lplane, stride=2), :] = back
    for lq in range(lx):
        rows = wide_ref[pl.ds(lq * ly * gz, ly * gz), :].reshape(ly, 1, gz, 128)
        rows = jnp.broadcast_to(rows, (ly, 2, gz, 128)).reshape(plane, 128)
        for x in (2 * lq, 2 * lq + 1):
            delta = (rows * slope_ref[pl.ds(x * plane, plane), :]).astype(BF).astype(F32)
            d_ref[x + 1, pl.ds(16, plane), :] = delta
            dt_ref[:, pl.ds((x + 1) * plane, plane)] = delta.T.astype(BF)
    left = jnp.concatenate([dt_ref[:, pl.ds((2 - a) * plane, gx * plane)] for a in range(3)], axis=0)
    got = jnp.dot(left, col_ref[...], preferred_element_type=F32)
    for a in range(3):
        for n in range(9):
            part_ref[pl.ds((a * 9 + n) * 128, 128), :] = got[
                a * 128 : (a + 1) * 128, n * 128 : (n + 1) * 128
            ].T.astype(part_ref.dtype)
    row = pl.multiple_of(j * brows, 8)
    for q in range(bx + 2):
        win_ref[q] = d_ref[k * bx + q, pl.ds(row, brows + 32), :]


def grad_volume_kernel(win_ref, we_ref, gv_ref, vcol_ref, wt_ref, *, bx, brows, gz):
    for n in range(9):
        b, c = divmod(n, 3)
        for a in range(3):
            wt_ref[a, pl.ds(n * 128, 128), :] = we_ref[a, b, c].astype(F32).T.astype(BF)
    cell = depth_of(brows, gz)
    for q in range(bx + 2):
        for n, (b, c) in enumerate(STEPS):
            vcol_ref[pl.ds(q * brows, brows), pl.ds(n * 128, 128)] = shifted(
                win_ref, (q,), 16, brows, cell, gz, (-b, -c)
            ).astype(BF)
    total = None
    for a in range(3):
        term = jnp.dot(vcol_ref[pl.ds((2 - a) * brows, bx * brows), :], wt_ref[a], preferred_element_type=F32)
        total = term if total is None else total + term
    gv_ref[...] = total.astype(BF)


def turned(value, axis, by):
    count = lax.axis_size(axis)
    return lax.ppermute(value, axis, [(i, (i + by) % count) for i in range(count)])


def call(kernel, outs, scratch, args, name, far=(), raw=()):
    args = [
        pltpu.with_memory_space_constraint(arg, pltpu.HBM if n in raw else pltpu.VMEM)
        for n, arg in enumerate(args)
    ]
    outs = [out if n in far else pltpu.VMEM(out.shape, out.dtype) for n, out in enumerate(outs)]
    return pl.pallas_call(
        kernel,
        out_shape=outs,
        in_specs=[
            pl.BlockSpec(memory_space=pltpu.HBM if n in raw else pltpu.VMEM) for n in range(len(args))
        ],
        out_specs=[pl.BlockSpec(memory_space=pltpu.VMEM)] * len(outs),
        scratch_shapes=scratch,
        compiler_params=pltpu.CompilerParams(vmem_limit_bytes=VMEM_BYTES),
        name=name,
    )(*args)


def whole_sample(volume, early_weight, late_weight, cotangent):
    nk, nj, nr = (lax.axis_size(axis) for axis in ("space", "chan", "rep"))
    _, bx, by, gz, _ = volume.shape
    _, cx, ly, lz, cl = cotangent.shape
    gx, gy, lx = bx * nk, by * nj, cx * nk
    plane, lplane, brows = gy * gz, ly * lz, by * gz
    rows, lrows = gx * plane, lx * lplane
    scale = 1.0 / math.sqrt(nr * lrows)
    sds = jax.ShapeDtypeStruct

    mine = volume.reshape(bx * brows, 128)
    line = [mine] + [turned(mine, "space", dk) for dk in range(1, nk)]
    blocks = list(line)
    for dj in range(1, nj):
        blocks += [turned(block, "chan", dj) for block in line]
    cot = cotangent.reshape(cx * lplane, cl)
    held = lax.optimization_barrier((cot, *line[1:]))[0]
    cots = [cot] + [turned(held, "space", dk) for dk in range(1, nk)]

    count = nk * nj
    we, wl, col, slope, pooled = call(
        functools.partial(early_kernel, nk=nk, nj=nj, dims=(gx, gy, gz, lx, ly, lz, bx, by)),
        [
            sds(early_weight.shape, BF),
            sds(late_weight.shape, BF),
            sds((rows, 9 * 128), BF),
            sds((rows, 128), F32),
            sds((lrows, 128), BF),
        ],
        [
            pltpu.VMEM((gx, plane + 32, 128), F32),
            pltpu.VMEM((bx * brows, 128), BF),
            pltpu.VMEM((9 * 128, 3 * 128), BF),
            pltpu.VMEM((rows, 3 * 128), F32),
            pltpu.VMEM((ly * gz, 128), F32),
            pltpu.SemaphoreType.DMA((3,)),
        ],
        blocks + [early_weight, late_weight],
        "early",
        raw=(0, count, count + 1),
    )
    pooled_delta, back, back_mine = call(
        functools.partial(late_kernel, nk=nk, dims=(lx, ly, lz, cx)),
        [sds((lrows, 128 + cl), BF), sds((lrows, 128), BF), sds((lrows, 128), F32)],
        [
            pltpu.VMEM((lx, lplane + 16, 128), F32),
            pltpu.VMEM((lrows, 9 * 128), BF),
            pltpu.VMEM((lx, lplane + 16, cl), F32),
            pltpu.VMEM((lrows, cl), F32),
        ],
        [pooled] + cots + [wl],
        "late",
    )
    pd_other = turned(pooled_delta, "rep", 1)
    back_other = turned(back, "chan", 1)
    (late,) = call(
        functools.partial(late_grad_kernel, dims=(lx, ly, lz), scale=scale),
        [sds((27 * 128, cl), BF)],
        [pltpu.VMEM((2, lx + 2, lplane + 16, 128), F32), pltpu.VMEM((2, (lx + 2) * lplane, 9 * 128), BF)],
        [pooled_delta, pd_other],
        "late_grad",
        far=(0,),
    )
    back_mine, late = lax.optimization_barrier((back_mine, late))
    part, win = call(
        functools.partial(early_grad_kernel, dims=(gx, gy, gz, lx, ly, lz, bx, by)),
        [sds((27 * 128, 128), BF), sds((bx + 2, brows + 32, 128), F32)],
        [
            pltpu.VMEM((lx * ly * gz, 128), F32),
            pltpu.VMEM((gx + 2, plane + 32, 128), F32),
            pltpu.VMEM((128, (gx + 2) * plane), BF),
        ],
        [back_mine, back_other, slope, col],
        "early_grad",
    )
    part_other = turned(part, "rep", 1)
    (gv,) = call(
        functools.partial(grad_volume_kernel, bx=bx, brows=brows, gz=gz),
        [sds((bx * brows, 128), BF)],
        [pltpu.VMEM(((bx + 2) * brows, 9 * 128), BF), pltpu.VMEM((3, 9 * 128, 128), BF)],
        [win, we],
        "grad_volume",
        far=(0,),
    )
    early = ((part.astype(F32) + part_other.astype(F32)) * scale).astype(BF)
    return (
        early.reshape(3, 3, 3, 128, 128),
        late.reshape(3, 3, 3, 128, cl),
        gv.reshape(1, bx, by, gz, 128),
    )


def solution(mesh):
    few = mesh.shape["space"] * mesh.shape["chan"] <= GATHER_BLOCKS
    alone = mesh.shape["rep"] == 2 and mesh.shape["chan"] == 2
    return jax.shard_map(
        whole_sample if few and alone else per_device,
        mesh=mesh,
        in_specs=(
            P(("groups", "rep"), "space", "chan", None, None),
            P(),
            P(None, None, None, None, "chan"),
            P(("groups", "rep"), "space", None, None, "chan"),
        ),
        out_specs=(
            P("groups", None, None, None, None),
            P("groups", None, None, None, "chan"),
            P(("groups", "rep"), "space", "chan", None, None),
        ),
        check_vma=False,
    )
```

```python
import functools
import math

import jax
import jax.numpy as jnp
from jax import lax
from jax.experimental import pallas as pl
from jax.experimental.pallas import tpu as pltpu
from jax.sharding import PartitionSpec as P

BF = jnp.bfloat16
F32 = jnp.float32
VMEM_BYTES = 14 * 2**20
GATHER_BLOCKS = 8


def padded_2(block, sides, width):
    for axis, dim in sides:
        count = lax.axis_size(axis)
        forward = [(i, i + 1) for i in range(count - 1)]
        backward = [(target, source) for source, target in forward]
        low = lax.ppermute(
            lax.slice_in_dim(block, block.shape[dim] - width, None, axis=dim), axis, forward
        )
        high = lax.ppermute(lax.slice_in_dim(block, 0, width, axis=dim), axis, backward)
        block = jnp.concatenate([low, block, high], axis=dim)
    return block


def gelu_tanh(value):
    return jax.nn.gelu(value, approximate=True)


def conv_padded(padded, weight):
    depth = padded.shape[1] - 2
    height = padded.shape[2] - 2
    length = padded.shape[3] - 2
    total = None
    for first in range(3):
        for second in range(3):
            for third in range(3):
                window = padded[
                    :, first : first + depth, second : second + height, third : third + length
                ]
                term = jnp.einsum(
                    "sxyzc,co->sxyzo",
                    window,
                    weight[first, second, third],
                    preferred_element_type=jnp.float32,
                )
                total = term if total is None else total + term
    return total


def kernel_grad(padded, delta):
    depth = delta.shape[1]
    height = delta.shape[2]
    length = delta.shape[3]
    planes = []
    for first in range(3):
        for second in range(3):
            for third in range(3):
                window = padded[
                    :, first : first + depth, second : second + height, third : third + length
                ]
                planes.append(
                    jnp.einsum("sxyzc,sxyzo->co", window, delta, preferred_element_type=jnp.float32)
                )
    stacked = jnp.stack(planes, axis=0)
    return stacked.reshape((3, 3, 3) + stacked.shape[1:])


def flipped(weight):
    return jnp.swapaxes(weight[::-1, ::-1, ::-1], 3, 4)


def pad_dims(field, dims):
    widths = [(1, 1) if place in dims else (0, 0) for place in range(field.ndim)]
    return jnp.pad(field, widths)


def pool_cells(field):
    s, x, y, z, c = field.shape
    return jnp.mean(field.reshape(s, x // 2, 2, y // 2, 2, z // 2, 2, c), axis=(2, 4, 6))


def spread_cells(field):
    s, x, y, z, c = field.shape
    wide = jnp.broadcast_to(field[:, :, None, :, None, :, None, :], (s, x, 2, y, 2, z, 2, c))
    return wide.reshape(s, 2 * x, 2 * y, 2 * z, c) * 0.125


def late_layer(joined, late_weight, cotangent):
    rim = padded_2(joined, (("space", 1),), 1)
    late_pad = pad_dims(rim, (2, 3))
    pre_late = conv_padded(late_pad, late_weight)
    delta_late = jax.vjp(gelu_tanh, pre_late)[1](cotangent.astype(jnp.float32))[0].astype(
        jnp.bfloat16
    )
    late_part = kernel_grad(late_pad, delta_late)
    delta_rim = padded_2(delta_late, (("space", 1),), 1)
    back_partial = conv_padded(pad_dims(delta_rim, (2, 3)), flipped(late_weight))
    return (back_partial, late_part)


def per_device(volume, early_weight, late_weight, cotangent):
    count = (
        cotangent.shape[0]
        * lax.axis_size("rep")
        * cotangent.shape[1]
        * lax.axis_size("space")
        * cotangent.shape[2]
        * cotangent.shape[3]
    )
    scale = 1.0 / math.sqrt(count)
    haloed = padded_2(volume, (("space", 1), ("chan", 2)), 1)
    padded_in = pad_dims(haloed, (3,))
    pre_early = conv_padded(padded_in, early_weight)
    pooled = pool_cells(gelu_tanh(pre_early)).astype(jnp.bfloat16)
    joined = lax.all_gather(pooled, "chan", axis=2, tiled=True)
    back_partial, late_part = late_layer(joined, late_weight, cotangent)
    back_rows = lax.psum_scatter(back_partial, "chan", scatter_dimension=2, tiled=True)
    delta_early = jax.vjp(gelu_tanh, pre_early)[1](spread_cells(back_rows))[0].astype(jnp.bfloat16)
    early_part = kernel_grad(padded_in, delta_early)
    delta_halo = padded_2(delta_early, (("space", 1), ("chan", 2)), 1)
    grad_volume = conv_padded(pad_dims(delta_halo, (3,)), flipped(early_weight)).astype(
        jnp.bfloat16
    )
    early_total = lax.psum(early_part, ("space", "chan", "rep"))
    grad_early = (early_total * scale).astype(jnp.bfloat16)
    late_total = lax.psum(late_part, ("space", "rep"))
    grad_late = (late_total * scale).astype(jnp.bfloat16)
    return (grad_early, grad_late, grad_volume)


NT = (((1,), (1,)), ((), ()))


def gelu_and_slope(v):
    k = 0.7978845608028654
    sq = v * v
    t = jnp.tanh(k * (v + 0.044715 * (v * sq)))
    half = 0.5 * (1.0 + t)
    return v * half, half + 0.5 * v * (1.0 - t * t) * (k * (1.0 + 0.134145 * sq))


def depth_of(rows, period):
    return lax.broadcasted_iota(jnp.int32, (rows, 128), 0) % period


def shifted(ref, lead, start, rows, cell, period, step):
    dy, dz = step
    got = ref[lead + (pl.ds(start + dy * period + dz, rows), slice(None))]
    if dz == 0:
        return got
    lanes = got.shape[1] // 128
    edge = (cell == 0) if dz < 0 else (cell == period - 1)
    edge = jnp.concatenate([edge] * lanes, axis=1) if lanes > 1 else edge
    return jnp.where(edge, 0.0, got)


STEPS = [(b, c) for b in (-1, 0, 1) for c in (-1, 0, 1)]


def fold(parts, rows):
    zero = jnp.zeros((rows, parts[0].shape[1]), F32)
    return (
        parts[1]
        + jnp.concatenate([zero, parts[0][:-rows]], axis=0)
        + jnp.concatenate([parts[2][rows:], zero], axis=0)
    )


def early_kernel(*refs, nk, dims):
    gx, gy, gz, lx, ly, lz, bx, by = dims
    blocks, refs = refs[:nk], refs[nk:]
    we_hbm, wl_hbm, we_ref, wl_ref, wcat_ref, half_ref, slope_ref, send_ref, edge_ref = refs[:9]
    vol_ref, own_ref, col_ref, p_ref, pre_ref, h_ref, row_ref, sems = refs[9:]
    k, j = lax.axis_index("space"), lax.axis_index("chan")
    brows, hl, line = by * gz, by // 2 * lz, gx * gz
    own_copy = pltpu.make_async_copy(blocks[0], own_ref, sems.at[0])
    we_copy = pltpu.make_async_copy(we_hbm, we_ref, sems.at[1])
    wl_copy = pltpu.make_async_copy(wl_hbm, wl_ref, sems.at[2])
    we_copy.start()
    own_copy.start()

    vol_ref[:, pl.ds(0, 16), :] = jnp.zeros((gx, 16, 128), F32)
    vol_ref[:, pl.ds(16 + brows, 16), :] = jnp.zeros((gx, 16, 128), F32)
    for n, dk in [*enumerate(far_first(nk), 1), (0, 0)]:
        if n == 0:
            own_copy.wait()
        src = blocks[n] if n else own_ref
        kk = partner(k, dk, nk)
        for q in range(bx):
            got = src[pl.ds(q * brows, brows), :]
            vol_ref[kk * bx + q, pl.ds(16, brows), :] = got.astype(F32)
            half_ref[pl.ds(pl.multiple_of((kk * bx + q) * brows, brows), brows), :] = got

    cell = depth_of(brows, gz)
    for x in range(gx):
        for n, step in enumerate(STEPS):
            col_ref[pl.ds(x * brows, brows), pl.ds(n * 128, 128)] = shifted(
                vol_ref, (x,), 16, brows, cell, gz, step
            ).astype(BF)

    we_copy.wait()
    wl_copy.start()
    for n in range(9):
        b, c = divmod(n, 3)
        for a in range(3):
            wcat_ref[pl.ds(n * 128, 128), pl.ds(a * 128, 128)] = we_ref[a, b, c]
    p_ref[...] = jnp.dot(col_ref[...], wcat_ref[...], preferred_element_type=F32)

    outer = pl.multiple_of((brows - gz) * (1 - j), gz)
    inner = pl.multiple_of((brows - 2 * gz) * (1 - j) + gz * j, gz)
    for x in range(gx):
        row_ref[pl.ds(x * gz, gz), :] = vol_ref[x, pl.ds(16 + outer, gz), :]
    row = row_ref[...]
    rcell = depth_of(line, gz)
    trio = [
        jnp.where(rcell == 0, 0.0, pltpu.roll(row, 1, 0)),
        row,
        jnp.where(rcell == gz - 1, 0.0, pltpu.roll(row, line - 1, 0)),
    ]
    taps = wcat_ref[pl.ds(pl.multiple_of(j * (6 * 128), 128), 3 * 128), :]
    given = jnp.dot(jnp.concatenate(trio, axis=1).astype(BF), taps, preferred_element_type=F32)
    given = fold([given[:, a * 128 : (a + 1) * 128] for a in range(3)], gz)

    for lq in range(lx):
        pair = None
        for x in (2 * lq, 2 * lq + 1):
            pre = p_ref[pl.ds(x * brows, brows), pl.ds(128, 128)]
            if x > 0:
                pre = pre + p_ref[pl.ds((x - 1) * brows, brows), pl.ds(0, 128)]
            if x < gx - 1:
                pre = pre + p_ref[pl.ds((x + 1) * brows, brows), pl.ds(256, 128)]
            pre_ref[x] = pre
            h, slope = gelu_and_slope(pre)
            slope_ref[pl.ds(x * brows, brows), :] = slope
            pair = h if pair is None else pair + h
        wide = pair.reshape(by // 2, 2, gz, 128)
        h_ref[...] = (wide[:, 0] + wide[:, 1]).reshape(by // 2 * gz, 128)
        pooled = (h_ref[pl.ds(0, hl, stride=2), :] + h_ref[pl.ds(1, hl, stride=2), :]) * 0.125
        send_ref[pl.ds(lq * hl, hl), :] = pooled.astype(BF)
    for x in range(gx):
        edge_ref[pl.ds(x * gz, gz), :] = pre_ref[x, pl.ds(inner, gz), :]
        edge_ref[pl.ds(line + x * gz, gz), :] = pre_ref[x, pl.ds(outer, gz), :]
    edge_ref[pl.ds(2 * line, line), :] = given
    send_ref[pl.ds(lx * hl, 3 * line), :] = edge_ref[...].astype(BF)
    wl_copy.wait()


def border_pool(inner, outer, tmp_ref, tile_ref, dims):
    lx, lz, gz = dims
    h, slope = gelu_and_slope(outer)
    h = (h + gelu_and_slope(inner)[0]).reshape(lx, 2, gz, 128)
    tmp_ref[...] = (h[:, 0] + h[:, 1]).reshape(lx * gz, 128)
    got = (tmp_ref[pl.ds(0, lx * lz, stride=2), :] + tmp_ref[pl.ds(1, lx * lz, stride=2), :]) * 0.125
    got = got.astype(BF).astype(F32)
    for x in range(lx):
        for copy in range(2):
            tile_ref[pl.ds((2 * x + copy) * lz, lz), :] = got[x * lz : (x + 1) * lz]
    return slope


def late_kernel(*refs, nk, dims):
    gx, gz, lx, ly, lz, cx = dims
    sent_ref, got_ref, edge_ref, cots, refs = *refs[:3], refs[3 : nk + 3], refs[nk + 3 :]
    wl_ref, pd_ref, back_ref, mine_ref, patch_ref = refs[:5]
    pool_ref, lcol_ref, dl_ref, cot_ref, tmp_ref, tile_ref = refs[5:]
    lplane, hl, line = ly * lz, ly // 2 * lz, gx * gz
    cl = wl_ref.shape[-1]
    crow = cx * lplane
    k, j = lax.axis_index("space"), lax.axis_index("chan")
    edges = got_ref[pl.ds(lx * hl, 3 * line), :].astype(F32)
    lrow = lax.broadcasted_iota(jnp.int32, (hl, 128), 0)
    for x in range(lx):
        pool_ref[x, pl.ds(0, 8), :] = jnp.zeros((8, 128), F32)
        pool_ref[x, pl.ds(8 + lplane, 8), :] = jnp.zeros((8, 128), F32)
    sides = (
        (j, sent_ref, edge_ref[pl.ds(0, line), :], edge_ref[pl.ds(line, line), :] + edges[2 * line :]),
        (1 - j, got_ref, edges[:line], edges[line : 2 * line] + edge_ref[pl.ds(2 * line, line), :]),
    )
    for n, (side, ref, inner, outer) in enumerate(sides):
        slope = border_pool(inner, outer, tmp_ref, tile_ref, (lx, lz, gz))
        if n == 0:
            patch_ref[...] = slope
        first = (hl - lz) * (1 - side)
        border = (lrow >= first) & (lrow < first + lz)
        for x in range(lx):
            tiles = jnp.concatenate([tile_ref[pl.ds(x * 2 * lz, 2 * lz), :]] * (hl // (2 * lz)), axis=0)
            start = pl.multiple_of(8 + side * hl, 8)
            pool_ref[x, pl.ds(start, hl), :] = jnp.where(
                border, tiles, ref[pl.ds(x * hl, hl), :].astype(F32)
            )
    for x in range(lx):
        pd_ref[pl.ds(x * lplane, lplane), pl.ds(0, 128)] = pool_ref[x, pl.ds(8, lplane), :].astype(BF)

    lcell = depth_of(lplane, lz)
    for x in range(lx):
        for n, step in enumerate(STEPS):
            lcol_ref[pl.ds(x * lplane, lplane), pl.ds(n * 128, 128)] = shifted(
                pool_ref, (x,), 8, lplane, lcell, lz, step
            ).astype(BF)
    lcol = lcol_ref[...]
    parts = [
        jnp.dot(lcol, wl_ref[a].reshape(9 * 128, cl), preferred_element_type=F32) for a in range(3)
    ]
    for x in range(lx):
        dl_ref[x, pl.ds(0, 8), :] = jnp.zeros((8, cl), F32)
        dl_ref[x, pl.ds(8 + lplane, 8), :] = jnp.zeros((8, cl), F32)
    pre = fold(parts, lplane)
    slope = gelu_and_slope(pre)[1]
    for n, dk in enumerate([0, *far_first(nk)]):
        kk = partner(k, dk, nk)
        start = pl.multiple_of(kk * crow, 8)
        cot_ref[pl.ds(start, crow), :] = cots[n][...].astype(F32)
    delta = (cot_ref[...] * slope).astype(BF)
    pd_ref[:, pl.ds(128, cl)] = delta
    wide = delta.astype(F32)
    for x in range(lx):
        dl_ref[x, pl.ds(8, lplane), :] = wide[x * lplane : (x + 1) * lplane]
    total = None
    for n, (b, c) in enumerate(STEPS):
        part = jnp.concatenate(
            [shifted(dl_ref, (x,), 8, lplane, lcell, lz, (-b, -c)) for x in range(lx)], axis=0
        ).astype(BF)
        w = wl_ref[:, b + 1, c + 1].reshape(3 * 128, cl)
        term = lax.dot_general(part, w, NT, preferred_element_type=F32)
        total = term if total is None else total + term
    back = fold([total[:, (2 - a) * 128 : (3 - a) * 128] for a in range(3)], lplane)
    back_ref[...] = back.astype(BF)
    mine_ref[...] = back


def late_grad_kernel(mine_ref, other_ref, out_ref, pool_ref, lcol_ref, *, dims, scale):
    lx, ly, lz = dims
    lplane = ly * lz
    rows = lx * lplane
    lcell = depth_of(lplane, lz)
    pool_ref[...] = jnp.zeros(pool_ref.shape, F32)
    for s, ref in enumerate((mine_ref, other_ref)):
        for x in range(lx):
            pool_ref[s, x + 1, pl.ds(8, lplane), :] = ref[pl.ds(x * lplane, lplane), pl.ds(0, 128)].astype(F32)
        for x in range(lx + 2):
            for n, step in enumerate(STEPS):
                lcol_ref[s, pl.ds(x * lplane, lplane), pl.ds(n * 128, 128)] = shifted(
                    pool_ref, (s, x), 8, lplane, lcell, lz, step
                ).astype(BF)
    cl = mine_ref.shape[1] - 128
    delta = jnp.concatenate([mine_ref[:, pl.ds(128, cl)], other_ref[:, pl.ds(128, cl)]], axis=0)
    for a in range(3):
        left = jnp.concatenate([lcol_ref[s, pl.ds(a * lplane, rows), :] for s in (0, 1)], axis=0)
        got = lax.dot_general(left, delta, (((0,), (0,)), ((), ())), preferred_element_type=F32)
        out_ref[pl.ds(a * 9 * 128, 9 * 128), :] = (got * scale).astype(BF)


def other_kernel(
    half_ref, got_ref, wcat_ref, col_ref, slope_ref, vol_ref, p_ref, *, dims
):
    gx, gy, gz, lx, ly, lz, bx, by = dims
    brows = by * gz
    j = lax.axis_index("chan")
    vol_ref[:, :, pl.ds(0, 16), :] = jnp.zeros((2, gx, 16, 128), F32)
    vol_ref[:, :, pl.ds(16 + brows, 16), :] = jnp.zeros((2, gx, 16, 128), F32)
    for h, src in enumerate((half_ref, got_ref)):
        for x in range(gx):
            vol_ref[h, x, pl.ds(16, brows), :] = src[pl.ds(x * brows, brows), :].astype(F32)
    for h, side in enumerate((j, 1 - j)):
        into = pl.multiple_of((16 + brows) * (1 - side) + (16 - gz) * side, 8)
        start = pl.multiple_of(16 + (brows - gz) * side, 8)
        for x in range(gx):
            vol_ref[h, x, pl.ds(into, gz), :] = vol_ref[1 - h, x, pl.ds(start, gz), :]
    cell = depth_of(brows, gz)
    for h in (1, 0):
        for x in range(gx):
            for n, step in enumerate(STEPS):
                col_ref[pl.ds((h * gx + x) * brows, brows), pl.ds(n * 128, 128)] = shifted(
                    vol_ref, (h, x), 16, brows, cell, gz, step
                ).astype(BF)
    p_ref[...] = jnp.dot(
        col_ref[pl.ds(gx * brows, gx * brows), :], wcat_ref[...], preferred_element_type=F32
    )
    for x in range(gx):
        pre = p_ref[pl.ds(x * brows, brows), pl.ds(128, 128)]
        if x > 0:
            pre = pre + p_ref[pl.ds((x - 1) * brows, brows), pl.ds(0, 128)]
        if x < gx - 1:
            pre = pre + p_ref[pl.ds((x + 1) * brows, brows), pl.ds(256, 128)]
        slope_ref[pl.ds(x * brows, brows), :] = gelu_and_slope(pre)[1]


def early_grad_kernel(
    mine_ref, other_ref, slope_ref, far_ref, patch_ref, col_ref,
    part_ref, win_ref, wide_ref, d_ref, dt_ref, *, dims
):
    gx, gy, gz, lx, ly, lz, bx, by = dims
    plane, lplane = gy * gz, ly * lz
    k, j = lax.axis_index("space"), lax.axis_index("chan")
    brows = by * gz
    span = (gx + 2) * brows
    for q in (0, gx + 1):
        d_ref[q] = jnp.zeros(d_ref.shape[1:], F32)
    d_ref[:, pl.ds(0, 16), :] = jnp.zeros((gx + 2, 16, 128), F32)
    d_ref[:, pl.ds(16 + plane, 16), :] = jnp.zeros((gx + 2, 16, 128), F32)
    for h in (0, 1):
        dt_ref[:, pl.ds(h * span, brows)] = jnp.zeros((128, brows), BF)
        dt_ref[:, pl.ds((h + 1) * span - brows, brows)] = jnp.zeros((128, brows), BF)
    back = (mine_ref[...] + other_ref[...].astype(F32)) * 0.125
    wide_ref[pl.ds(0, lx * lplane, stride=2), :] = back
    wide_ref[pl.ds(1, lx * lplane, stride=2), :] = back
    first = (brows - gz) * (1 - j)
    row = lax.broadcasted_iota(jnp.int32, (brows, 128), 0)
    border = (row >= first) & (row < first + gz)
    for lq in range(lx):
        for h, side in enumerate((j, 1 - j)):
            start = pl.multiple_of(lq * ly * gz + side * (by // 2 * gz), 8)
            rows = wide_ref[pl.ds(start, by // 2 * gz), :].reshape(by // 2, 1, gz, 128)
            rows = jnp.broadcast_to(rows, (by // 2, 2, gz, 128)).reshape(brows, 128)
            for x in (2 * lq, 2 * lq + 1):
                slope = (far_ref if h else slope_ref)[pl.ds(x * brows, brows), :]
                if h == 0:
                    tiles = jnp.concatenate([patch_ref[pl.ds(x * gz, gz), :]] * by, axis=0)
                    slope = jnp.where(border, tiles, slope)
                delta = (rows * slope).astype(BF).astype(F32)
                d_ref[x + 1, pl.ds(pl.multiple_of(16 + side * brows, 8), brows), :] = delta
                dt_ref[:, pl.ds(h * span + (x + 1) * brows, brows)] = delta.T.astype(BF)
    left = jnp.concatenate(
        [
            jnp.concatenate(
                [dt_ref[:, pl.ds(h * span + (2 - a) * brows, gx * brows)] for h in (0, 1)], axis=1
            )
            for a in range(3)
        ],
        axis=0,
    )
    got = jnp.dot(left, col_ref[...], preferred_element_type=F32)
    for a in range(3):
        for n in range(9):
            part_ref[pl.ds((a * 9 + n) * 128, 128), :] = got[
                a * 128 : (a + 1) * 128, n * 128 : (n + 1) * 128
            ].T.astype(part_ref.dtype)
    row = pl.multiple_of(j * brows, 8)
    for q in range(bx + 2):
        win_ref[q] = d_ref[k * bx + q, pl.ds(row, brows + 32), :]


def grad_volume_kernel(win_ref, we_ref, gv_ref, vcol_ref, wt_ref, *, bx, brows, gz):
    for n in range(9):
        b, c = divmod(n, 3)
        for a in range(3):
            wt_ref[a, pl.ds(n * 128, 128), :] = we_ref[a, b, c].astype(F32).T.astype(BF)
    cell = depth_of(brows, gz)
    for q in range(bx + 2):
        for n, (b, c) in enumerate(STEPS):
            vcol_ref[pl.ds(q * brows, brows), pl.ds(n * 128, 128)] = shifted(
                win_ref, (q,), 16, brows, cell, gz, (-b, -c)
            ).astype(BF)
    total = None
    for a in range(3):
        term = jnp.dot(vcol_ref[pl.ds((2 - a) * brows, bx * brows), :], wt_ref[a], preferred_element_type=F32)
        total = term if total is None else total + term
    gv_ref[...] = total.astype(BF)


def far_first(count):
    return range(count - 1, 0, -1)


def partner(index, by, count):
    if count & (count - 1) == 0:
        return index ^ by
    return lax.rem(index + count - by, count)


def turned(value, axis, by):
    count = lax.axis_size(axis)
    pairs = count & (count - 1) == 0
    return lax.ppermute(value, axis, [(i, i ^ by if pairs else (i + by) % count) for i in range(count)])


def call(kernel, outs, scratch, args, name, far=(), raw=()):
    args = [
        pltpu.with_memory_space_constraint(arg, pltpu.HBM if n in raw else pltpu.VMEM)
        for n, arg in enumerate(args)
    ]
    outs = [out if n in far else pltpu.VMEM(out.shape, out.dtype) for n, out in enumerate(outs)]
    return pl.pallas_call(
        kernel,
        out_shape=outs,
        in_specs=[
            pl.BlockSpec(memory_space=pltpu.HBM if n in raw else pltpu.VMEM) for n in range(len(args))
        ],
        out_specs=[pl.BlockSpec(memory_space=pltpu.VMEM)] * len(outs),
        scratch_shapes=scratch,
        compiler_params=pltpu.CompilerParams(vmem_limit_bytes=VMEM_BYTES),
        name=name,
    )(*args)


def whole_sample(volume, early_weight, late_weight, cotangent):
    nk, nj, nr = (lax.axis_size(axis) for axis in ("space", "chan", "rep"))
    _, bx, by, gz, _ = volume.shape
    _, cx, ly, lz, cl = cotangent.shape
    gx, gy, lx = bx * nk, by * nj, cx * nk
    plane, lplane, brows = gy * gz, ly * lz, by * gz
    rows, lrows = gx * plane, lx * lplane
    scale = 1.0 / math.sqrt(nr * lrows)
    sds = jax.ShapeDtypeStruct

    mine = volume.reshape(bx * brows, 128)
    line = [mine] + [turned(mine, "space", dk) for dk in far_first(nk)]
    cot = cotangent.reshape(cx * lplane, cl)
    cots = [cot] + [turned(cot, "space", dk) for dk in far_first(nk)]

    dims = (gx, gy, gz, lx, ly, lz, bx, by)
    hrows, edge = gx * brows, 3 * gx * gz
    we, wl, wcat, half, slope, send, edges = call(
        functools.partial(early_kernel, nk=nk, dims=dims),
        [
            sds(early_weight.shape, BF),
            sds(late_weight.shape, BF),
            sds((9 * 128, 3 * 128), BF),
            sds((hrows, 128), BF),
            sds((hrows, 128), F32),
            sds((lrows // 2 + edge, 128), BF),
            sds((edge, 128), F32),
        ],
        [
            pltpu.VMEM((gx, brows + 32, 128), F32),
            pltpu.VMEM((bx * brows, 128), BF),
            pltpu.VMEM((hrows, 9 * 128), BF),
            pltpu.VMEM((hrows, 3 * 128), F32),
            pltpu.VMEM((gx, brows, 128), F32),
            pltpu.VMEM((by // 2 * gz, 128), F32),
            pltpu.VMEM((gx * gz, 128), F32),
            pltpu.SemaphoreType.DMA((3,)),
        ],
        line + [early_weight, late_weight],
        "early",
        raw=(0, nk, nk + 1),
    )
    ready, *cots[1:] = lax.optimization_barrier((send, *cots[1:]))
    send_other = turned(ready, "chan", 1)
    half_other = turned(half, "chan", 1)
    pooled_delta, back, back_mine, patch = call(
        functools.partial(late_kernel, nk=nk, dims=(gx, gz, lx, ly, lz, cx)),
        [
            sds((lrows, 128 + cl), BF),
            sds((lrows, 128), BF),
            sds((lrows, 128), F32),
            sds((gx * gz, 128), F32),
        ],
        [
            pltpu.VMEM((lx, lplane + 16, 128), F32),
            pltpu.VMEM((lrows, 9 * 128), BF),
            pltpu.VMEM((lx, lplane + 16, cl), F32),
            pltpu.VMEM((lrows, cl), F32),
            pltpu.VMEM((lx * gz, 128), F32),
            pltpu.VMEM((lx * 2 * lz, 128), F32),
        ],
        [send, send_other, edges] + cots + [wl],
        "late",
    )
    pd_other = turned(pooled_delta, "rep", 1)
    back_other = turned(back, "chan", 1)
    (late,) = call(
        functools.partial(late_grad_kernel, dims=(lx, ly, lz), scale=scale),
        [sds((27 * 128, cl), BF)],
        [pltpu.VMEM((2, lx + 2, lplane + 16, 128), F32), pltpu.VMEM((2, (lx + 2) * lplane, 9 * 128), BF)],
        [pooled_delta, pd_other],
        "late_grad",
        far=(0,),
    )
    half_other, wcat, _ = lax.optimization_barrier((half_other, wcat, back))
    col, far_slope = call(
        functools.partial(other_kernel, dims=dims),
        [sds((rows, 9 * 128), BF), sds((hrows, 128), F32)],
        [pltpu.VMEM((2, gx, brows + 32, 128), F32), pltpu.VMEM((hrows, 3 * 128), F32)],
        [half, half_other, wcat],
        "other",
    )
    back_mine, late = lax.optimization_barrier((back_mine, late))
    part, win = call(
        functools.partial(early_grad_kernel, dims=dims),
        [sds((27 * 128, 128), BF), sds((bx + 2, brows + 32, 128), F32)],
        [
            pltpu.VMEM((lx * ly * gz, 128), F32),
            pltpu.VMEM((gx + 2, plane + 32, 128), F32),
            pltpu.VMEM((128, (gx + 2) * plane), BF),
        ],
        [back_mine, back_other, slope, far_slope, patch, col],
        "early_grad",
    )
    part_other = turned(part, "rep", 1)
    (gv,) = call(
        functools.partial(grad_volume_kernel, bx=bx, brows=brows, gz=gz),
        [sds((bx * brows, 128), BF)],
        [pltpu.VMEM(((bx + 2) * brows, 9 * 128), BF), pltpu.VMEM((3, 9 * 128, 128), BF)],
        [win, we],
        "grad_volume",
        far=(0,),
    )
    early = ((part.astype(F32) + part_other.astype(F32)) * scale).astype(BF)
    return (
        early.reshape(3, 3, 3, 128, 128),
        late.reshape(3, 3, 3, 128, cl),
        gv.reshape(1, bx, by, gz, 128),
    )


def solution(mesh):
    few = mesh.shape["space"] * mesh.shape["chan"] <= GATHER_BLOCKS
    alone = mesh.shape["rep"] == 2 and mesh.shape["chan"] == 2
    return jax.shard_map(
        whole_sample if few and alone else per_device,
        mesh=mesh,
        in_specs=(
            P(("groups", "rep"), "space", "chan", None, None),
            P(),
            P(None, None, None, None, "chan"),
            P(("groups", "rep"), "space", None, None, "chan"),
        ),
        out_specs=(
            P("groups", None, None, None, None),
            P("groups", None, None, None, "chan"),
            P(("groups", "rep"), "space", "chan", None, None),
        ),
        check_vma=False,
    )
```

```python
import functools
import math

import jax
import jax.numpy as jnp
from jax import lax
from jax.experimental import pallas as pl
from jax.experimental.pallas import tpu as pltpu
from jax.sharding import PartitionSpec as P

BF = jnp.bfloat16
F32 = jnp.float32
VMEM_BYTES = 14 * 2**20
GATHER_BLOCKS = 8


def padded_2(block, sides, width):
    for axis, dim in sides:
        count = lax.axis_size(axis)
        forward = [(i, i + 1) for i in range(count - 1)]
        backward = [(target, source) for source, target in forward]
        low = lax.ppermute(
            lax.slice_in_dim(block, block.shape[dim] - width, None, axis=dim), axis, forward
        )
        high = lax.ppermute(lax.slice_in_dim(block, 0, width, axis=dim), axis, backward)
        block = jnp.concatenate([low, block, high], axis=dim)
    return block


def gelu_tanh(value):
    return jax.nn.gelu(value, approximate=True)


def conv_padded(padded, weight):
    depth = padded.shape[1] - 2
    height = padded.shape[2] - 2
    length = padded.shape[3] - 2
    total = None
    for first in range(3):
        for second in range(3):
            for third in range(3):
                window = padded[
                    :, first : first + depth, second : second + height, third : third + length
                ]
                term = jnp.einsum(
                    "sxyzc,co->sxyzo",
                    window,
                    weight[first, second, third],
                    preferred_element_type=jnp.float32,
                )
                total = term if total is None else total + term
    return total


def kernel_grad(padded, delta):
    depth = delta.shape[1]
    height = delta.shape[2]
    length = delta.shape[3]
    planes = []
    for first in range(3):
        for second in range(3):
            for third in range(3):
                window = padded[
                    :, first : first + depth, second : second + height, third : third + length
                ]
                planes.append(
                    jnp.einsum("sxyzc,sxyzo->co", window, delta, preferred_element_type=jnp.float32)
                )
    stacked = jnp.stack(planes, axis=0)
    return stacked.reshape((3, 3, 3) + stacked.shape[1:])


def flipped(weight):
    return jnp.swapaxes(weight[::-1, ::-1, ::-1], 3, 4)


def pad_dims(field, dims):
    widths = [(1, 1) if place in dims else (0, 0) for place in range(field.ndim)]
    return jnp.pad(field, widths)


def pool_cells(field):
    s, x, y, z, c = field.shape
    return jnp.mean(field.reshape(s, x // 2, 2, y // 2, 2, z // 2, 2, c), axis=(2, 4, 6))


def spread_cells(field):
    s, x, y, z, c = field.shape
    wide = jnp.broadcast_to(field[:, :, None, :, None, :, None, :], (s, x, 2, y, 2, z, 2, c))
    return wide.reshape(s, 2 * x, 2 * y, 2 * z, c) * 0.125


def late_layer(joined, late_weight, cotangent):
    rim = padded_2(joined, (("space", 1),), 1)
    late_pad = pad_dims(rim, (2, 3))
    pre_late = conv_padded(late_pad, late_weight)
    delta_late = jax.vjp(gelu_tanh, pre_late)[1](cotangent.astype(jnp.float32))[0].astype(
        jnp.bfloat16
    )
    late_part = kernel_grad(late_pad, delta_late)
    delta_rim = padded_2(delta_late, (("space", 1),), 1)
    back_partial = conv_padded(pad_dims(delta_rim, (2, 3)), flipped(late_weight))
    return (back_partial, late_part)


def per_device(volume, early_weight, late_weight, cotangent):
    count = (
        cotangent.shape[0]
        * lax.axis_size("rep")
        * cotangent.shape[1]
        * lax.axis_size("space")
        * cotangent.shape[2]
        * cotangent.shape[3]
    )
    scale = 1.0 / math.sqrt(count)
    haloed = padded_2(volume, (("space", 1), ("chan", 2)), 1)
    padded_in = pad_dims(haloed, (3,))
    pre_early = conv_padded(padded_in, early_weight)
    pooled = pool_cells(gelu_tanh(pre_early)).astype(jnp.bfloat16)
    joined = lax.all_gather(pooled, "chan", axis=2, tiled=True)
    back_partial, late_part = late_layer(joined, late_weight, cotangent)
    back_rows = lax.psum_scatter(back_partial, "chan", scatter_dimension=2, tiled=True)
    delta_early = jax.vjp(gelu_tanh, pre_early)[1](spread_cells(back_rows))[0].astype(jnp.bfloat16)
    early_part = kernel_grad(padded_in, delta_early)
    delta_halo = padded_2(delta_early, (("space", 1), ("chan", 2)), 1)
    grad_volume = conv_padded(pad_dims(delta_halo, (3,)), flipped(early_weight)).astype(
        jnp.bfloat16
    )
    early_total = lax.psum(early_part, ("space", "chan", "rep"))
    grad_early = (early_total * scale).astype(jnp.bfloat16)
    late_total = lax.psum(late_part, ("space", "rep"))
    grad_late = (late_total * scale).astype(jnp.bfloat16)
    return (grad_early, grad_late, grad_volume)


NT = (((1,), (1,)), ((), ()))


def gelu_and_slope(v):
    k = 0.7978845608028654
    sq = v * v
    t = jnp.tanh(k * (v + 0.044715 * (v * sq)))
    half = 0.5 * (1.0 + t)
    return v * half, half + 0.5 * v * (1.0 - t * t) * (k * (1.0 + 0.134145 * sq))


def depth_of(rows, period):
    return lax.broadcasted_iota(jnp.int32, (rows, 128), 0) % period


def shifted(ref, lead, start, rows, cell, period, step):
    dy, dz = step
    got = ref[lead + (pl.ds(start + dy * period + dz, rows), slice(None))]
    if dz == 0:
        return got
    lanes = got.shape[1] // 128
    edge = (cell == 0) if dz < 0 else (cell == period - 1)
    edge = jnp.concatenate([edge] * lanes, axis=1) if lanes > 1 else edge
    return jnp.where(edge, 0.0, got)


STEPS = [(b, c) for b in (-1, 0, 1) for c in (-1, 0, 1)]


def fold(parts, rows):
    zero = jnp.zeros((rows, parts[0].shape[1]), F32)
    return (
        parts[1]
        + jnp.concatenate([zero, parts[0][:-rows]], axis=0)
        + jnp.concatenate([parts[2][rows:], zero], axis=0)
    )


def begin_kernel(own_hbm, we_hbm, own_ref, we_ref, wcat_ref, sems):
    own = pltpu.make_async_copy(own_hbm, own_ref, sems.at[3])
    copies = [pltpu.make_async_copy(we_hbm.at[a], we_ref.at[a], sems.at[a]) for a in range(3)]
    for copy in (*copies, own):
        copy.start()
    for a in range(3):
        copies[a].wait()
        for n in range(9):
            b, c = divmod(n, 3)
            wcat_ref[pl.ds(n * 128, 128), pl.ds(a * 128, 128)] = we_ref[a, b, c]
    own.wait()


def early_kernel(*refs, nk, dims):
    gx, gy, gz, lx, ly, lz, bx, by = dims
    blocks, refs = refs[:nk], refs[nk:]
    wcat_ref, half_ref, slope_ref, send_ref, edge_ref = refs[:5]
    vol_ref, col_ref, p_ref, pre_ref, h_ref, row_ref = refs[5:]
    k, j = lax.axis_index("space"), lax.axis_index("chan")
    brows, hl, line = by * gz, by // 2 * lz, gx * gz
    vol_ref[:, pl.ds(0, 16), :] = jnp.zeros((gx, 16, 128), F32)
    vol_ref[:, pl.ds(16 + brows, 16), :] = jnp.zeros((gx, 16, 128), F32)
    for n, dk in enumerate([0, *far_first(nk)]):
        src = blocks[n]
        kk = partner(k, dk, nk)
        for q in range(bx):
            got = src[pl.ds(q * brows, brows), :]
            vol_ref[kk * bx + q, pl.ds(16, brows), :] = got.astype(F32)
            half_ref[pl.ds(pl.multiple_of((kk * bx + q) * brows, brows), brows), :] = got

    cell = depth_of(brows, gz)
    for x in range(gx):
        for n, step in enumerate(STEPS):
            col_ref[pl.ds(x * brows, brows), pl.ds(n * 128, 128)] = shifted(
                vol_ref, (x,), 16, brows, cell, gz, step
            ).astype(BF)

    p_ref[...] = jnp.dot(col_ref[...], wcat_ref[...], preferred_element_type=F32)

    outer = pl.multiple_of((brows - gz) * (1 - j), gz)
    inner = pl.multiple_of((brows - 2 * gz) * (1 - j) + gz * j, gz)
    for x in range(gx):
        row_ref[pl.ds(x * gz, gz), :] = vol_ref[x, pl.ds(16 + outer, gz), :]
    row = row_ref[...]
    rcell = depth_of(line, gz)
    trio = [
        jnp.where(rcell == 0, 0.0, pltpu.roll(row, 1, 0)),
        row,
        jnp.where(rcell == gz - 1, 0.0, pltpu.roll(row, line - 1, 0)),
    ]
    taps = wcat_ref[pl.ds(pl.multiple_of(j * (6 * 128), 128), 3 * 128), :]
    given = jnp.dot(jnp.concatenate(trio, axis=1).astype(BF), taps, preferred_element_type=F32)
    given = fold([given[:, a * 128 : (a + 1) * 128] for a in range(3)], gz)

    for lq in range(lx):
        pair = None
        for x in (2 * lq, 2 * lq + 1):
            pre = p_ref[pl.ds(x * brows, brows), pl.ds(128, 128)]
            if x > 0:
                pre = pre + p_ref[pl.ds((x - 1) * brows, brows), pl.ds(0, 128)]
            if x < gx - 1:
                pre = pre + p_ref[pl.ds((x + 1) * brows, brows), pl.ds(256, 128)]
            pre_ref[x] = pre
            h, slope = gelu_and_slope(pre)
            slope_ref[pl.ds(x * brows, brows), :] = slope
            pair = h if pair is None else pair + h
        wide = pair.reshape(by // 2, 2, gz, 128)
        h_ref[...] = (wide[:, 0] + wide[:, 1]).reshape(by // 2 * gz, 128)
        pooled = (h_ref[pl.ds(0, hl, stride=2), :] + h_ref[pl.ds(1, hl, stride=2), :]) * 0.125
        send_ref[pl.ds(lq * hl, hl), :] = pooled.astype(BF)
    for x in range(gx):
        edge_ref[pl.ds(x * gz, gz), :] = pre_ref[x, pl.ds(inner, gz), :]
        edge_ref[pl.ds(line + x * gz, gz), :] = pre_ref[x, pl.ds(outer, gz), :]
    edge_ref[pl.ds(2 * line, line), :] = given
    send_ref[pl.ds(lx * hl, 3 * line), :] = edge_ref[...].astype(BF)


def fetch_kernel(far_ref, near_ref, back_ref, sems):
    copies = [pltpu.make_async_copy(far_ref.at[a], near_ref.at[a], sems.at[a]) for a in range(3)]
    cl = near_ref.shape[-1]
    for copy in copies:
        copy.start()
    for a in range(3):
        copies[a].wait()
        for n in range(9):
            b, c = divmod(n, 3)
            back_ref[pl.ds(n * cl, cl), pl.ds(a * 128, 128)] = near_ref[a, b, c].astype(F32).T.astype(BF)


def border_pool(inner, outer, tmp_ref, tile_ref, dims):
    lx, lz, gz = dims
    h, slope = gelu_and_slope(outer)
    h = (h + gelu_and_slope(inner)[0]).reshape(lx, 2, gz, 128)
    tmp_ref[...] = (h[:, 0] + h[:, 1]).reshape(lx * gz, 128)
    got = (tmp_ref[pl.ds(0, lx * lz, stride=2), :] + tmp_ref[pl.ds(1, lx * lz, stride=2), :]) * 0.125
    got = got.astype(BF).astype(F32)
    for x in range(lx):
        for copy in range(2):
            tile_ref[pl.ds((2 * x + copy) * lz, lz), :] = got[x * lz : (x + 1) * lz]
    return slope


def late_kernel(*refs, nk, dims):
    gx, gz, lx, ly, lz, cx = dims
    sent_ref, got_ref, edge_ref, cots, refs = *refs[:3], refs[3 : nk + 3], refs[nk + 3 :]
    wl_ref, wback_ref, pd_ref, back_ref, mine_ref, patch_ref = refs[:6]
    pool_ref, lcol_ref, dl_ref, dcol_ref, cot_ref, tmp_ref, tile_ref = refs[6:]
    lplane, hl, line = ly * lz, ly // 2 * lz, gx * gz
    cl = wl_ref.shape[-1]
    crow = cx * lplane
    k, j = lax.axis_index("space"), lax.axis_index("chan")
    edges = got_ref[pl.ds(lx * hl, 3 * line), :].astype(F32)
    lrow = lax.broadcasted_iota(jnp.int32, (hl, 128), 0)
    for x in range(lx):
        pool_ref[x, pl.ds(0, 8), :] = jnp.zeros((8, 128), F32)
        pool_ref[x, pl.ds(8 + lplane, 8), :] = jnp.zeros((8, 128), F32)
    sides = (
        (j, sent_ref, edge_ref[pl.ds(0, line), :], edge_ref[pl.ds(line, line), :] + edges[2 * line :]),
        (1 - j, got_ref, edges[:line], edges[line : 2 * line] + edge_ref[pl.ds(2 * line, line), :]),
    )
    for n, (side, ref, inner, outer) in enumerate(sides):
        slope = border_pool(inner, outer, tmp_ref, tile_ref, (lx, lz, gz))
        if n == 0:
            patch_ref[...] = slope
        first = (hl - lz) * (1 - side)
        border = (lrow >= first) & (lrow < first + lz)
        for x in range(lx):
            tiles = jnp.concatenate([tile_ref[pl.ds(x * 2 * lz, 2 * lz), :]] * (hl // (2 * lz)), axis=0)
            start = pl.multiple_of(8 + side * hl, 8)
            pool_ref[x, pl.ds(start, hl), :] = jnp.where(
                border, tiles, ref[pl.ds(x * hl, hl), :].astype(F32)
            )
    for x in range(lx):
        pd_ref[pl.ds(x * lplane, lplane), pl.ds(0, 128)] = pool_ref[x, pl.ds(8, lplane), :].astype(BF)

    lcell = depth_of(lplane, lz)
    for x in range(lx):
        for n, step in enumerate(STEPS):
            lcol_ref[pl.ds(x * lplane, lplane), pl.ds(n * 128, 128)] = shifted(
                pool_ref, (x,), 8, lplane, lcell, lz, step
            ).astype(BF)
    lcol = lcol_ref[...]
    parts = [
        jnp.dot(lcol, wl_ref[a].reshape(9 * 128, cl), preferred_element_type=F32) for a in range(3)
    ]
    for x in range(lx):
        dl_ref[x, pl.ds(0, 8), :] = jnp.zeros((8, cl), F32)
        dl_ref[x, pl.ds(8 + lplane, 8), :] = jnp.zeros((8, cl), F32)
    pre = fold(parts, lplane)
    slope = gelu_and_slope(pre)[1]
    for n, dk in enumerate([0, *far_first(nk)]):
        kk = partner(k, dk, nk)
        start = pl.multiple_of(kk * crow, 8)
        cot_ref[pl.ds(start, crow), :] = cots[n][...].astype(F32)
    delta = (cot_ref[...] * slope).astype(BF)
    pd_ref[:, pl.ds(128, cl)] = delta
    wide = delta.astype(F32)
    for x in range(lx):
        dl_ref[x, pl.ds(8, lplane), :] = wide[x * lplane : (x + 1) * lplane]
    for n, (b, c) in enumerate(STEPS):
        for x in range(lx):
            dcol_ref[pl.ds(x * lplane, lplane), pl.ds(n * cl, cl)] = shifted(
                dl_ref, (x,), 8, lplane, lcell, lz, (-b, -c)
            ).astype(BF)
    total = jnp.dot(dcol_ref[...], wback_ref[...], preferred_element_type=F32)
    back = fold([total[:, (2 - a) * 128 : (3 - a) * 128] for a in range(3)], lplane)
    back_ref[...] = back.astype(BF)
    mine_ref[...] = back


def late_grad_kernel(mine_ref, other_ref, out_ref, pool_ref, lcol_ref, wide_ref, *, dims, scale):
    lx, ly, lz = dims
    lplane = ly * lz
    rows = lx * lplane
    cl = mine_ref.shape[1] - 128
    lcell = depth_of(lplane, lz)
    for x in range(lx):
        pool_ref[x, pl.ds(0, 8), :] = jnp.zeros((8, 128), F32)
        pool_ref[x, pl.ds(8 + lplane, 8), :] = jnp.zeros((8, 128), F32)
    for s, ref in enumerate((mine_ref, other_ref)):
        for x in range(lx):
            pool_ref[x, pl.ds(8, lplane), :] = ref[pl.ds(x * lplane, lplane), pl.ds(0, 128)].astype(F32)
        for x in range(lx):
            for n, step in enumerate(STEPS):
                lcol_ref[pl.ds(s * rows + x * lplane, lplane), pl.ds(n * 128, 128)] = shifted(
                    pool_ref, (x,), 8, lplane, lcell, lz, step
                ).astype(BF)
        zero = jnp.zeros((lplane, cl), BF)
        wide_ref[pl.ds(s * rows + rows - lplane, lplane), pl.ds(0, cl)] = zero
        wide_ref[pl.ds(s * rows, rows - lplane), pl.ds(0, cl)] = ref[pl.ds(lplane, rows - lplane), pl.ds(128, cl)]
        wide_ref[pl.ds(s * rows, rows), pl.ds(cl, cl)] = ref[:, pl.ds(128, cl)]
        wide_ref[pl.ds(s * rows, lplane), pl.ds(2 * cl, cl)] = zero
        wide_ref[pl.ds(s * rows + lplane, rows - lplane), pl.ds(2 * cl, cl)] = ref[
            pl.ds(0, rows - lplane), pl.ds(128, cl)
        ]
    got = lax.dot_general(
        lcol_ref[...], wide_ref[...], (((0,), (0,)), ((), ())), preferred_element_type=F32
    )
    for a in range(3):
        out_ref[pl.ds(a * 9 * 128, 9 * 128), :] = (got[:, a * cl : (a + 1) * cl] * scale).astype(BF)


def other_kernel(
    half_ref, got_ref, wcat_ref, col_ref, slope_ref, vol_ref, p_ref, *, dims
):
    gx, gy, gz, lx, ly, lz, bx, by = dims
    brows = by * gz
    j = lax.axis_index("chan")
    vol_ref[:, :, pl.ds(0, 16), :] = jnp.zeros((2, gx, 16, 128), F32)
    vol_ref[:, :, pl.ds(16 + brows, 16), :] = jnp.zeros((2, gx, 16, 128), F32)
    for h, src in enumerate((half_ref, got_ref)):
        for x in range(gx):
            vol_ref[h, x, pl.ds(16, brows), :] = src[pl.ds(x * brows, brows), :].astype(F32)
    for h, side in enumerate((j, 1 - j)):
        into = pl.multiple_of((16 + brows) * (1 - side) + (16 - gz) * side, 8)
        start = pl.multiple_of(16 + (brows - gz) * side, 8)
        for x in range(gx):
            vol_ref[h, x, pl.ds(into, gz), :] = vol_ref[1 - h, x, pl.ds(start, gz), :]
    cell = depth_of(brows, gz)
    for h in (1, 0):
        for x in range(gx):
            for n, step in enumerate(STEPS):
                col_ref[pl.ds((h * gx + x) * brows, brows), pl.ds(n * 128, 128)] = shifted(
                    vol_ref, (h, x), 16, brows, cell, gz, step
                ).astype(BF)
    p_ref[...] = jnp.dot(
        col_ref[pl.ds(gx * brows, gx * brows), :], wcat_ref[...], preferred_element_type=F32
    )
    for x in range(gx):
        pre = p_ref[pl.ds(x * brows, brows), pl.ds(128, 128)]
        if x > 0:
            pre = pre + p_ref[pl.ds((x - 1) * brows, brows), pl.ds(0, 128)]
        if x < gx - 1:
            pre = pre + p_ref[pl.ds((x + 1) * brows, brows), pl.ds(256, 128)]
        slope_ref[pl.ds(x * brows, brows), :] = gelu_and_slope(pre)[1]


def early_grad_kernel(
    mine_ref, other_ref, slope_ref, far_ref, patch_ref, col_ref,
    part_ref, win_ref, wide_ref, d_ref, dt_ref, *, dims
):
    gx, gy, gz, lx, ly, lz, bx, by = dims
    plane, lplane = gy * gz, ly * lz
    k, j = lax.axis_index("space"), lax.axis_index("chan")
    brows = by * gz
    span = (gx + 2) * brows
    for q in (0, gx + 1):
        d_ref[q] = jnp.zeros(d_ref.shape[1:], F32)
    d_ref[:, pl.ds(0, 16), :] = jnp.zeros((gx + 2, 16, 128), F32)
    d_ref[:, pl.ds(16 + plane, 16), :] = jnp.zeros((gx + 2, 16, 128), F32)
    for h in (0, 1):
        dt_ref[:, pl.ds(h * span, brows)] = jnp.zeros((128, brows), BF)
        dt_ref[:, pl.ds((h + 1) * span - brows, brows)] = jnp.zeros((128, brows), BF)
    back = (mine_ref[...] + other_ref[...].astype(F32)) * 0.125
    wide_ref[pl.ds(0, lx * lplane, stride=2), :] = back
    wide_ref[pl.ds(1, lx * lplane, stride=2), :] = back
    first = (brows - gz) * (1 - j)
    row = lax.broadcasted_iota(jnp.int32, (brows, 128), 0)
    border = (row >= first) & (row < first + gz)
    for lq in range(lx):
        for h, side in enumerate((j, 1 - j)):
            start = pl.multiple_of(lq * ly * gz + side * (by // 2 * gz), 8)
            rows = wide_ref[pl.ds(start, by // 2 * gz), :].reshape(by // 2, 1, gz, 128)
            rows = jnp.broadcast_to(rows, (by // 2, 2, gz, 128)).reshape(brows, 128)
            for x in (2 * lq, 2 * lq + 1):
                slope = (far_ref if h else slope_ref)[pl.ds(x * brows, brows), :]
                if h == 0:
                    tiles = jnp.concatenate([patch_ref[pl.ds(x * gz, gz), :]] * by, axis=0)
                    slope = jnp.where(border, tiles, slope)
                delta = (rows * slope).astype(BF).astype(F32)
                d_ref[x + 1, pl.ds(pl.multiple_of(16 + side * brows, 8), brows), :] = delta
                dt_ref[:, pl.ds(h * span + (x + 1) * brows, brows)] = delta.T.astype(BF)
    left = jnp.concatenate(
        [
            jnp.concatenate(
                [dt_ref[:, pl.ds(h * span + (2 - a) * brows, gx * brows)] for h in (0, 1)], axis=1
            )
            for a in range(3)
        ],
        axis=0,
    )
    got = jnp.dot(left, col_ref[...], preferred_element_type=F32)
    for a in range(3):
        for n in range(9):
            part_ref[pl.ds((a * 9 + n) * 128, 128), :] = got[
                a * 128 : (a + 1) * 128, n * 128 : (n + 1) * 128
            ].T.astype(part_ref.dtype)
    row = pl.multiple_of(j * brows, 8)
    for q in range(bx + 2):
        win_ref[q] = d_ref[k * bx + q, pl.ds(row, brows + 32), :]


def grad_volume_kernel(win_ref, we_ref, gv_ref, vcol_ref, wt_ref, *, bx, brows, gz):
    for n in range(9):
        b, c = divmod(n, 3)
        for a in range(3):
            wt_ref[a, pl.ds(n * 128, 128), :] = we_ref[a, b, c].astype(F32).T.astype(BF)
    cell = depth_of(brows, gz)
    for q in range(bx + 2):
        for n, (b, c) in enumerate(STEPS):
            vcol_ref[pl.ds(q * brows, brows), pl.ds(n * 128, 128)] = shifted(
                win_ref, (q,), 16, brows, cell, gz, (-b, -c)
            ).astype(BF)
    total = None
    for a in range(3):
        term = jnp.dot(vcol_ref[pl.ds((2 - a) * brows, bx * brows), :], wt_ref[a], preferred_element_type=F32)
        total = term if total is None else total + term
    gv_ref[...] = total.astype(BF)


def far_first(count):
    return range(count - 1, 0, -1)


def partner(index, by, count):
    if count & (count - 1) == 0:
        return index ^ by
    return lax.rem(index + count - by, count)


def turned(value, axis, by):
    count = lax.axis_size(axis)
    pairs = count & (count - 1) == 0
    return lax.ppermute(value, axis, [(i, i ^ by if pairs else (i + by) % count) for i in range(count)])


def call(kernel, outs, scratch, args, name, far=(), raw=()):
    args = [
        pltpu.with_memory_space_constraint(arg, pltpu.HBM if n in raw else pltpu.VMEM)
        for n, arg in enumerate(args)
    ]
    outs = [out if n in far else pltpu.VMEM(out.shape, out.dtype) for n, out in enumerate(outs)]
    return pl.pallas_call(
        kernel,
        out_shape=outs,
        in_specs=[
            pl.BlockSpec(memory_space=pltpu.HBM if n in raw else pltpu.VMEM) for n in range(len(args))
        ],
        out_specs=[pl.BlockSpec(memory_space=pltpu.VMEM)] * len(outs),
        scratch_shapes=scratch,
        compiler_params=pltpu.CompilerParams(vmem_limit_bytes=VMEM_BYTES),
        name=name,
    )(*args)


def whole_sample(volume, early_weight, late_weight, cotangent):
    nk, nj, nr = (lax.axis_size(axis) for axis in ("space", "chan", "rep"))
    _, bx, by, gz, _ = volume.shape
    _, cx, ly, lz, cl = cotangent.shape
    gx, gy, lx = bx * nk, by * nj, cx * nk
    plane, lplane, brows = gy * gz, ly * lz, by * gz
    rows, lrows = gx * plane, lx * lplane
    scale = 1.0 / math.sqrt(nr * lrows)
    sds = jax.ShapeDtypeStruct

    mine = volume.reshape(bx * brows, 128)
    line = [mine] + [turned(mine, "space", dk) for dk in far_first(nk)]
    cot = cotangent.reshape(cx * lplane, cl)
    own, we, wcat = call(
        begin_kernel,
        [sds(mine.shape, BF), sds(early_weight.shape, BF), sds((9 * 128, 3 * 128), BF)],
        [pltpu.SemaphoreType.DMA((4,))],
        [mine, early_weight],
        "begin",
        raw=(0, 1),
    )
    line[0] = own
    cots = [cot] + [turned(cot, "space", dk) for dk in far_first(nk)]

    dims = (gx, gy, gz, lx, ly, lz, bx, by)
    hrows, edge = gx * brows, 3 * gx * gz
    half, slope, send, edges = call(
        functools.partial(early_kernel, nk=nk, dims=dims),
        [
            sds((hrows, 128), BF),
            sds((hrows, 128), F32),
            sds((lrows // 2 + edge, 128), BF),
            sds((edge, 128), F32),
        ],
        [
            pltpu.VMEM((gx, brows + 32, 128), F32),
            pltpu.VMEM((hrows, 9 * 128), BF),
            pltpu.VMEM((hrows, 3 * 128), F32),
            pltpu.VMEM((gx, brows, 128), F32),
            pltpu.VMEM((by // 2 * gz, 128), F32),
            pltpu.VMEM((gx * gz, 128), F32),
        ],
        line + [wcat],
        "early",
    )
    ready, *cots[1:] = lax.optimization_barrier((send, *cots[1:]))
    send_other = turned(ready, "chan", 1)
    half_other = turned(half, "chan", 1)
    held, _ = lax.optimization_barrier((late_weight, send))
    wl, wback = call(
        fetch_kernel,
        [sds(late_weight.shape, BF), sds((9 * cl, 3 * 128), BF)],
        [pltpu.SemaphoreType.DMA((3,))],
        [held],
        "fetch",
        raw=(0,),
    )
    pooled_delta, back, back_mine, patch = call(
        functools.partial(late_kernel, nk=nk, dims=(gx, gz, lx, ly, lz, cx)),
        [
            sds((lrows, 128 + cl), BF),
            sds((lrows, 128), BF),
            sds((lrows, 128), F32),
            sds((gx * gz, 128), F32),
        ],
        [
            pltpu.VMEM((lx, lplane + 16, 128), F32),
            pltpu.VMEM((lrows, 9 * 128), BF),
            pltpu.VMEM((lx, lplane + 16, cl), F32),
            pltpu.VMEM((lrows, 9 * cl), BF),
            pltpu.VMEM((lrows, cl), F32),
            pltpu.VMEM((lx * gz, 128), F32),
            pltpu.VMEM((lx * 2 * lz, 128), F32),
        ],
        [send, send_other, edges] + cots + [wl, wback],
        "late",
    )
    pd_other = turned(pooled_delta, "rep", 1)
    back_other = turned(back, "chan", 1)
    (late,) = call(
        functools.partial(late_grad_kernel, dims=(lx, ly, lz), scale=scale),
        [sds((27 * 128, cl), BF)],
        [
            pltpu.VMEM((lx, lplane + 16, 128), F32),
            pltpu.VMEM((2 * lrows, 9 * 128), BF),
            pltpu.VMEM((2 * lrows, 3 * cl), BF),
        ],
        [pooled_delta, pd_other],
        "late_grad",
    )
    half_other, wcat, _ = lax.optimization_barrier((half_other, wcat, back))
    col, far_slope = call(
        functools.partial(other_kernel, dims=dims),
        [sds((rows, 9 * 128), BF), sds((hrows, 128), F32)],
        [pltpu.VMEM((2, gx, brows + 32, 128), F32), pltpu.VMEM((hrows, 3 * 128), F32)],
        [half, half_other, wcat],
        "other",
    )
    back_mine, late = lax.optimization_barrier((back_mine, late))
    part, win = call(
        functools.partial(early_grad_kernel, dims=dims),
        [sds((27 * 128, 128), BF), sds((bx + 2, brows + 32, 128), F32)],
        [
            pltpu.VMEM((lx * ly * gz, 128), F32),
            pltpu.VMEM((gx + 2, plane + 32, 128), F32),
            pltpu.VMEM((128, (gx + 2) * plane), BF),
        ],
        [back_mine, back_other, slope, far_slope, patch, col],
        "early_grad",
    )
    part_other = turned(part, "rep", 1)
    (gv,) = call(
        functools.partial(grad_volume_kernel, bx=bx, brows=brows, gz=gz),
        [sds((bx * brows, 128), BF)],
        [pltpu.VMEM(((bx + 2) * brows, 9 * 128), BF), pltpu.VMEM((3, 9 * 128, 128), BF)],
        [win, we],
        "grad_volume",
        far=(0,),
    )
    early = ((part.astype(F32) + part_other.astype(F32)) * scale).astype(BF)
    return (
        early.reshape(3, 3, 3, 128, 128),
        late.reshape(3, 3, 3, 128, cl),
        gv.reshape(1, bx, by, gz, 128),
    )


def solution(mesh):
    few = mesh.shape["space"] * mesh.shape["chan"] <= GATHER_BLOCKS
    alone = mesh.shape["rep"] == 2 and mesh.shape["chan"] == 2
    return jax.shard_map(
        whole_sample if few and alone else per_device,
        mesh=mesh,
        in_specs=(
            P(("groups", "rep"), "space", "chan", None, None),
            P(),
            P(None, None, None, None, "chan"),
            P(("groups", "rep"), "space", None, None, "chan"),
        ),
        out_specs=(
            P("groups", None, None, None, None),
            P("groups", None, None, None, "chan"),
            P(("groups", "rep"), "space", "chan", None, None),
        ),
        check_vma=False,
    )
```

```python
import functools
import math

import jax
import jax.numpy as jnp
from jax import lax
from jax.experimental import pallas as pl
from jax.experimental.pallas import tpu as pltpu
from jax.sharding import PartitionSpec as P

BF = jnp.bfloat16
F32 = jnp.float32
VMEM_BYTES = 14 * 2**20
GATHER_BLOCKS = 8


def padded_2(block, sides, width):
    for axis, dim in sides:
        count = lax.axis_size(axis)
        forward = [(i, i + 1) for i in range(count - 1)]
        backward = [(target, source) for source, target in forward]
        low = lax.ppermute(
            lax.slice_in_dim(block, block.shape[dim] - width, None, axis=dim), axis, forward
        )
        high = lax.ppermute(lax.slice_in_dim(block, 0, width, axis=dim), axis, backward)
        block = jnp.concatenate([low, block, high], axis=dim)
    return block


def gelu_tanh(value):
    return jax.nn.gelu(value, approximate=True)


def conv_padded(padded, weight):
    depth = padded.shape[1] - 2
    height = padded.shape[2] - 2
    length = padded.shape[3] - 2
    total = None
    for first in range(3):
        for second in range(3):
            for third in range(3):
                window = padded[
                    :, first : first + depth, second : second + height, third : third + length
                ]
                term = jnp.einsum(
                    "sxyzc,co->sxyzo",
                    window,
                    weight[first, second, third],
                    preferred_element_type=jnp.float32,
                )
                total = term if total is None else total + term
    return total


def kernel_grad(padded, delta):
    depth = delta.shape[1]
    height = delta.shape[2]
    length = delta.shape[3]
    planes = []
    for first in range(3):
        for second in range(3):
            for third in range(3):
                window = padded[
                    :, first : first + depth, second : second + height, third : third + length
                ]
                planes.append(
                    jnp.einsum("sxyzc,sxyzo->co", window, delta, preferred_element_type=jnp.float32)
                )
    stacked = jnp.stack(planes, axis=0)
    return stacked.reshape((3, 3, 3) + stacked.shape[1:])


def flipped(weight):
    return jnp.swapaxes(weight[::-1, ::-1, ::-1], 3, 4)


def pad_dims(field, dims):
    widths = [(1, 1) if place in dims else (0, 0) for place in range(field.ndim)]
    return jnp.pad(field, widths)


def pool_cells(field):
    s, x, y, z, c = field.shape
    return jnp.mean(field.reshape(s, x // 2, 2, y // 2, 2, z // 2, 2, c), axis=(2, 4, 6))


def spread_cells(field):
    s, x, y, z, c = field.shape
    wide = jnp.broadcast_to(field[:, :, None, :, None, :, None, :], (s, x, 2, y, 2, z, 2, c))
    return wide.reshape(s, 2 * x, 2 * y, 2 * z, c) * 0.125


def late_layer(joined, late_weight, cotangent):
    rim = padded_2(joined, (("space", 1),), 1)
    late_pad = pad_dims(rim, (2, 3))
    pre_late = conv_padded(late_pad, late_weight)
    delta_late = jax.vjp(gelu_tanh, pre_late)[1](cotangent.astype(jnp.float32))[0].astype(
        jnp.bfloat16
    )
    late_part = kernel_grad(late_pad, delta_late)
    delta_rim = padded_2(delta_late, (("space", 1),), 1)
    back_partial = conv_padded(pad_dims(delta_rim, (2, 3)), flipped(late_weight))
    return (back_partial, late_part)


def per_device(volume, early_weight, late_weight, cotangent):
    count = (
        cotangent.shape[0]
        * lax.axis_size("rep")
        * cotangent.shape[1]
        * lax.axis_size("space")
        * cotangent.shape[2]
        * cotangent.shape[3]
    )
    scale = 1.0 / math.sqrt(count)
    haloed = padded_2(volume, (("space", 1), ("chan", 2)), 1)
    padded_in = pad_dims(haloed, (3,))
    pre_early = conv_padded(padded_in, early_weight)
    pooled = pool_cells(gelu_tanh(pre_early)).astype(jnp.bfloat16)
    joined = lax.all_gather(pooled, "chan", axis=2, tiled=True)
    back_partial, late_part = late_layer(joined, late_weight, cotangent)
    back_rows = lax.psum_scatter(back_partial, "chan", scatter_dimension=2, tiled=True)
    delta_early = jax.vjp(gelu_tanh, pre_early)[1](spread_cells(back_rows))[0].astype(jnp.bfloat16)
    early_part = kernel_grad(padded_in, delta_early)
    delta_halo = padded_2(delta_early, (("space", 1), ("chan", 2)), 1)
    grad_volume = conv_padded(pad_dims(delta_halo, (3,)), flipped(early_weight)).astype(
        jnp.bfloat16
    )
    early_total = lax.psum(early_part, ("space", "chan", "rep"))
    grad_early = (early_total * scale).astype(jnp.bfloat16)
    late_total = lax.psum(late_part, ("space", "rep"))
    grad_late = (late_total * scale).astype(jnp.bfloat16)
    return (grad_early, grad_late, grad_volume)


NT = (((1,), (1,)), ((), ()))


def gelu_and_slope(v):
    k = 0.7978845608028654
    sq = v * v
    t = jnp.tanh(k * (v + 0.044715 * (v * sq)))
    half = 0.5 * (1.0 + t)
    return v * half, half + 0.5 * v * (1.0 - t * t) * (k * (1.0 + 0.134145 * sq))


def depth_of(rows, period):
    return lax.broadcasted_iota(jnp.int32, (rows, 128), 0) % period


def shifted(ref, lead, start, rows, cell, period, step):
    dy, dz = step
    got = ref[lead + (pl.ds(start + dy * period + dz, rows), slice(None))]
    if dz == 0:
        return got
    lanes = got.shape[1] // 128
    edge = (cell == 0) if dz < 0 else (cell == period - 1)
    edge = jnp.concatenate([edge] * lanes, axis=1) if lanes > 1 else edge
    return jnp.where(edge, 0.0, got)


STEPS = [(b, c) for b in (-1, 0, 1) for c in (-1, 0, 1)]


def fold(parts, rows):
    zero = jnp.zeros((rows, parts[0].shape[1]), F32)
    return (
        parts[1]
        + jnp.concatenate([zero, parts[0][:-rows]], axis=0)
        + jnp.concatenate([parts[2][rows:], zero], axis=0)
    )


def begin_kernel(own_hbm, we_hbm, own_ref, we_ref, wcat_ref, sems):
    own = pltpu.make_async_copy(own_hbm, own_ref, sems.at[3])
    copies = [pltpu.make_async_copy(we_hbm.at[a], we_ref.at[a], sems.at[a]) for a in range(3)]
    for copy in (*copies, own):
        copy.start()
    for a in range(3):
        copies[a].wait()
        for n in range(9):
            b, c = divmod(n, 3)
            wcat_ref[pl.ds(n * 128, 128), pl.ds(a * 128, 128)] = we_ref[a, b, c]
    own.wait()


def early_kernel(*refs, nk, dims):
    gx, gy, gz, lx, ly, lz, bx, by = dims
    blocks, refs = refs[:nk], refs[nk:]
    wcat_ref, half_ref, slope_ref, send_ref, edge_ref = refs[:5]
    vol_ref, col_ref, p_ref, pre_ref, h_ref, row_ref = refs[5:]
    k, j = lax.axis_index("space"), lax.axis_index("chan")
    brows, hl, line = by * gz, by // 2 * lz, gx * gz
    vol_ref[:, pl.ds(0, 16), :] = jnp.zeros((gx, 16, 128), F32)
    vol_ref[:, pl.ds(16 + brows, 16), :] = jnp.zeros((gx, 16, 128), F32)
    for n, dk in enumerate([0, *steps_of(nk)]):
        src = blocks[n]
        kk = partner(k, dk, nk)
        for q in range(bx):
            got = src[pl.ds(q * brows, brows), :]
            vol_ref[kk * bx + q, pl.ds(16, brows), :] = got.astype(F32)
            half_ref[pl.ds(pl.multiple_of((kk * bx + q) * brows, brows), brows), :] = got

    cell = depth_of(brows, gz)
    for x in range(gx):
        for n, step in enumerate(STEPS):
            col_ref[pl.ds(x * brows, brows), pl.ds(n * 128, 128)] = shifted(
                vol_ref, (x,), 16, brows, cell, gz, step
            ).astype(BF)

    p_ref[...] = jnp.dot(col_ref[...], wcat_ref[...], preferred_element_type=F32)

    outer = pl.multiple_of((brows - gz) * (1 - j), gz)
    inner = pl.multiple_of((brows - 2 * gz) * (1 - j) + gz * j, gz)
    for x in range(gx):
        row_ref[pl.ds(x * gz, gz), :] = vol_ref[x, pl.ds(16 + outer, gz), :]
    row = row_ref[...]
    rcell = depth_of(line, gz)
    trio = [
        jnp.where(rcell == 0, 0.0, pltpu.roll(row, 1, 0)),
        row,
        jnp.where(rcell == gz - 1, 0.0, pltpu.roll(row, line - 1, 0)),
    ]
    taps = wcat_ref[pl.ds(pl.multiple_of(j * (6 * 128), 128), 3 * 128), :]
    given = jnp.dot(jnp.concatenate(trio, axis=1).astype(BF), taps, preferred_element_type=F32)
    given = fold([given[:, a * 128 : (a + 1) * 128] for a in range(3)], gz)

    for lq in range(lx):
        pair = None
        for x in (2 * lq, 2 * lq + 1):
            pre = p_ref[pl.ds(x * brows, brows), pl.ds(128, 128)]
            if x > 0:
                pre = pre + p_ref[pl.ds((x - 1) * brows, brows), pl.ds(0, 128)]
            if x < gx - 1:
                pre = pre + p_ref[pl.ds((x + 1) * brows, brows), pl.ds(256, 128)]
            pre_ref[x] = pre
            h, slope = gelu_and_slope(pre)
            slope_ref[pl.ds(x * brows, brows), :] = slope
            pair = h if pair is None else pair + h
        wide = pair.reshape(by // 2, 2, gz, 128)
        h_ref[...] = (wide[:, 0] + wide[:, 1]).reshape(by // 2 * gz, 128)
        pooled = (h_ref[pl.ds(0, hl, stride=2), :] + h_ref[pl.ds(1, hl, stride=2), :]) * 0.125
        send_ref[pl.ds(lq * hl, hl), :] = pooled.astype(BF)
    for x in range(gx):
        edge_ref[pl.ds(x * gz, gz), :] = pre_ref[x, pl.ds(inner, gz), :]
        edge_ref[pl.ds(line + x * gz, gz), :] = pre_ref[x, pl.ds(outer, gz), :]
    edge_ref[pl.ds(2 * line, line), :] = given
    send_ref[pl.ds(lx * hl, 3 * line), :] = edge_ref[...].astype(BF)


def fetch_kernel(far_ref, we_ref, near_ref, back_ref, wt_ref, sems):
    copies = [pltpu.make_async_copy(far_ref.at[a], near_ref.at[a], sems.at[a]) for a in range(3)]
    cl = near_ref.shape[-1]
    for copy in copies:
        copy.start()
    for n in range(9):
        b, c = divmod(n, 3)
        for a in range(3):
            wt_ref[a, pl.ds(n * 128, 128), :] = we_ref[a, b, c].astype(F32).T.astype(BF)
    for a in range(3):
        copies[a].wait()
        for n in range(9):
            b, c = divmod(n, 3)
            back_ref[pl.ds(n * cl, cl), pl.ds(a * 128, 128)] = near_ref[a, b, c].astype(F32).T.astype(BF)


def border_pool(inner, outer, tmp_ref, tile_ref, dims):
    lx, lz, gz = dims
    h, slope = gelu_and_slope(outer)
    h = (h + gelu_and_slope(inner)[0]).reshape(lx, 2, gz, 128)
    tmp_ref[...] = (h[:, 0] + h[:, 1]).reshape(lx * gz, 128)
    got = (tmp_ref[pl.ds(0, lx * lz, stride=2), :] + tmp_ref[pl.ds(1, lx * lz, stride=2), :]) * 0.125
    got = got.astype(BF).astype(F32)
    for x in range(lx):
        for copy in range(2):
            tile_ref[pl.ds((2 * x + copy) * lz, lz), :] = got[x * lz : (x + 1) * lz]
    return slope


def late_kernel(*refs, nk, dims):
    gx, gz, lx, ly, lz, cx = dims
    sent_ref, got_ref, edge_ref, cots, refs = *refs[:3], refs[3 : nk + 3], refs[nk + 3 :]
    wl_ref, pd_ref, patch_ref = refs[:3]
    pool_ref, lcol_ref, cot_ref, tmp_ref, tile_ref = refs[3:]
    lplane, hl, line = ly * lz, ly // 2 * lz, gx * gz
    cl = wl_ref.shape[-1]
    crow = cx * lplane
    k, j = lax.axis_index("space"), lax.axis_index("chan")
    edges = got_ref[pl.ds(lx * hl, 3 * line), :].astype(F32)
    lrow = lax.broadcasted_iota(jnp.int32, (hl, 128), 0)
    for x in range(lx):
        pool_ref[x, pl.ds(0, 8), :] = jnp.zeros((8, 128), F32)
        pool_ref[x, pl.ds(8 + lplane, 8), :] = jnp.zeros((8, 128), F32)
    sides = (
        (j, sent_ref, edge_ref[pl.ds(0, line), :], edge_ref[pl.ds(line, line), :] + edges[2 * line :]),
        (1 - j, got_ref, edges[:line], edges[line : 2 * line] + edge_ref[pl.ds(2 * line, line), :]),
    )
    for n, (side, ref, inner, outer) in enumerate(sides):
        slope = border_pool(inner, outer, tmp_ref, tile_ref, (lx, lz, gz))
        if n == 0:
            patch_ref[...] = slope
        first = (hl - lz) * (1 - side)
        border = (lrow >= first) & (lrow < first + lz)
        for x in range(lx):
            tiles = jnp.concatenate([tile_ref[pl.ds(x * 2 * lz, 2 * lz), :]] * (hl // (2 * lz)), axis=0)
            start = pl.multiple_of(8 + side * hl, 8)
            pool_ref[x, pl.ds(start, hl), :] = jnp.where(
                border, tiles, ref[pl.ds(x * hl, hl), :].astype(F32)
            )
    for x in range(lx):
        pd_ref[pl.ds(x * lplane, lplane), pl.ds(0, 128)] = pool_ref[x, pl.ds(8, lplane), :].astype(BF)

    lcell = depth_of(lplane, lz)
    for x in range(lx):
        for n, step in enumerate(STEPS):
            lcol_ref[pl.ds(x * lplane, lplane), pl.ds(n * 128, 128)] = shifted(
                pool_ref, (x,), 8, lplane, lcell, lz, step
            ).astype(BF)
    lcol = lcol_ref[...]
    parts = [
        jnp.dot(lcol, wl_ref[a].reshape(9 * 128, cl), preferred_element_type=F32) for a in range(3)
    ]
    pre = fold(parts, lplane)
    slope = gelu_and_slope(pre)[1]
    for n, dk in enumerate([0, *steps_of(nk)]):
        kk = partner(k, dk, nk)
        start = pl.multiple_of(kk * crow, 8)
        cot_ref[pl.ds(start, crow), :] = cots[n][...].astype(F32)
    delta = (cot_ref[...] * slope).astype(BF)
    pd_ref[:, pl.ds(128, cl)] = delta


def late_back_kernel(pd_ref, wback_ref, back_ref, mine_ref, dl_ref, dcol_ref, *, dims):
    lx, ly, lz = dims
    lplane = ly * lz
    cl = pd_ref.shape[1] - 128
    lcell = depth_of(lplane, lz)
    for x in range(lx):
        dl_ref[x, pl.ds(0, 8), :] = jnp.zeros((8, cl), F32)
        dl_ref[x, pl.ds(8 + lplane, 8), :] = jnp.zeros((8, cl), F32)
        dl_ref[x, pl.ds(8, lplane), :] = pd_ref[pl.ds(x * lplane, lplane), pl.ds(128, cl)].astype(F32)
    for n, (b, c) in enumerate(STEPS):
        for x in range(lx):
            dcol_ref[pl.ds(x * lplane, lplane), pl.ds(n * cl, cl)] = shifted(
                dl_ref, (x,), 8, lplane, lcell, lz, (-b, -c)
            ).astype(BF)
    total = jnp.dot(dcol_ref[...], wback_ref[...], preferred_element_type=F32)
    back = fold([total[:, (2 - a) * 128 : (3 - a) * 128] for a in range(3)], lplane)
    back_ref[...] = back.astype(BF)
    mine_ref[...] = back


def late_grad_kernel(mine_ref, other_ref, out_ref, pool_ref, lcol_ref, wide_ref, *, dims, scale):
    lx, ly, lz = dims
    lplane = ly * lz
    rows = lx * lplane
    cl = mine_ref.shape[1] - 128
    lcell = depth_of(lplane, lz)
    for x in range(lx):
        pool_ref[x, pl.ds(0, 8), :] = jnp.zeros((8, 128), F32)
        pool_ref[x, pl.ds(8 + lplane, 8), :] = jnp.zeros((8, 128), F32)
    for s, ref in enumerate((mine_ref, other_ref)):
        for x in range(lx):
            pool_ref[x, pl.ds(8, lplane), :] = ref[pl.ds(x * lplane, lplane), pl.ds(0, 128)].astype(F32)
        for x in range(lx):
            for n, step in enumerate(STEPS):
                lcol_ref[pl.ds(s * rows + x * lplane, lplane), pl.ds(n * 128, 128)] = shifted(
                    pool_ref, (x,), 8, lplane, lcell, lz, step
                ).astype(BF)
        zero = jnp.zeros((lplane, cl), BF)
        wide_ref[pl.ds(s * rows + rows - lplane, lplane), pl.ds(0, cl)] = zero
        wide_ref[pl.ds(s * rows, rows - lplane), pl.ds(0, cl)] = ref[pl.ds(lplane, rows - lplane), pl.ds(128, cl)]
        wide_ref[pl.ds(s * rows, rows), pl.ds(cl, cl)] = ref[:, pl.ds(128, cl)]
        wide_ref[pl.ds(s * rows, lplane), pl.ds(2 * cl, cl)] = zero
        wide_ref[pl.ds(s * rows + lplane, rows - lplane), pl.ds(2 * cl, cl)] = ref[
            pl.ds(0, rows - lplane), pl.ds(128, cl)
        ]
    got = lax.dot_general(
        lcol_ref[...], wide_ref[...], (((0,), (0,)), ((), ())), preferred_element_type=F32
    )
    for a in range(3):
        out_ref[pl.ds(a * 9 * 128, 9 * 128), :] = (got[:, a * cl : (a + 1) * cl] * scale).astype(BF)


def other_kernel(
    half_ref, got_ref, wcat_ref, col_ref, slope_ref, vol_ref, p_ref, *, dims
):
    gx, gy, gz, lx, ly, lz, bx, by = dims
    brows = by * gz
    j = lax.axis_index("chan")
    vol_ref[:, :, pl.ds(0, 16), :] = jnp.zeros((2, gx, 16, 128), F32)
    vol_ref[:, :, pl.ds(16 + brows, 16), :] = jnp.zeros((2, gx, 16, 128), F32)
    for h, src in enumerate((half_ref, got_ref)):
        for x in range(gx):
            vol_ref[h, x, pl.ds(16, brows), :] = src[pl.ds(x * brows, brows), :].astype(F32)
    for h, side in enumerate((j, 1 - j)):
        into = pl.multiple_of((16 + brows) * (1 - side) + (16 - gz) * side, 8)
        start = pl.multiple_of(16 + (brows - gz) * side, 8)
        for x in range(gx):
            vol_ref[h, x, pl.ds(into, gz), :] = vol_ref[1 - h, x, pl.ds(start, gz), :]
    cell = depth_of(brows, gz)
    for h in (1, 0):
        for x in range(gx):
            for n, step in enumerate(STEPS):
                col_ref[pl.ds((h * gx + x) * brows, brows), pl.ds(n * 128, 128)] = shifted(
                    vol_ref, (h, x), 16, brows, cell, gz, step
                ).astype(BF)
    p_ref[...] = jnp.dot(
        col_ref[pl.ds(gx * brows, gx * brows), :], wcat_ref[...], preferred_element_type=F32
    )
    for x in range(gx):
        pre = p_ref[pl.ds(x * brows, brows), pl.ds(128, 128)]
        if x > 0:
            pre = pre + p_ref[pl.ds((x - 1) * brows, brows), pl.ds(0, 128)]
        if x < gx - 1:
            pre = pre + p_ref[pl.ds((x + 1) * brows, brows), pl.ds(256, 128)]
        slope_ref[pl.ds(x * brows, brows), :] = gelu_and_slope(pre)[1]


def early_grad_kernel(
    mine_ref, other_ref, slope_ref, far_ref, patch_ref, col_ref, late_ref,
    part_ref, win_ref, out_ref, wide_ref, d_ref, dt_ref, sem, *, dims
):
    leave = pltpu.make_async_copy(late_ref, out_ref, sem)
    leave.start()
    gx, gy, gz, lx, ly, lz, bx, by = dims
    plane, lplane = gy * gz, ly * lz
    k, j = lax.axis_index("space"), lax.axis_index("chan")
    brows = by * gz
    span = (gx + 2) * brows
    for q in (0, gx + 1):
        d_ref[q] = jnp.zeros(d_ref.shape[1:], F32)
    d_ref[:, pl.ds(0, 16), :] = jnp.zeros((gx + 2, 16, 128), F32)
    d_ref[:, pl.ds(16 + plane, 16), :] = jnp.zeros((gx + 2, 16, 128), F32)
    for h in (0, 1):
        dt_ref[:, pl.ds(h * span, brows)] = jnp.zeros((128, brows), BF)
        dt_ref[:, pl.ds((h + 1) * span - brows, brows)] = jnp.zeros((128, brows), BF)
    back = (mine_ref[...] + other_ref[...].astype(F32)) * 0.125
    wide_ref[pl.ds(0, lx * lplane, stride=2), :] = back
    wide_ref[pl.ds(1, lx * lplane, stride=2), :] = back
    first = (brows - gz) * (1 - j)
    row = lax.broadcasted_iota(jnp.int32, (brows, 128), 0)
    border = (row >= first) & (row < first + gz)
    for lq in range(lx):
        for h, side in enumerate((j, 1 - j)):
            start = pl.multiple_of(lq * ly * gz + side * (by // 2 * gz), 8)
            rows = wide_ref[pl.ds(start, by // 2 * gz), :].reshape(by // 2, 1, gz, 128)
            rows = jnp.broadcast_to(rows, (by // 2, 2, gz, 128)).reshape(brows, 128)
            for x in (2 * lq, 2 * lq + 1):
                slope = (far_ref if h else slope_ref)[pl.ds(x * brows, brows), :]
                if h == 0:
                    tiles = jnp.concatenate([patch_ref[pl.ds(x * gz, gz), :]] * by, axis=0)
                    slope = jnp.where(border, tiles, slope)
                delta = (rows * slope).astype(BF).astype(F32)
                d_ref[x + 1, pl.ds(pl.multiple_of(16 + side * brows, 8), brows), :] = delta
                dt_ref[:, pl.ds(h * span + (x + 1) * brows, brows)] = delta.T.astype(BF)
    left = jnp.concatenate(
        [
            jnp.concatenate(
                [dt_ref[:, pl.ds(h * span + (2 - a) * brows, gx * brows)] for h in (0, 1)], axis=1
            )
            for a in range(3)
        ],
        axis=0,
    )
    got = jnp.dot(left, col_ref[...], preferred_element_type=F32)
    for a in range(3):
        for n in range(9):
            part_ref[pl.ds((a * 9 + n) * 128, 128), :] = got[
                a * 128 : (a + 1) * 128, n * 128 : (n + 1) * 128
            ].T.astype(part_ref.dtype)
    row = pl.multiple_of(j * brows, 8)
    for q in range(bx + 2):
        win_ref[q] = d_ref[k * bx + q, pl.ds(row, brows + 32), :]
    leave.wait()


def grad_volume_kernel(win_ref, wt_ref, gv_ref, vcol_ref, *, bx, brows, gz):
    cell = depth_of(brows, gz)
    for q in range(bx + 2):
        for n, (b, c) in enumerate(STEPS):
            vcol_ref[pl.ds(q * brows, brows), pl.ds(n * 128, 128)] = shifted(
                win_ref, (q,), 16, brows, cell, gz, (-b, -c)
            ).astype(BF)
    total = None
    for a in range(3):
        term = jnp.dot(vcol_ref[pl.ds((2 - a) * brows, bx * brows), :], wt_ref[a], preferred_element_type=F32)
        total = term if total is None else total + term
    gv_ref[...] = total.astype(BF)


def steps_of(count):
    return range(1, count)


def partner(index, by, count):
    if count & (count - 1) == 0:
        return index ^ by
    return lax.rem(index + count - by, count)


def turned(value, axis, by):
    count = lax.axis_size(axis)
    pairs = count & (count - 1) == 0
    return lax.ppermute(value, axis, [(i, i ^ by if pairs else (i + by) % count) for i in range(count)])


def call(kernel, outs, scratch, args, name, far=(), raw=(), away=()):
    args = [
        pltpu.with_memory_space_constraint(arg, pltpu.HBM if n in raw else pltpu.VMEM)
        for n, arg in enumerate(args)
    ]
    outs = [out if n in (*far, *away) else pltpu.VMEM(out.shape, out.dtype) for n, out in enumerate(outs)]
    return pl.pallas_call(
        kernel,
        out_shape=outs,
        in_specs=[
            pl.BlockSpec(memory_space=pltpu.HBM if n in raw else pltpu.VMEM) for n in range(len(args))
        ],
        out_specs=[
            pl.BlockSpec(memory_space=pltpu.HBM if n in away else pltpu.VMEM) for n in range(len(outs))
        ],
        scratch_shapes=scratch,
        compiler_params=pltpu.CompilerParams(vmem_limit_bytes=VMEM_BYTES),
        name=name,
    )(*args)


def whole_sample(volume, early_weight, late_weight, cotangent):
    nk, nj, nr = (lax.axis_size(axis) for axis in ("space", "chan", "rep"))
    _, bx, by, gz, _ = volume.shape
    _, cx, ly, lz, cl = cotangent.shape
    gx, gy, lx = bx * nk, by * nj, cx * nk
    plane, lplane, brows = gy * gz, ly * lz, by * gz
    rows, lrows = gx * plane, lx * lplane
    scale = 1.0 / math.sqrt(nr * lrows)
    sds = jax.ShapeDtypeStruct

    mine = volume.reshape(bx * brows, 128)
    line = [mine] + [turned(mine, "space", dk) for dk in steps_of(nk)]
    cot = cotangent.reshape(cx * lplane, cl)
    own, we, wcat = call(
        begin_kernel,
        [sds(mine.shape, BF), sds(early_weight.shape, BF), sds((9 * 128, 3 * 128), BF)],
        [pltpu.SemaphoreType.DMA((4,))],
        [mine, early_weight],
        "begin",
        raw=(0, 1),
    )
    line[0] = own
    cots = [cot] + [turned(cot, "space", dk) for dk in steps_of(nk)]

    dims = (gx, gy, gz, lx, ly, lz, bx, by)
    hrows, edge = gx * brows, 3 * gx * gz
    half, slope, send, edges = call(
        functools.partial(early_kernel, nk=nk, dims=dims),
        [
            sds((hrows, 128), BF),
            sds((hrows, 128), F32),
            sds((lrows // 2 + edge, 128), BF),
            sds((edge, 128), F32),
        ],
        [
            pltpu.VMEM((gx, brows + 32, 128), F32),
            pltpu.VMEM((hrows, 9 * 128), BF),
            pltpu.VMEM((hrows, 3 * 128), F32),
            pltpu.VMEM((gx, brows, 128), F32),
            pltpu.VMEM((by // 2 * gz, 128), F32),
            pltpu.VMEM((gx * gz, 128), F32),
        ],
        line + [wcat],
        "early",
    )
    ready, *cots[1:] = lax.optimization_barrier((send, *cots[1:]))
    send_other = turned(ready, "chan", 1)
    half_other = turned(half, "chan", 1)
    held, _ = lax.optimization_barrier((late_weight, send))
    wl, wback, wt = call(
        fetch_kernel,
        [sds(late_weight.shape, BF), sds((9 * cl, 3 * 128), BF), sds((3, 9 * 128, 128), BF)],
        [pltpu.SemaphoreType.DMA((3,))],
        [held, we],
        "fetch",
        raw=(0,),
    )
    pooled_delta, patch = call(
        functools.partial(late_kernel, nk=nk, dims=(gx, gz, lx, ly, lz, cx)),
        [sds((lrows, 128 + cl), BF), sds((gx * gz, 128), F32)],
        [
            pltpu.VMEM((lx, lplane + 16, 128), F32),
            pltpu.VMEM((lrows, 9 * 128), BF),
            pltpu.VMEM((lrows, cl), F32),
            pltpu.VMEM((lx * gz, 128), F32),
            pltpu.VMEM((lx * 2 * lz, 128), F32),
        ],
        [send, send_other, edges] + cots + [wl],
        "late",
    )
    back, back_mine = call(
        functools.partial(late_back_kernel, dims=(lx, ly, lz)),
        [sds((lrows, 128), BF), sds((lrows, 128), F32)],
        [pltpu.VMEM((lx, lplane + 16, cl), F32), pltpu.VMEM((lrows, 9 * cl), BF)],
        [pooled_delta, wback],
        "late_back",
    )
    pd_other = turned(pooled_delta, "rep", 1)
    back_other = turned(back, "chan", 1)
    (late,) = call(
        functools.partial(late_grad_kernel, dims=(lx, ly, lz), scale=scale),
        [sds((27 * 128, cl), BF)],
        [
            pltpu.VMEM((lx, lplane + 16, 128), F32),
            pltpu.VMEM((2 * lrows, 9 * 128), BF),
            pltpu.VMEM((2 * lrows, 3 * cl), BF),
        ],
        [pooled_delta, pd_other],
        "late_grad",
    )
    half_other, wcat, _ = lax.optimization_barrier((half_other, wcat, back))
    col, far_slope = call(
        functools.partial(other_kernel, dims=dims),
        [sds((rows, 9 * 128), BF), sds((hrows, 128), F32)],
        [pltpu.VMEM((2, gx, brows + 32, 128), F32), pltpu.VMEM((hrows, 3 * 128), F32)],
        [half, half_other, wcat],
        "other",
    )
    back_mine, late = lax.optimization_barrier((back_mine, late))
    part, win, late = call(
        functools.partial(early_grad_kernel, dims=dims),
        [sds((27 * 128, 128), BF), sds((bx + 2, brows + 32, 128), F32), sds(late.shape, BF)],
        [
            pltpu.VMEM((lx * ly * gz, 128), F32),
            pltpu.VMEM((gx + 2, plane + 32, 128), F32),
            pltpu.VMEM((128, (gx + 2) * plane), BF),
            pltpu.SemaphoreType.DMA(()),
        ],
        [back_mine, back_other, slope, far_slope, patch, col, late],
        "early_grad",
        away=(2,),
    )
    part_other = turned(part, "rep", 1)
    (gv,) = call(
        functools.partial(grad_volume_kernel, bx=bx, brows=brows, gz=gz),
        [sds((bx * brows, 128), BF)],
        [pltpu.VMEM(((bx + 2) * brows, 9 * 128), BF)],
        [win, wt],
        "grad_volume",
        far=(0,),
    )
    early = ((part.astype(F32) + part_other.astype(F32)) * scale).astype(BF)
    return (
        early.reshape(3, 3, 3, 128, 128),
        late.reshape(3, 3, 3, 128, cl),
        gv.reshape(1, bx, by, gz, 128),
    )


def solution(mesh):
    few = mesh.shape["space"] * mesh.shape["chan"] <= GATHER_BLOCKS
    alone = mesh.shape["rep"] == 2 and mesh.shape["chan"] == 2
    return jax.shard_map(
        whole_sample if few and alone else per_device,
        mesh=mesh,
        in_specs=(
            P(("groups", "rep"), "space", "chan", None, None),
            P(),
            P(None, None, None, None, "chan"),
            P(("groups", "rep"), "space", None, None, "chan"),
        ),
        out_specs=(
            P("groups", None, None, None, None),
            P("groups", None, None, None, "chan"),
            P(("groups", "rep"), "space", "chan", None, None),
        ),
        check_vma=False,
    )
```

```python
import functools
import math

import jax
import jax.numpy as jnp
from jax import lax
from jax.experimental import pallas as pl
from jax.experimental.pallas import tpu as pltpu
from jax.sharding import PartitionSpec as P

BF = jnp.bfloat16
F32 = jnp.float32
VMEM_BYTES = 14 * 2**20
GATHER_BLOCKS = 8
EARLY_TAPS = 5


def padded_2(block, sides, width):
    for axis, dim in sides:
        count = lax.axis_size(axis)
        forward = [(i, i + 1) for i in range(count - 1)]
        backward = [(target, source) for source, target in forward]
        low = lax.ppermute(
            lax.slice_in_dim(block, block.shape[dim] - width, None, axis=dim), axis, forward
        )
        high = lax.ppermute(lax.slice_in_dim(block, 0, width, axis=dim), axis, backward)
        block = jnp.concatenate([low, block, high], axis=dim)
    return block


def gelu_tanh(value):
    return jax.nn.gelu(value, approximate=True)


def conv_padded(padded, weight):
    depth = padded.shape[1] - 2
    height = padded.shape[2] - 2
    length = padded.shape[3] - 2
    total = None
    for first in range(3):
        for second in range(3):
            for third in range(3):
                window = padded[
                    :, first : first + depth, second : second + height, third : third + length
                ]
                term = jnp.einsum(
                    "sxyzc,co->sxyzo",
                    window,
                    weight[first, second, third],
                    preferred_element_type=jnp.float32,
                )
                total = term if total is None else total + term
    return total


def kernel_grad(padded, delta):
    depth = delta.shape[1]
    height = delta.shape[2]
    length = delta.shape[3]
    planes = []
    for first in range(3):
        for second in range(3):
            for third in range(3):
                window = padded[
                    :, first : first + depth, second : second + height, third : third + length
                ]
                planes.append(
                    jnp.einsum("sxyzc,sxyzo->co", window, delta, preferred_element_type=jnp.float32)
                )
    stacked = jnp.stack(planes, axis=0)
    return stacked.reshape((3, 3, 3) + stacked.shape[1:])


def flipped(weight):
    return jnp.swapaxes(weight[::-1, ::-1, ::-1], 3, 4)


def pad_dims(field, dims):
    widths = [(1, 1) if place in dims else (0, 0) for place in range(field.ndim)]
    return jnp.pad(field, widths)


def pool_cells(field):
    s, x, y, z, c = field.shape
    return jnp.mean(field.reshape(s, x // 2, 2, y // 2, 2, z // 2, 2, c), axis=(2, 4, 6))


def spread_cells(field):
    s, x, y, z, c = field.shape
    wide = jnp.broadcast_to(field[:, :, None, :, None, :, None, :], (s, x, 2, y, 2, z, 2, c))
    return wide.reshape(s, 2 * x, 2 * y, 2 * z, c) * 0.125


def late_layer(joined, late_weight, cotangent):
    rim = padded_2(joined, (("space", 1),), 1)
    late_pad = pad_dims(rim, (2, 3))
    pre_late = conv_padded(late_pad, late_weight)
    delta_late = jax.vjp(gelu_tanh, pre_late)[1](cotangent.astype(jnp.float32))[0].astype(
        jnp.bfloat16
    )
    late_part = kernel_grad(late_pad, delta_late)
    delta_rim = padded_2(delta_late, (("space", 1),), 1)
    back_partial = conv_padded(pad_dims(delta_rim, (2, 3)), flipped(late_weight))
    return (back_partial, late_part)


def per_device(volume, early_weight, late_weight, cotangent):
    count = (
        cotangent.shape[0]
        * lax.axis_size("rep")
        * cotangent.shape[1]
        * lax.axis_size("space")
        * cotangent.shape[2]
        * cotangent.shape[3]
    )
    scale = 1.0 / math.sqrt(count)
    haloed = padded_2(volume, (("space", 1), ("chan", 2)), 1)
    padded_in = pad_dims(haloed, (3,))
    pre_early = conv_padded(padded_in, early_weight)
    pooled = pool_cells(gelu_tanh(pre_early)).astype(jnp.bfloat16)
    joined = lax.all_gather(pooled, "chan", axis=2, tiled=True)
    back_partial, late_part = late_layer(joined, late_weight, cotangent)
    back_rows = lax.psum_scatter(back_partial, "chan", scatter_dimension=2, tiled=True)
    delta_early = jax.vjp(gelu_tanh, pre_early)[1](spread_cells(back_rows))[0].astype(jnp.bfloat16)
    early_part = kernel_grad(padded_in, delta_early)
    delta_halo = padded_2(delta_early, (("space", 1), ("chan", 2)), 1)
    grad_volume = conv_padded(pad_dims(delta_halo, (3,)), flipped(early_weight)).astype(
        jnp.bfloat16
    )
    early_total = lax.psum(early_part, ("space", "chan", "rep"))
    grad_early = (early_total * scale).astype(jnp.bfloat16)
    late_total = lax.psum(late_part, ("space", "rep"))
    grad_late = (late_total * scale).astype(jnp.bfloat16)
    return (grad_early, grad_late, grad_volume)


NT = (((1,), (1,)), ((), ()))


def gelu_and_slope(v):
    k = 0.7978845608028654
    sq = v * v
    t = jnp.tanh(k * (v + 0.044715 * (v * sq)))
    half = 0.5 * (1.0 + t)
    return v * half, half + 0.5 * v * (1.0 - t * t) * (k * (1.0 + 0.134145 * sq))


def depth_of(rows, period):
    return lax.broadcasted_iota(jnp.int32, (rows, 128), 0) % period


def shifted(ref, lead, start, rows, cell, period, step):
    dy, dz = step
    got = ref[lead + (pl.ds(start + dy * period + dz, rows), slice(None))]
    if dz == 0:
        return got
    lanes = got.shape[1] // 128
    edge = (cell == 0) if dz < 0 else (cell == period - 1)
    edge = jnp.concatenate([edge] * lanes, axis=1) if lanes > 1 else edge
    return jnp.where(edge, 0.0, got)


STEPS = [(b, c) for b in (-1, 0, 1) for c in (-1, 0, 1)]


def fold(parts, rows):
    zero = jnp.zeros((rows, parts[0].shape[1]), F32)
    return (
        parts[1]
        + jnp.concatenate([zero, parts[0][:-rows]], axis=0)
        + jnp.concatenate([parts[2][rows:], zero], axis=0)
    )


def begin_kernel(own_hbm, we_hbm, own_ref, we_ref, wcat_ref, sems):
    own = pltpu.make_async_copy(own_hbm, own_ref, sems.at[3])
    copies = [pltpu.make_async_copy(we_hbm.at[a], we_ref.at[a], sems.at[a]) for a in range(3)]
    for copy in (*copies, own):
        copy.start()
    for a in range(3):
        copies[a].wait()
        for n in range(9):
            b, c = divmod(n, 3)
            wcat_ref[pl.ds(n * 128, 128), pl.ds(a * 128, 128)] = we_ref[a, b, c]
    own.wait()


def early_kernel(*refs, nk, dims):
    gx, gy, gz, lx, ly, lz, bx, by = dims
    blocks, refs = refs[:nk], refs[nk:]
    wcat_ref, half_ref, slope_ref, send_ref, edge_ref = refs[:5]
    vol_ref, col_ref, p_ref, pre_ref, h_ref, row_ref = refs[5:]
    k, j = lax.axis_index("space"), lax.axis_index("chan")
    brows, hl, line = by * gz, by // 2 * lz, gx * gz
    vol_ref[:, pl.ds(0, 16), :] = jnp.zeros((gx, 16, 128), F32)
    vol_ref[:, pl.ds(16 + brows, 16), :] = jnp.zeros((gx, 16, 128), F32)
    for n, dk in enumerate([0, *steps_of(nk)]):
        src = blocks[n]
        kk = partner(k, dk, nk)
        for q in range(bx):
            got = src[pl.ds(q * brows, brows), :]
            vol_ref[kk * bx + q, pl.ds(16, brows), :] = got.astype(F32)
            half_ref[pl.ds(pl.multiple_of((kk * bx + q) * brows, brows), brows), :] = got

    cell = depth_of(brows, gz)
    for x in range(gx):
        for n, step in enumerate(STEPS):
            col_ref[pl.ds(x * brows, brows), pl.ds(n * 128, 128)] = shifted(
                vol_ref, (x,), 16, brows, cell, gz, step
            ).astype(BF)

    p_ref[...] = jnp.dot(col_ref[...], wcat_ref[...], preferred_element_type=F32)

    outer = pl.multiple_of((brows - gz) * (1 - j), gz)
    inner = pl.multiple_of((brows - 2 * gz) * (1 - j) + gz * j, gz)
    for x in range(gx):
        row_ref[pl.ds(x * gz, gz), :] = vol_ref[x, pl.ds(16 + outer, gz), :]
    row = row_ref[...]
    rcell = depth_of(line, gz)
    trio = [
        jnp.where(rcell == 0, 0.0, pltpu.roll(row, 1, 0)),
        row,
        jnp.where(rcell == gz - 1, 0.0, pltpu.roll(row, line - 1, 0)),
    ]
    taps = wcat_ref[pl.ds(pl.multiple_of(j * (6 * 128), 128), 3 * 128), :]
    given = jnp.dot(jnp.concatenate(trio, axis=1).astype(BF), taps, preferred_element_type=F32)
    given = fold([given[:, a * 128 : (a + 1) * 128] for a in range(3)], gz)

    for lq in range(lx):
        pair = None
        for x in (2 * lq, 2 * lq + 1):
            pre = p_ref[pl.ds(x * brows, brows), pl.ds(128, 128)]
            if x > 0:
                pre = pre + p_ref[pl.ds((x - 1) * brows, brows), pl.ds(0, 128)]
            if x < gx - 1:
                pre = pre + p_ref[pl.ds((x + 1) * brows, brows), pl.ds(256, 128)]
            pre_ref[x] = pre
            h, slope = gelu_and_slope(pre)
            slope_ref[pl.ds(x * brows, brows), :] = slope
            pair = h if pair is None else pair + h
        wide = pair.reshape(by // 2, 2, gz, 128)
        h_ref[...] = (wide[:, 0] + wide[:, 1]).reshape(by // 2 * gz, 128)
        pooled = (h_ref[pl.ds(0, hl, stride=2), :] + h_ref[pl.ds(1, hl, stride=2), :]) * 0.125
        send_ref[pl.ds(lq * hl, hl), :] = pooled.astype(BF)
    for x in range(gx):
        edge_ref[pl.ds(x * gz, gz), :] = pre_ref[x, pl.ds(inner, gz), :]
        edge_ref[pl.ds(line + x * gz, gz), :] = pre_ref[x, pl.ds(outer, gz), :]
    edge_ref[pl.ds(2 * line, line), :] = given
    send_ref[pl.ds(lx * hl, 3 * line), :] = edge_ref[...].astype(BF)


def fetch_kernel(far_ref, we_ref, near_ref, back_ref, wt_ref, sems):
    copies = [pltpu.make_async_copy(far_ref.at[a], near_ref.at[a], sems.at[a]) for a in range(3)]
    cl = near_ref.shape[-1]
    for copy in copies:
        copy.start()
    for n in range(9):
        b, c = divmod(n, 3)
        for a in range(3):
            wt_ref[a, pl.ds(n * 128, 128), :] = we_ref[a, b, c].astype(F32).T.astype(BF)
    for a in range(3):
        copies[a].wait()
        for n in range(9):
            b, c = divmod(n, 3)
            back_ref[pl.ds(n * cl, cl), pl.ds(a * 128, 128)] = near_ref[a, b, c].astype(F32).T.astype(BF)


def border_pool(inner, outer, tmp_ref, tile_ref, dims):
    lx, lz, gz = dims
    h, slope = gelu_and_slope(outer)
    h = (h + gelu_and_slope(inner)[0]).reshape(lx, 2, gz, 128)
    tmp_ref[...] = (h[:, 0] + h[:, 1]).reshape(lx * gz, 128)
    got = (tmp_ref[pl.ds(0, lx * lz, stride=2), :] + tmp_ref[pl.ds(1, lx * lz, stride=2), :]) * 0.125
    got = got.astype(BF).astype(F32)
    for x in range(lx):
        for copy in range(2):
            tile_ref[pl.ds((2 * x + copy) * lz, lz), :] = got[x * lz : (x + 1) * lz]
    return slope


def late_kernel(*refs, nk, dims):
    gx, gz, lx, ly, lz, cx = dims
    sent_ref, got_ref, edge_ref, cots, refs = *refs[:3], refs[3 : nk + 3], refs[nk + 3 :]
    wl_ref, pd_ref, patch_ref = refs[:3]
    pool_ref, lcol_ref, cot_ref, tmp_ref, tile_ref = refs[3:]
    lplane, hl, line = ly * lz, ly // 2 * lz, gx * gz
    cl = wl_ref.shape[-1]
    crow = cx * lplane
    k, j = lax.axis_index("space"), lax.axis_index("chan")
    edges = got_ref[pl.ds(lx * hl, 3 * line), :].astype(F32)
    lrow = lax.broadcasted_iota(jnp.int32, (hl, 128), 0)
    for x in range(lx):
        pool_ref[x, pl.ds(0, 8), :] = jnp.zeros((8, 128), F32)
        pool_ref[x, pl.ds(8 + lplane, 8), :] = jnp.zeros((8, 128), F32)
    sides = (
        (j, sent_ref, edge_ref[pl.ds(0, line), :], edge_ref[pl.ds(line, line), :] + edges[2 * line :]),
        (1 - j, got_ref, edges[:line], edges[line : 2 * line] + edge_ref[pl.ds(2 * line, line), :]),
    )
    for n, (side, ref, inner, outer) in enumerate(sides):
        slope = border_pool(inner, outer, tmp_ref, tile_ref, (lx, lz, gz))
        if n == 0:
            patch_ref[...] = slope
        first = (hl - lz) * (1 - side)
        border = (lrow >= first) & (lrow < first + lz)
        for x in range(lx):
            tiles = jnp.concatenate([tile_ref[pl.ds(x * 2 * lz, 2 * lz), :]] * (hl // (2 * lz)), axis=0)
            start = pl.multiple_of(8 + side * hl, 8)
            pool_ref[x, pl.ds(start, hl), :] = jnp.where(
                border, tiles, ref[pl.ds(x * hl, hl), :].astype(F32)
            )
    for x in range(lx):
        pd_ref[pl.ds(x * lplane, lplane), pl.ds(0, 128)] = pool_ref[x, pl.ds(8, lplane), :].astype(BF)

    lcell = depth_of(lplane, lz)
    for x in range(lx):
        for n, step in enumerate(STEPS):
            lcol_ref[pl.ds(x * lplane, lplane), pl.ds(n * 128, 128)] = shifted(
                pool_ref, (x,), 8, lplane, lcell, lz, step
            ).astype(BF)
    lcol = lcol_ref[...]
    parts = [
        jnp.dot(lcol, wl_ref[a].reshape(9 * 128, cl), preferred_element_type=F32) for a in range(3)
    ]
    pre = fold(parts, lplane)
    slope = gelu_and_slope(pre)[1]
    for n, dk in enumerate([0, *steps_of(nk)]):
        kk = partner(k, dk, nk)
        start = pl.multiple_of(kk * crow, 8)
        cot_ref[pl.ds(start, crow), :] = cots[n][...].astype(F32).reshape(crow, cl)
    delta = (cot_ref[...] * slope).astype(BF)
    pd_ref[:, pl.ds(128, cl)] = delta


def late_back_kernel(pd_ref, wback_ref, back_ref, mine_ref, dl_ref, dcol_ref, *, dims):
    lx, ly, lz = dims
    lplane = ly * lz
    cl = pd_ref.shape[1] - 128
    lcell = depth_of(lplane, lz)
    for x in range(lx):
        dl_ref[x, pl.ds(0, 8), :] = jnp.zeros((8, cl), F32)
        dl_ref[x, pl.ds(8 + lplane, 8), :] = jnp.zeros((8, cl), F32)
        dl_ref[x, pl.ds(8, lplane), :] = pd_ref[pl.ds(x * lplane, lplane), pl.ds(128, cl)].astype(F32)
    for n, (b, c) in enumerate(STEPS):
        for x in range(lx):
            dcol_ref[pl.ds(x * lplane, lplane), pl.ds(n * cl, cl)] = shifted(
                dl_ref, (x,), 8, lplane, lcell, lz, (-b, -c)
            ).astype(BF)
    total = jnp.dot(dcol_ref[...], wback_ref[...], preferred_element_type=F32)
    back = fold([total[:, (2 - a) * 128 : (3 - a) * 128] for a in range(3)], lplane)
    back_ref[...] = back.astype(BF)
    mine_ref[...] = back


def late_grad_kernel(mine_ref, other_ref, out_ref, pool_ref, lcol_ref, wide_ref, *, dims, scale):
    lx, ly, lz = dims
    lplane = ly * lz
    rows = lx * lplane
    cl = mine_ref.shape[1] - 128
    lcell = depth_of(lplane, lz)
    for x in range(lx):
        pool_ref[x, pl.ds(0, 8), :] = jnp.zeros((8, 128), F32)
        pool_ref[x, pl.ds(8 + lplane, 8), :] = jnp.zeros((8, 128), F32)
    for s, ref in enumerate((mine_ref, other_ref)):
        for x in range(lx):
            pool_ref[x, pl.ds(8, lplane), :] = ref[pl.ds(x * lplane, lplane), pl.ds(0, 128)].astype(F32)
        for x in range(lx):
            for n, step in enumerate(STEPS):
                lcol_ref[pl.ds(s * rows + x * lplane, lplane), pl.ds(n * 128, 128)] = shifted(
                    pool_ref, (x,), 8, lplane, lcell, lz, step
                ).astype(BF)
        zero = jnp.zeros((lplane, cl), BF)
        wide_ref[pl.ds(s * rows + rows - lplane, lplane), pl.ds(0, cl)] = zero
        wide_ref[pl.ds(s * rows, rows - lplane), pl.ds(0, cl)] = ref[pl.ds(lplane, rows - lplane), pl.ds(128, cl)]
        wide_ref[pl.ds(s * rows, rows), pl.ds(cl, cl)] = ref[:, pl.ds(128, cl)]
        wide_ref[pl.ds(s * rows, lplane), pl.ds(2 * cl, cl)] = zero
        wide_ref[pl.ds(s * rows + lplane, rows - lplane), pl.ds(2 * cl, cl)] = ref[
            pl.ds(0, rows - lplane), pl.ds(128, cl)
        ]
    got = lax.dot_general(
        lcol_ref[...], wide_ref[...], (((0,), (0,)), ((), ())), preferred_element_type=F32
    )
    for a in range(3):
        out_ref[pl.ds(a * 9 * 128, 9 * 128), :] = (got[:, a * cl : (a + 1) * cl] * scale).astype(BF)


def other_kernel(
    half_ref, got_ref, wcat_ref, col_ref, slope_ref, vol_ref, p_ref, *, dims
):
    gx, gy, gz, lx, ly, lz, bx, by = dims
    brows = by * gz
    j = lax.axis_index("chan")
    vol_ref[:, :, pl.ds(0, 16), :] = jnp.zeros((2, gx, 16, 128), F32)
    vol_ref[:, :, pl.ds(16 + brows, 16), :] = jnp.zeros((2, gx, 16, 128), F32)
    for h, src in enumerate((half_ref, got_ref)):
        for x in range(gx):
            vol_ref[h, x, pl.ds(16, brows), :] = src[pl.ds(x * brows, brows), :].astype(F32)
    for h, side in enumerate((j, 1 - j)):
        into = pl.multiple_of((16 + brows) * (1 - side) + (16 - gz) * side, 8)
        start = pl.multiple_of(16 + (brows - gz) * side, 8)
        for x in range(gx):
            vol_ref[h, x, pl.ds(into, gz), :] = vol_ref[1 - h, x, pl.ds(start, gz), :]
    cell = depth_of(brows, gz)
    for h in (1, 0):
        for x in range(gx):
            for n, step in enumerate(STEPS):
                col_ref[pl.ds((h * gx + x) * brows, brows), pl.ds(n * 128, 128)] = shifted(
                    vol_ref, (h, x), 16, brows, cell, gz, step
                ).astype(BF)
    p_ref[...] = jnp.dot(
        col_ref[pl.ds(gx * brows, gx * brows), :], wcat_ref[...], preferred_element_type=F32
    )
    for x in range(gx):
        pre = p_ref[pl.ds(x * brows, brows), pl.ds(128, 128)]
        if x > 0:
            pre = pre + p_ref[pl.ds((x - 1) * brows, brows), pl.ds(0, 128)]
        if x < gx - 1:
            pre = pre + p_ref[pl.ds((x + 1) * brows, brows), pl.ds(256, 128)]
        slope_ref[pl.ds(x * brows, brows), :] = gelu_and_slope(pre)[1]


def tap_terms(left_ref, col_ref, part_ref, first, count):
    got = jnp.dot(left_ref[...], col_ref[:, pl.ds(first * 128, count * 128)], preferred_element_type=F32)
    for a in range(3):
        for n in range(count):
            part_ref[pl.ds((a * count + n) * 128, 128), :] = got[
                a * 128 : (a + 1) * 128, n * 128 : (n + 1) * 128
            ].T.astype(part_ref.dtype)


def more_kernel(left_ref, col_ref, part_ref):
    tap_terms(left_ref, col_ref, part_ref, EARLY_TAPS, 9 - EARLY_TAPS)


def finish_kernel(one_ref, one_got_ref, two_ref, two_got_ref, out_ref, sum_ref, sems, *, scale):
    copies = []
    for a in range(3):
        at = a * 9 * 128
        for mine_ref, got_ref, count in (
            (one_ref, one_got_ref, EARLY_TAPS), (two_ref, two_got_ref, 9 - EARLY_TAPS)
        ):
            rows = pl.ds(a * count * 128, count * 128)
            total = mine_ref[rows, :].astype(F32) + got_ref[rows, :].astype(F32)
            sum_ref[pl.ds(at, count * 128), :] = (total * scale).astype(BF)
            at += count * 128
        rows = pl.ds(a * 9 * 128, 9 * 128)
        copies.append(pltpu.make_async_copy(sum_ref.at[rows], out_ref.at[rows], sems.at[a]))
        copies[-1].start()
    for copy in copies:
        copy.wait()


def early_grad_kernel(
    mine_ref, other_ref, slope_ref, far_ref, patch_ref, col_ref, late_ref,
    part_ref, win_ref, out_ref, left_ref, wide_ref, d_ref, sem, *, dims
):
    leave = pltpu.make_async_copy(late_ref, out_ref, sem)
    leave.start()
    gx, gy, gz, lx, ly, lz, bx, by = dims
    plane, lplane = gy * gz, ly * lz
    k, j = lax.axis_index("space"), lax.axis_index("chan")
    brows = by * gz
    half = gx * brows
    for q in (0, gx + 1):
        d_ref[q] = jnp.zeros(d_ref.shape[1:], F32)
    d_ref[:, pl.ds(0, 16), :] = jnp.zeros((gx + 2, 16, 128), F32)
    d_ref[:, pl.ds(16 + plane, 16), :] = jnp.zeros((gx + 2, 16, 128), F32)
    for h in (0, 1):
        left_ref[pl.ds(0, 128), pl.ds((h + 1) * half - brows, brows)] = jnp.zeros((128, brows), BF)
        left_ref[pl.ds(2 * 128, 128), pl.ds(h * half, brows)] = jnp.zeros((128, brows), BF)
    back = (mine_ref[...] + other_ref[...].astype(F32)) * 0.125
    wide_ref[pl.ds(0, lx * lplane, stride=2), :] = back
    wide_ref[pl.ds(1, lx * lplane, stride=2), :] = back
    first = (brows - gz) * (1 - j)
    row = lax.broadcasted_iota(jnp.int32, (brows, 128), 0)
    border = (row >= first) & (row < first + gz)
    for lq in range(lx):
        for h, side in enumerate((j, 1 - j)):
            start = pl.multiple_of(lq * ly * gz + side * (by // 2 * gz), 8)
            rows = wide_ref[pl.ds(start, by // 2 * gz), :].reshape(by // 2, 1, gz, 128)
            rows = jnp.broadcast_to(rows, (by // 2, 2, gz, 128)).reshape(brows, 128)
            for x in (2 * lq, 2 * lq + 1):
                slope = (far_ref if h else slope_ref)[pl.ds(x * brows, brows), :]
                if h == 0:
                    tiles = jnp.concatenate([patch_ref[pl.ds(x * gz, gz), :]] * by, axis=0)
                    slope = jnp.where(border, tiles, slope)
                delta = (rows * slope).astype(BF).astype(F32)
                d_ref[x + 1, pl.ds(pl.multiple_of(16 + side * brows, 8), brows), :] = delta
                tile = delta.T.astype(BF)
                for a in range(3):
                    if 0 <= x + a - 1 < gx:
                        left_ref[pl.ds(a * 128, 128), pl.ds(h * half + (x + a - 1) * brows, brows)] = tile
    tap_terms(left_ref, col_ref, part_ref, 0, EARLY_TAPS)
    row = pl.multiple_of(j * brows, 8)
    for q in range(bx + 2):
        win_ref[q] = d_ref[k * bx + q, pl.ds(row, brows + 32), :]
    leave.wait()


def grad_volume_kernel(win_ref, wt_ref, gv_ref, vcol_ref, *, bx, brows, gz):
    cell = depth_of(brows, gz)
    for q in range(bx + 2):
        for n, (b, c) in enumerate(STEPS):
            vcol_ref[pl.ds(q * brows, brows), pl.ds(n * 128, 128)] = shifted(
                win_ref, (q,), 16, brows, cell, gz, (-b, -c)
            ).astype(BF)
    total = None
    for a in range(3):
        term = jnp.dot(vcol_ref[pl.ds((2 - a) * brows, bx * brows), :], wt_ref[a], preferred_element_type=F32)
        total = term if total is None else total + term
    gv_ref[...] = total.astype(BF)


def steps_of(count):
    return range(1, count)


def partner(index, by, count):
    if count & (count - 1) == 0:
        return index ^ by
    return lax.rem(index + count - by, count)


def turned(value, axis, by):
    count = lax.axis_size(axis)
    pairs = count & (count - 1) == 0
    return lax.ppermute(value, axis, [(i, i ^ by if pairs else (i + by) % count) for i in range(count)])


def call(kernel, outs, scratch, args, name, far=(), raw=(), away=()):
    args = [
        pltpu.with_memory_space_constraint(arg, pltpu.HBM if n in raw else pltpu.VMEM)
        for n, arg in enumerate(args)
    ]
    outs = [out if n in (*far, *away) else pltpu.VMEM(out.shape, out.dtype) for n, out in enumerate(outs)]
    return pl.pallas_call(
        kernel,
        out_shape=outs,
        in_specs=[
            pl.BlockSpec(memory_space=pltpu.HBM if n in raw else pltpu.VMEM) for n in range(len(args))
        ],
        out_specs=[
            pl.BlockSpec(memory_space=pltpu.HBM if n in away else pltpu.VMEM) for n in range(len(outs))
        ],
        scratch_shapes=scratch,
        compiler_params=pltpu.CompilerParams(vmem_limit_bytes=VMEM_BYTES),
        name=name,
    )(*args)


def whole_sample(volume, early_weight, late_weight, cotangent):
    nk, nj, nr = (lax.axis_size(axis) for axis in ("space", "chan", "rep"))
    _, bx, by, gz, _ = volume.shape
    _, cx, ly, lz, cl = cotangent.shape
    gx, gy, lx = bx * nk, by * nj, cx * nk
    plane, lplane, brows = gy * gz, ly * lz, by * gz
    rows, lrows = gx * plane, lx * lplane
    scale = 1.0 / math.sqrt(nr * lrows)
    sds = jax.ShapeDtypeStruct

    mine = volume.reshape(bx * brows, 128)
    line = [mine] + [turned(mine, "space", dk) for dk in steps_of(nk)]
    cot = cotangent.reshape(cx * ly, lz, cl)
    own, we, wcat = call(
        begin_kernel,
        [sds(mine.shape, BF), sds(early_weight.shape, BF), sds((9 * 128, 3 * 128), BF)],
        [pltpu.SemaphoreType.DMA((4,))],
        [mine, early_weight],
        "begin",
        raw=(0, 1),
    )
    line[0] = own
    cots = [cot] + [turned(cot, "space", dk) for dk in steps_of(nk)]

    dims = (gx, gy, gz, lx, ly, lz, bx, by)
    hrows, edge = gx * brows, 3 * gx * gz
    half, slope, send, edges = call(
        functools.partial(early_kernel, nk=nk, dims=dims),
        [
            sds((hrows, 128), BF),
            sds((hrows, 128), F32),
            sds((lrows // 2 + edge, 128), BF),
            sds((edge, 128), F32),
        ],
        [
            pltpu.VMEM((gx, brows + 32, 128), F32),
            pltpu.VMEM((hrows, 9 * 128), BF),
            pltpu.VMEM((hrows, 3 * 128), F32),
            pltpu.VMEM((gx, brows, 128), F32),
            pltpu.VMEM((by // 2 * gz, 128), F32),
            pltpu.VMEM((gx * gz, 128), F32),
        ],
        line + [wcat],
        "early",
    )
    ready, *cots[1:] = lax.optimization_barrier((send, *cots[1:]))
    send_other = turned(ready, "chan", 1)
    half_other = turned(half, "chan", 1)
    held, _ = lax.optimization_barrier((late_weight, send))
    wl, wback, wt = call(
        fetch_kernel,
        [sds(late_weight.shape, BF), sds((9 * cl, 3 * 128), BF), sds((3, 9 * 128, 128), BF)],
        [pltpu.SemaphoreType.DMA((3,))],
        [held, we],
        "fetch",
        raw=(0,),
    )
    pooled_delta, patch = call(
        functools.partial(late_kernel, nk=nk, dims=(gx, gz, lx, ly, lz, cx)),
        [sds((lrows, 128 + cl), BF), sds((gx * gz, 128), F32)],
        [
            pltpu.VMEM((lx, lplane + 16, 128), F32),
            pltpu.VMEM((lrows, 9 * 128), BF),
            pltpu.VMEM((lrows, cl), F32),
            pltpu.VMEM((lx * gz, 128), F32),
            pltpu.VMEM((lx * 2 * lz, 128), F32),
        ],
        [send, send_other, edges] + cots + [wl],
        "late",
    )
    back, back_mine = call(
        functools.partial(late_back_kernel, dims=(lx, ly, lz)),
        [sds((lrows, 128), BF), sds((lrows, 128), F32)],
        [pltpu.VMEM((lx, lplane + 16, cl), F32), pltpu.VMEM((lrows, 9 * cl), BF)],
        [pooled_delta, wback],
        "late_back",
    )
    pd_other = turned(pooled_delta, "rep", 1)
    back_other = turned(back, "chan", 1)
    (late,) = call(
        functools.partial(late_grad_kernel, dims=(lx, ly, lz), scale=scale),
        [sds((27 * 128, cl), BF)],
        [
            pltpu.VMEM((lx, lplane + 16, 128), F32),
            pltpu.VMEM((2 * lrows, 9 * 128), BF),
            pltpu.VMEM((2 * lrows, 3 * cl), BF),
        ],
        [pooled_delta, pd_other],
        "late_grad",
    )
    half_other, wcat, _, late = lax.optimization_barrier((half_other, wcat, back, late))
    col, far_slope = call(
        functools.partial(other_kernel, dims=dims),
        [sds((rows, 9 * 128), BF), sds((hrows, 128), F32)],
        [pltpu.VMEM((2, gx, brows + 32, 128), F32), pltpu.VMEM((hrows, 3 * 128), F32)],
        [half, half_other, wcat],
        "other",
    )
    back_mine, late = lax.optimization_barrier((back_mine, late))
    part, win, late, left = call(
        functools.partial(early_grad_kernel, dims=dims),
        [
            sds((3 * EARLY_TAPS * 128, 128), BF),
            sds((bx + 2, brows + 32, 128), F32),
            sds(late.shape, BF),
            sds((3 * 128, rows), BF),
        ],
        [
            pltpu.VMEM((lx * ly * gz, 128), F32),
            pltpu.VMEM((gx + 2, plane + 32, 128), F32),
            pltpu.SemaphoreType.DMA(()),
        ],
        [back_mine, back_other, slope, far_slope, patch, col, late],
        "early_grad",
        away=(2,),
    )
    part_other = turned(part, "rep", 1)
    (more,) = call(more_kernel, [sds((3 * (9 - EARLY_TAPS) * 128, 128), BF)], [], [left, col], "more")
    more_other = turned(more, "rep", 1)
    win, _ = lax.optimization_barrier((win, more))
    (gv,) = call(
        functools.partial(grad_volume_kernel, bx=bx, brows=brows, gz=gz),
        [sds((bx * brows, 128), BF)],
        [pltpu.VMEM(((bx + 2) * brows, 9 * 128), BF)],
        [win, wt],
        "grad_volume",
        far=(0,),
    )
    (early,) = call(
        functools.partial(finish_kernel, scale=scale),
        [sds((27 * 128, 128), BF)],
        [pltpu.VMEM((27 * 128, 128), BF), pltpu.SemaphoreType.DMA((3,))],
        [part, part_other, more, more_other],
        "finish",
        away=(0,),
    )
    return (
        early.reshape(3, 3, 3, 128, 128),
        late.reshape(3, 3, 3, 128, cl),
        gv.reshape(1, bx, by, gz, 128),
    )


def solution(mesh):
    few = mesh.shape["space"] * mesh.shape["chan"] <= GATHER_BLOCKS
    alone = mesh.shape["rep"] == 2 and mesh.shape["chan"] == 2
    return jax.shard_map(
        whole_sample if few and alone else per_device,
        mesh=mesh,
        in_specs=(
            P(("groups", "rep"), "space", "chan", None, None),
            P(),
            P(None, None, None, None, "chan"),
            P(("groups", "rep"), "space", None, None, "chan"),
        ),
        out_specs=(
            P("groups", None, None, None, None),
            P("groups", None, None, None, "chan"),
            P(("groups", "rep"), "space", "chan", None, None),
        ),
        check_vma=False,
    )
```

```python
import functools
import math

import jax
import jax.numpy as jnp
from jax import lax
from jax.experimental import pallas as pl
from jax.experimental.pallas import tpu as pltpu
from jax.sharding import PartitionSpec as P

BF = jnp.bfloat16
F32 = jnp.float32
VMEM_BYTES = 14 * 2**20
GATHER_BLOCKS = 8
EARLY_TAPS = 5


def padded_2(block, sides, width):
    for axis, dim in sides:
        count = lax.axis_size(axis)
        forward = [(i, i + 1) for i in range(count - 1)]
        backward = [(target, source) for source, target in forward]
        low = lax.ppermute(
            lax.slice_in_dim(block, block.shape[dim] - width, None, axis=dim), axis, forward
        )
        high = lax.ppermute(lax.slice_in_dim(block, 0, width, axis=dim), axis, backward)
        block = jnp.concatenate([low, block, high], axis=dim)
    return block


def gelu_tanh(value):
    return jax.nn.gelu(value, approximate=True)


def conv_padded(padded, weight):
    depth = padded.shape[1] - 2
    height = padded.shape[2] - 2
    length = padded.shape[3] - 2
    total = None
    for first in range(3):
        for second in range(3):
            for third in range(3):
                window = padded[
                    :, first : first + depth, second : second + height, third : third + length
                ]
                term = jnp.einsum(
                    "sxyzc,co->sxyzo",
                    window,
                    weight[first, second, third],
                    preferred_element_type=jnp.float32,
                )
                total = term if total is None else total + term
    return total


def kernel_grad(padded, delta):
    depth = delta.shape[1]
    height = delta.shape[2]
    length = delta.shape[3]
    planes = []
    for first in range(3):
        for second in range(3):
            for third in range(3):
                window = padded[
                    :, first : first + depth, second : second + height, third : third + length
                ]
                planes.append(
                    jnp.einsum("sxyzc,sxyzo->co", window, delta, preferred_element_type=jnp.float32)
                )
    stacked = jnp.stack(planes, axis=0)
    return stacked.reshape((3, 3, 3) + stacked.shape[1:])


def flipped(weight):
    return jnp.swapaxes(weight[::-1, ::-1, ::-1], 3, 4)


def pad_dims(field, dims):
    widths = [(1, 1) if place in dims else (0, 0) for place in range(field.ndim)]
    return jnp.pad(field, widths)


def pool_cells(field):
    s, x, y, z, c = field.shape
    return jnp.mean(field.reshape(s, x // 2, 2, y // 2, 2, z // 2, 2, c), axis=(2, 4, 6))


def spread_cells(field):
    s, x, y, z, c = field.shape
    wide = jnp.broadcast_to(field[:, :, None, :, None, :, None, :], (s, x, 2, y, 2, z, 2, c))
    return wide.reshape(s, 2 * x, 2 * y, 2 * z, c) * 0.125


def late_layer(joined, late_weight, cotangent):
    rim = padded_2(joined, (("space", 1),), 1)
    late_pad = pad_dims(rim, (2, 3))
    pre_late = conv_padded(late_pad, late_weight)
    delta_late = jax.vjp(gelu_tanh, pre_late)[1](cotangent.astype(jnp.float32))[0].astype(
        jnp.bfloat16
    )
    late_part = kernel_grad(late_pad, delta_late)
    delta_rim = padded_2(delta_late, (("space", 1),), 1)
    back_partial = conv_padded(pad_dims(delta_rim, (2, 3)), flipped(late_weight))
    return (back_partial, late_part)


def per_device(volume, early_weight, late_weight, cotangent):
    count = (
        cotangent.shape[0]
        * lax.axis_size("rep")
        * cotangent.shape[1]
        * lax.axis_size("space")
        * cotangent.shape[2]
        * cotangent.shape[3]
    )
    scale = 1.0 / math.sqrt(count)
    haloed = padded_2(volume, (("space", 1), ("chan", 2)), 1)
    padded_in = pad_dims(haloed, (3,))
    pre_early = conv_padded(padded_in, early_weight)
    pooled = pool_cells(gelu_tanh(pre_early)).astype(jnp.bfloat16)
    joined = lax.all_gather(pooled, "chan", axis=2, tiled=True)
    back_partial, late_part = late_layer(joined, late_weight, cotangent)
    back_rows = lax.psum_scatter(back_partial, "chan", scatter_dimension=2, tiled=True)
    delta_early = jax.vjp(gelu_tanh, pre_early)[1](spread_cells(back_rows))[0].astype(jnp.bfloat16)
    early_part = kernel_grad(padded_in, delta_early)
    delta_halo = padded_2(delta_early, (("space", 1), ("chan", 2)), 1)
    grad_volume = conv_padded(pad_dims(delta_halo, (3,)), flipped(early_weight)).astype(
        jnp.bfloat16
    )
    early_total = lax.psum(early_part, ("space", "chan", "rep"))
    grad_early = (early_total * scale).astype(jnp.bfloat16)
    late_total = lax.psum(late_part, ("space", "rep"))
    grad_late = (late_total * scale).astype(jnp.bfloat16)
    return (grad_early, grad_late, grad_volume)


NT = (((1,), (1,)), ((), ()))


def gelu_and_slope(v):
    k = 0.7978845608028654
    sq = v * v
    t = jnp.tanh(k * (v + 0.044715 * (v * sq)))
    half = 0.5 * (1.0 + t)
    return v * half, half + 0.5 * v * (1.0 - t * t) * (k * (1.0 + 0.134145 * sq))


def depth_of(rows, period):
    return lax.broadcasted_iota(jnp.int32, (rows, 128), 0) % period


def shifted(ref, lead, start, rows, cell, period, step):
    dy, dz = step
    got = ref[lead + (pl.ds(start + dy * period + dz, rows), slice(None))]
    if dz == 0:
        return got
    lanes = got.shape[1] // 128
    edge = (cell == 0) if dz < 0 else (cell == period - 1)
    edge = jnp.concatenate([edge] * lanes, axis=1) if lanes > 1 else edge
    return jnp.where(edge, 0.0, got)


STEPS = [(b, c) for b in (-1, 0, 1) for c in (-1, 0, 1)]


def fold(parts, rows):
    zero = jnp.zeros((rows, parts[0].shape[1]), F32)
    return (
        parts[1]
        + jnp.concatenate([zero, parts[0][:-rows]], axis=0)
        + jnp.concatenate([parts[2][rows:], zero], axis=0)
    )


def begin_kernel(own_hbm, we_hbm, own_ref, we_ref, wcat_ref, sems):
    own = pltpu.make_async_copy(own_hbm, own_ref, sems.at[3])
    copies = [pltpu.make_async_copy(we_hbm.at[a], we_ref.at[a], sems.at[a]) for a in range(3)]
    for copy in (*copies, own):
        copy.start()
    for a in range(3):
        copies[a].wait()
        for n in range(9):
            b, c = divmod(n, 3)
            wcat_ref[pl.ds(n * 128, 128), pl.ds(a * 128, 128)] = we_ref[a, b, c]
    own.wait()


def early_kernel(*refs, nk, dims):
    gx, gy, gz, lx, ly, lz, bx, by = dims
    blocks, refs = refs[:nk], refs[nk:]
    wcat_ref, half_ref, slope_ref, send_ref, edge_ref = refs[:5]
    vol_ref, col_ref, p_ref, pre_ref, h_ref, row_ref = refs[5:]
    k, j = lax.axis_index("space"), lax.axis_index("chan")
    brows, hl, line = by * gz, by // 2 * lz, gx * gz
    vol_ref[:, pl.ds(0, 16), :] = jnp.zeros((gx, 16, 128), F32)
    vol_ref[:, pl.ds(16 + brows, 16), :] = jnp.zeros((gx, 16, 128), F32)
    for n, dk in enumerate([0, *steps_of(nk)]):
        src = blocks[n]
        kk = partner(k, dk, nk)
        for q in range(bx):
            got = src[pl.ds(q * brows, brows), :]
            vol_ref[kk * bx + q, pl.ds(16, brows), :] = got.astype(F32)
            half_ref[pl.ds(pl.multiple_of((kk * bx + q) * brows, brows), brows), :] = got

    cell = depth_of(brows, gz)
    for x in range(gx):
        for n, step in enumerate(STEPS):
            col_ref[pl.ds(x * brows, brows), pl.ds(n * 128, 128)] = shifted(
                vol_ref, (x,), 16, brows, cell, gz, step
            ).astype(BF)

    p_ref[...] = jnp.dot(col_ref[...], wcat_ref[...], preferred_element_type=F32)

    outer = pl.multiple_of((brows - gz) * (1 - j), gz)
    inner = pl.multiple_of((brows - 2 * gz) * (1 - j) + gz * j, gz)
    for x in range(gx):
        row_ref[pl.ds(x * gz, gz), :] = vol_ref[x, pl.ds(16 + outer, gz), :]
    row = row_ref[...]
    rcell = depth_of(line, gz)
    trio = [
        jnp.where(rcell == 0, 0.0, pltpu.roll(row, 1, 0)),
        row,
        jnp.where(rcell == gz - 1, 0.0, pltpu.roll(row, line - 1, 0)),
    ]
    taps = wcat_ref[pl.ds(pl.multiple_of(j * (6 * 128), 128), 3 * 128), :]
    given = jnp.dot(jnp.concatenate(trio, axis=1).astype(BF), taps, preferred_element_type=F32)
    given = fold([given[:, a * 128 : (a + 1) * 128] for a in range(3)], gz)

    for lq in range(lx):
        pair = None
        for x in (2 * lq, 2 * lq + 1):
            pre = p_ref[pl.ds(x * brows, brows), pl.ds(128, 128)]
            if x > 0:
                pre = pre + p_ref[pl.ds((x - 1) * brows, brows), pl.ds(0, 128)]
            if x < gx - 1:
                pre = pre + p_ref[pl.ds((x + 1) * brows, brows), pl.ds(256, 128)]
            pre_ref[x] = pre
            h, slope = gelu_and_slope(pre)
            slope_ref[pl.ds(x * brows, brows), :] = slope
            pair = h if pair is None else pair + h
        wide = pair.reshape(by // 2, 2, gz, 128)
        h_ref[...] = (wide[:, 0] + wide[:, 1]).reshape(by // 2 * gz, 128)
        pooled = (h_ref[pl.ds(0, hl, stride=2), :] + h_ref[pl.ds(1, hl, stride=2), :]) * 0.125
        send_ref[pl.ds(lq * hl, hl), :] = pooled.astype(BF)
    for x in range(gx):
        edge_ref[pl.ds(x * gz, gz), :] = pre_ref[x, pl.ds(inner, gz), :]
        edge_ref[pl.ds(line + x * gz, gz), :] = pre_ref[x, pl.ds(outer, gz), :]
    edge_ref[pl.ds(2 * line, line), :] = given
    send_ref[pl.ds(lx * hl, 3 * line), :] = edge_ref[...].astype(BF)


def fetch_kernel(far_ref, we_ref, near_ref, back_ref, wt_ref, sems):
    copies = [pltpu.make_async_copy(far_ref.at[a], near_ref.at[a], sems.at[a]) for a in range(3)]
    cl = near_ref.shape[-1]
    for copy in copies:
        copy.start()
    for n in range(9):
        b, c = divmod(n, 3)
        for a in range(3):
            wt_ref[a, pl.ds(n * 128, 128), :] = we_ref[a, b, c].astype(F32).T.astype(BF)
    for a in range(3):
        copies[a].wait()
        for n in range(9):
            b, c = divmod(n, 3)
            back_ref[pl.ds(n * cl, cl), pl.ds(a * 128, 128)] = near_ref[a, b, c].astype(F32).T.astype(BF)


def border_pool(inner, outer, tmp_ref, tile_ref, dims):
    lx, lz, gz = dims
    h, slope = gelu_and_slope(outer)
    h = (h + gelu_and_slope(inner)[0]).reshape(lx, 2, gz, 128)
    tmp_ref[...] = (h[:, 0] + h[:, 1]).reshape(lx * gz, 128)
    got = (tmp_ref[pl.ds(0, lx * lz, stride=2), :] + tmp_ref[pl.ds(1, lx * lz, stride=2), :]) * 0.125
    got = got.astype(BF).astype(F32)
    for x in range(lx):
        for copy in range(2):
            tile_ref[pl.ds((2 * x + copy) * lz, lz), :] = got[x * lz : (x + 1) * lz]
    return slope


def late_kernel(*refs, nk, dims):
    gx, gz, lx, ly, lz, cx = dims
    sent_ref, got_ref, edge_ref, cots, refs = *refs[:3], refs[3 : nk + 3], refs[nk + 3 :]
    wl_ref, pd_ref, patch_ref = refs[:3]
    pool_ref, lcol_ref, cot_ref, tmp_ref, tile_ref = refs[3:]
    lplane, hl, line = ly * lz, ly // 2 * lz, gx * gz
    cl = wl_ref.shape[-1]
    crow = cx * lplane
    k, j = lax.axis_index("space"), lax.axis_index("chan")
    edges = got_ref[pl.ds(lx * hl, 3 * line), :].astype(F32)
    lrow = lax.broadcasted_iota(jnp.int32, (hl, 128), 0)
    for x in range(lx):
        pool_ref[x, pl.ds(0, 8), :] = jnp.zeros((8, 128), F32)
        pool_ref[x, pl.ds(8 + lplane, 8), :] = jnp.zeros((8, 128), F32)
    sides = (
        (j, sent_ref, edge_ref[pl.ds(0, line), :], edge_ref[pl.ds(line, line), :] + edges[2 * line :]),
        (1 - j, got_ref, edges[:line], edges[line : 2 * line] + edge_ref[pl.ds(2 * line, line), :]),
    )
    for n, (side, ref, inner, outer) in enumerate(sides):
        slope = border_pool(inner, outer, tmp_ref, tile_ref, (lx, lz, gz))
        if n == 0:
            patch_ref[...] = slope
        first = (hl - lz) * (1 - side)
        border = (lrow >= first) & (lrow < first + lz)
        for x in range(lx):
            tiles = jnp.concatenate([tile_ref[pl.ds(x * 2 * lz, 2 * lz), :]] * (hl // (2 * lz)), axis=0)
            start = pl.multiple_of(8 + side * hl, 8)
            pool_ref[x, pl.ds(start, hl), :] = jnp.where(
                border, tiles, ref[pl.ds(x * hl, hl), :].astype(F32)
            )
    for x in range(lx):
        pd_ref[pl.ds(x * lplane, lplane), pl.ds(0, 128)] = pool_ref[x, pl.ds(8, lplane), :].astype(BF)

    lcell = depth_of(lplane, lz)
    for x in range(lx):
        for n, step in enumerate(STEPS):
            lcol_ref[pl.ds(x * lplane, lplane), pl.ds(n * 128, 128)] = shifted(
                pool_ref, (x,), 8, lplane, lcell, lz, step
            ).astype(BF)
    lcol = lcol_ref[...]
    parts = [
        jnp.dot(lcol, wl_ref[a].reshape(9 * 128, cl), preferred_element_type=F32) for a in range(3)
    ]
    pre = fold(parts, lplane)
    slope = gelu_and_slope(pre)[1]
    for n, dk in enumerate([0, *steps_of(nk)]):
        kk = partner(k, dk, nk)
        start = pl.multiple_of(kk * crow, 8)
        cot_ref[pl.ds(start, crow), :] = cots[n][...].astype(F32).reshape(crow, cl)
    delta = (cot_ref[...] * slope).astype(BF)
    pd_ref[:, pl.ds(128, cl)] = delta


def late_back_kernel(pd_ref, wback_ref, back_ref, mine_ref, dl_ref, dcol_ref, *, dims):
    lx, ly, lz = dims
    lplane = ly * lz
    cl = pd_ref.shape[1] - 128
    lcell = depth_of(lplane, lz)
    for x in range(lx):
        dl_ref[x, pl.ds(0, 8), :] = jnp.zeros((8, cl), F32)
        dl_ref[x, pl.ds(8 + lplane, 8), :] = jnp.zeros((8, cl), F32)
        dl_ref[x, pl.ds(8, lplane), :] = pd_ref[pl.ds(x * lplane, lplane), pl.ds(128, cl)].astype(F32)
    for n, (b, c) in enumerate(STEPS):
        for x in range(lx):
            dcol_ref[pl.ds(x * lplane, lplane), pl.ds(n * cl, cl)] = shifted(
                dl_ref, (x,), 8, lplane, lcell, lz, (-b, -c)
            ).astype(BF)
    total = jnp.dot(dcol_ref[...], wback_ref[...], preferred_element_type=F32)
    back = fold([total[:, (2 - a) * 128 : (3 - a) * 128] for a in range(3)], lplane)
    back_ref[...] = back.astype(BF)
    mine_ref[...] = back


def late_grad_kernel(mine_ref, other_ref, out_ref, pool_ref, lcol_ref, wide_ref, *, dims, scale):
    lx, ly, lz = dims
    lplane = ly * lz
    rows = lx * lplane
    cl = mine_ref.shape[1] - 128
    lcell = depth_of(lplane, lz)
    for x in range(lx):
        pool_ref[x, pl.ds(0, 8), :] = jnp.zeros((8, 128), F32)
        pool_ref[x, pl.ds(8 + lplane, 8), :] = jnp.zeros((8, 128), F32)
    for s, ref in enumerate((mine_ref, other_ref)):
        for x in range(lx):
            pool_ref[x, pl.ds(8, lplane), :] = ref[pl.ds(x * lplane, lplane), pl.ds(0, 128)].astype(F32)
        for x in range(lx):
            for n, step in enumerate(STEPS):
                lcol_ref[pl.ds(s * rows + x * lplane, lplane), pl.ds(n * 128, 128)] = shifted(
                    pool_ref, (x,), 8, lplane, lcell, lz, step
                ).astype(BF)
        zero = jnp.zeros((lplane, cl), BF)
        wide_ref[pl.ds(s * rows + rows - lplane, lplane), pl.ds(0, cl)] = zero
        wide_ref[pl.ds(s * rows, rows - lplane), pl.ds(0, cl)] = ref[pl.ds(lplane, rows - lplane), pl.ds(128, cl)]
        wide_ref[pl.ds(s * rows, rows), pl.ds(cl, cl)] = ref[:, pl.ds(128, cl)]
        wide_ref[pl.ds(s * rows, lplane), pl.ds(2 * cl, cl)] = zero
        wide_ref[pl.ds(s * rows + lplane, rows - lplane), pl.ds(2 * cl, cl)] = ref[
            pl.ds(0, rows - lplane), pl.ds(128, cl)
        ]
    got = lax.dot_general(
        lcol_ref[...], wide_ref[...], (((0,), (0,)), ((), ())), preferred_element_type=F32
    )
    for a in range(3):
        out_ref[pl.ds(a * 9 * 128, 9 * 128), :] = (got[:, a * cl : (a + 1) * cl] * scale).astype(BF)


def other_kernel(
    half_ref, got_ref, wcat_ref, col_ref, slope_ref, vol_ref, p_ref, *, dims
):
    gx, gy, gz, lx, ly, lz, bx, by = dims
    brows = by * gz
    j = lax.axis_index("chan")
    vol_ref[:, :, pl.ds(0, 16), :] = jnp.zeros((2, gx, 16, 128), F32)
    vol_ref[:, :, pl.ds(16 + brows, 16), :] = jnp.zeros((2, gx, 16, 128), F32)
    for h, src in enumerate((half_ref, got_ref)):
        for x in range(gx):
            vol_ref[h, x, pl.ds(16, brows), :] = src[pl.ds(x * brows, brows), :].astype(F32)
    for h, side in enumerate((j, 1 - j)):
        into = pl.multiple_of((16 + brows) * (1 - side) + (16 - gz) * side, 8)
        start = pl.multiple_of(16 + (brows - gz) * side, 8)
        for x in range(gx):
            vol_ref[h, x, pl.ds(into, gz), :] = vol_ref[1 - h, x, pl.ds(start, gz), :]
    cell = depth_of(brows, gz)
    for h in (1, 0):
        for x in range(gx):
            for n, step in enumerate(STEPS):
                col_ref[pl.ds((h * gx + x) * brows, brows), pl.ds(n * 128, 128)] = shifted(
                    vol_ref, (h, x), 16, brows, cell, gz, step
                ).astype(BF)
    p_ref[...] = jnp.dot(
        col_ref[pl.ds(gx * brows, gx * brows), :], wcat_ref[...], preferred_element_type=F32
    )
    for x in range(gx):
        pre = p_ref[pl.ds(x * brows, brows), pl.ds(128, 128)]
        if x > 0:
            pre = pre + p_ref[pl.ds((x - 1) * brows, brows), pl.ds(0, 128)]
        if x < gx - 1:
            pre = pre + p_ref[pl.ds((x + 1) * brows, brows), pl.ds(256, 128)]
        slope_ref[pl.ds(x * brows, brows), :] = gelu_and_slope(pre)[1]


def tap_terms(left_ref, col_ref, part_ref, first, count):
    got = jnp.dot(left_ref[...], col_ref[:, pl.ds(first * 128, count * 128)], preferred_element_type=F32)
    for a in range(3):
        for n in range(count):
            part_ref[pl.ds((a * count + n) * 128, 128), :] = got[
                a * 128 : (a + 1) * 128, n * 128 : (n + 1) * 128
            ].T.astype(part_ref.dtype)


def more_kernel(left_ref, col_ref, part_ref):
    tap_terms(left_ref, col_ref, part_ref, EARLY_TAPS, 9 - EARLY_TAPS)


def finish_kernel(one_ref, one_got_ref, two_ref, two_got_ref, out_ref, sum_ref, sems, *, scale):
    copies = []
    for a in range(3):
        at = a * 9 * 128
        for mine_ref, got_ref, count in (
            (one_ref, one_got_ref, EARLY_TAPS), (two_ref, two_got_ref, 9 - EARLY_TAPS)
        ):
            rows = pl.ds(a * count * 128, count * 128)
            total = mine_ref[rows, :].astype(F32) + got_ref[rows, :].astype(F32)
            sum_ref[pl.ds(at, count * 128), :] = (total * scale).astype(BF)
            at += count * 128
        rows = pl.ds(a * 9 * 128, 9 * 128)
        copies.append(pltpu.make_async_copy(sum_ref.at[rows], out_ref.at[rows], sems.at[a]))
        copies[-1].start()
    for copy in copies:
        copy.wait()


def early_grad_kernel(
    mine_ref, other_ref, slope_ref, far_ref, patch_ref, col_ref, late_ref,
    part_ref, win_ref, out_ref, left_ref, wide_ref, d_ref, sem, *, dims
):
    leave = pltpu.make_async_copy(late_ref, out_ref, sem)
    leave.start()
    gx, gy, gz, lx, ly, lz, bx, by = dims
    plane, lplane = gy * gz, ly * lz
    k, j = lax.axis_index("space"), lax.axis_index("chan")
    brows = by * gz
    half = gx * brows
    for q in (0, gx + 1):
        d_ref[q] = jnp.zeros(d_ref.shape[1:], F32)
    d_ref[:, pl.ds(0, 16), :] = jnp.zeros((gx + 2, 16, 128), F32)
    d_ref[:, pl.ds(16 + plane, 16), :] = jnp.zeros((gx + 2, 16, 128), F32)
    for h in (0, 1):
        left_ref[pl.ds(0, 128), pl.ds((h + 1) * half - brows, brows)] = jnp.zeros((128, brows), BF)
        left_ref[pl.ds(2 * 128, 128), pl.ds(h * half, brows)] = jnp.zeros((128, brows), BF)
    back = (mine_ref[...] + other_ref[...].astype(F32)) * 0.125
    wide_ref[pl.ds(0, lx * lplane, stride=2), :] = back
    wide_ref[pl.ds(1, lx * lplane, stride=2), :] = back
    first = (brows - gz) * (1 - j)
    row = lax.broadcasted_iota(jnp.int32, (brows, 128), 0)
    border = (row >= first) & (row < first + gz)
    for lq in range(lx):
        for h, side in enumerate((j, 1 - j)):
            start = pl.multiple_of(lq * ly * gz + side * (by // 2 * gz), 8)
            rows = wide_ref[pl.ds(start, by // 2 * gz), :].reshape(by // 2, 1, gz, 128)
            rows = jnp.broadcast_to(rows, (by // 2, 2, gz, 128)).reshape(brows, 128)
            for x in (2 * lq, 2 * lq + 1):
                slope = (far_ref if h else slope_ref)[pl.ds(x * brows, brows), :]
                if h == 0:
                    tiles = jnp.concatenate([patch_ref[pl.ds(x * gz, gz), :]] * by, axis=0)
                    slope = jnp.where(border, tiles, slope)
                delta = (rows * slope).astype(BF).astype(F32)
                d_ref[x + 1, pl.ds(pl.multiple_of(16 + side * brows, 8), brows), :] = delta
                tile = delta.T.astype(BF)
                for a in range(3):
                    if 0 <= x + a - 1 < gx:
                        left_ref[pl.ds(a * 128, 128), pl.ds(h * half + (x + a - 1) * brows, brows)] = tile
    tap_terms(left_ref, col_ref, part_ref, 0, EARLY_TAPS)
    row = pl.multiple_of(j * brows, 8)
    for q in range(bx + 2):
        win_ref[q] = d_ref[k * bx + q, pl.ds(row, brows + 32), :]
    leave.wait()


def grad_volume_kernel(win_ref, wt_ref, gv_ref, vcol_ref, *, bx, brows, gz):
    cell = depth_of(brows, gz)
    for q in range(bx + 2):
        for n, (b, c) in enumerate(STEPS):
            vcol_ref[pl.ds(q * brows, brows), pl.ds(n * 128, 128)] = shifted(
                win_ref, (q,), 16, brows, cell, gz, (-b, -c)
            ).astype(BF)
    total = None
    for a in range(3):
        term = jnp.dot(vcol_ref[pl.ds((2 - a) * brows, bx * brows), :], wt_ref[a], preferred_element_type=F32)
        total = term if total is None else total + term
    gv_ref[...] = total.astype(BF)


def steps_of(count):
    return range(1, count)


def partner(index, by, count):
    if count & (count - 1) == 0:
        return index ^ by
    return lax.rem(index + count - by, count)


def turned(value, axis, by):
    count = lax.axis_size(axis)
    pairs = count & (count - 1) == 0
    return lax.ppermute(value, axis, [(i, i ^ by if pairs else (i + by) % count) for i in range(count)])


def call(kernel, outs, scratch, args, name, far=(), raw=(), away=()):
    args = [
        pltpu.with_memory_space_constraint(arg, pltpu.HBM if n in raw else pltpu.VMEM)
        for n, arg in enumerate(args)
    ]
    outs = [out if n in (*far, *away) else pltpu.VMEM(out.shape, out.dtype) for n, out in enumerate(outs)]
    return pl.pallas_call(
        kernel,
        out_shape=outs,
        in_specs=[
            pl.BlockSpec(memory_space=pltpu.HBM if n in raw else pltpu.VMEM) for n in range(len(args))
        ],
        out_specs=[
            pl.BlockSpec(memory_space=pltpu.HBM if n in away else pltpu.VMEM) for n in range(len(outs))
        ],
        scratch_shapes=scratch,
        compiler_params=pltpu.CompilerParams(vmem_limit_bytes=VMEM_BYTES),
        name=name,
    )(*args)


def whole_sample(volume, early_weight, late_weight, cotangent):
    nk, nj, nr = (lax.axis_size(axis) for axis in ("space", "chan", "rep"))
    _, bx, by, gz, _ = volume.shape
    _, cx, ly, lz, cl = cotangent.shape
    gx, gy, lx = bx * nk, by * nj, cx * nk
    plane, lplane, brows = gy * gz, ly * lz, by * gz
    rows, lrows = gx * plane, lx * lplane
    scale = 1.0 / math.sqrt(nr * lrows)
    sds = jax.ShapeDtypeStruct

    mine = volume.reshape(bx * brows, 128)
    line = [mine] + [turned(mine, "space", dk) for dk in steps_of(nk)]
    cot = cotangent.reshape(cx * ly, lz, cl)
    own, we, wcat = call(
        begin_kernel,
        [sds(mine.shape, BF), sds(early_weight.shape, BF), sds((9 * 128, 3 * 128), BF)],
        [pltpu.SemaphoreType.DMA((4,))],
        [mine, early_weight],
        "begin",
        raw=(0, 1),
    )
    line[0] = own
    late_steps = [dk for dk in range(1, nk) if nk & (nk - 1) == 0 and dk & (dk - 1)]
    cots = {dk: turned(cot, "space", dk) for dk in steps_of(nk) if dk not in late_steps}

    dims = (gx, gy, gz, lx, ly, lz, bx, by)
    hrows, edge = gx * brows, 3 * gx * gz
    half, slope, send, edges = call(
        functools.partial(early_kernel, nk=nk, dims=dims),
        [
            sds((hrows, 128), BF),
            sds((hrows, 128), F32),
            sds((lrows // 2 + edge, 128), BF),
            sds((edge, 128), F32),
        ],
        [
            pltpu.VMEM((gx, brows + 32, 128), F32),
            pltpu.VMEM((hrows, 9 * 128), BF),
            pltpu.VMEM((hrows, 3 * 128), F32),
            pltpu.VMEM((gx, brows, 128), F32),
            pltpu.VMEM((by // 2 * gz, 128), F32),
            pltpu.VMEM((gx * gz, 128), F32),
        ],
        line + [wcat],
        "early",
    )
    ready, cots = lax.optimization_barrier((send, cots))
    send_other = turned(ready, "chan", 1)
    half_other = turned(half, "chan", 1)
    for dk in late_steps:
        low = dk & -dk
        cots[dk] = turned(cots[dk ^ low], "space", low)
    cots = [cot] + [cots[dk] for dk in steps_of(nk)]
    held, _ = lax.optimization_barrier((late_weight, send))
    wl, wback, wt = call(
        fetch_kernel,
        [sds(late_weight.shape, BF), sds((9 * cl, 3 * 128), BF), sds((3, 9 * 128, 128), BF)],
        [pltpu.SemaphoreType.DMA((3,))],
        [held, we],
        "fetch",
        raw=(0,),
    )
    pooled_delta, patch = call(
        functools.partial(late_kernel, nk=nk, dims=(gx, gz, lx, ly, lz, cx)),
        [sds((lrows, 128 + cl), BF), sds((gx * gz, 128), F32)],
        [
            pltpu.VMEM((lx, lplane + 16, 128), F32),
            pltpu.VMEM((lrows, 9 * 128), BF),
            pltpu.VMEM((lrows, cl), F32),
            pltpu.VMEM((lx * gz, 128), F32),
            pltpu.VMEM((lx * 2 * lz, 128), F32),
        ],
        [send, send_other, edges] + cots + [wl],
        "late",
    )
    back, back_mine = call(
        functools.partial(late_back_kernel, dims=(lx, ly, lz)),
        [sds((lrows, 128), BF), sds((lrows, 128), F32)],
        [pltpu.VMEM((lx, lplane + 16, cl), F32), pltpu.VMEM((lrows, 9 * cl), BF)],
        [pooled_delta, wback],
        "late_back",
    )
    pd_other = turned(pooled_delta, "rep", 1)
    back_other = turned(back, "chan", 1)
    (late,) = call(
        functools.partial(late_grad_kernel, dims=(lx, ly, lz), scale=scale),
        [sds((27 * 128, cl), BF)],
        [
            pltpu.VMEM((lx, lplane + 16, 128), F32),
            pltpu.VMEM((2 * lrows, 9 * 128), BF),
            pltpu.VMEM((2 * lrows, 3 * cl), BF),
        ],
        [pooled_delta, pd_other],
        "late_grad",
    )
    half_other, wcat, _, late = lax.optimization_barrier((half_other, wcat, back, late))
    col, far_slope = call(
        functools.partial(other_kernel, dims=dims),
        [sds((rows, 9 * 128), BF), sds((hrows, 128), F32)],
        [pltpu.VMEM((2, gx, brows + 32, 128), F32), pltpu.VMEM((hrows, 3 * 128), F32)],
        [half, half_other, wcat],
        "other",
    )
    back_mine, late = lax.optimization_barrier((back_mine, late))
    part, win, late, left = call(
        functools.partial(early_grad_kernel, dims=dims),
        [
            sds((3 * EARLY_TAPS * 128, 128), BF),
            sds((bx + 2, brows + 32, 128), F32),
            sds(late.shape, BF),
            sds((3 * 128, rows), BF),
        ],
        [
            pltpu.VMEM((lx * ly * gz, 128), F32),
            pltpu.VMEM((gx + 2, plane + 32, 128), F32),
            pltpu.SemaphoreType.DMA(()),
        ],
        [back_mine, back_other, slope, far_slope, patch, col, late],
        "early_grad",
        away=(2,),
    )
    part_other = turned(part, "rep", 1)
    (more,) = call(more_kernel, [sds((3 * (9 - EARLY_TAPS) * 128, 128), BF)], [], [left, col], "more")
    more_other = turned(more, "rep", 1)
    win, _ = lax.optimization_barrier((win, more))
    (gv,) = call(
        functools.partial(grad_volume_kernel, bx=bx, brows=brows, gz=gz),
        [sds((bx * brows, 128), BF)],
        [pltpu.VMEM(((bx + 2) * brows, 9 * 128), BF)],
        [win, wt],
        "grad_volume",
        far=(0,),
    )
    (early,) = call(
        functools.partial(finish_kernel, scale=scale),
        [sds((27 * 128, 128), BF)],
        [pltpu.VMEM((27 * 128, 128), BF), pltpu.SemaphoreType.DMA((3,))],
        [part, part_other, more, more_other],
        "finish",
        away=(0,),
    )
    return (
        early.reshape(3, 3, 3, 128, 128),
        late.reshape(3, 3, 3, 128, cl),
        gv.reshape(1, bx, by, gz, 128),
    )


def solution(mesh):
    few = mesh.shape["space"] * mesh.shape["chan"] <= GATHER_BLOCKS
    alone = mesh.shape["rep"] == 2 and mesh.shape["chan"] == 2
    return jax.shard_map(
        whole_sample if few and alone else per_device,
        mesh=mesh,
        in_specs=(
            P(("groups", "rep"), "space", "chan", None, None),
            P(),
            P(None, None, None, None, "chan"),
            P(("groups", "rep"), "space", None, None, "chan"),
        ),
        out_specs=(
            P("groups", None, None, None, None),
            P("groups", None, None, None, "chan"),
            P(("groups", "rep"), "space", "chan", None, None),
        ),
        check_vma=False,
    )
```

```python
import functools
import math

import jax
import jax.numpy as jnp
from jax import lax
from jax.experimental import pallas as pl
from jax.experimental.pallas import tpu as pltpu
from jax.sharding import PartitionSpec as P

BF = jnp.bfloat16
F32 = jnp.float32
VMEM_BYTES = 14 * 2**20
GATHER_BLOCKS = 8
EARLY_TAPS = 5


def padded_2(block, sides, width):
    for axis, dim in sides:
        count = lax.axis_size(axis)
        forward = [(i, i + 1) for i in range(count - 1)]
        backward = [(target, source) for source, target in forward]
        low = lax.ppermute(
            lax.slice_in_dim(block, block.shape[dim] - width, None, axis=dim), axis, forward
        )
        high = lax.ppermute(lax.slice_in_dim(block, 0, width, axis=dim), axis, backward)
        block = jnp.concatenate([low, block, high], axis=dim)
    return block


def gelu_tanh(value):
    return jax.nn.gelu(value, approximate=True)


def conv_padded(padded, weight):
    depth = padded.shape[1] - 2
    height = padded.shape[2] - 2
    length = padded.shape[3] - 2
    total = None
    for first in range(3):
        for second in range(3):
            for third in range(3):
                window = padded[
                    :, first : first + depth, second : second + height, third : third + length
                ]
                term = jnp.einsum(
                    "sxyzc,co->sxyzo",
                    window,
                    weight[first, second, third],
                    preferred_element_type=jnp.float32,
                )
                total = term if total is None else total + term
    return total


def kernel_grad(padded, delta):
    depth = delta.shape[1]
    height = delta.shape[2]
    length = delta.shape[3]
    planes = []
    for first in range(3):
        for second in range(3):
            for third in range(3):
                window = padded[
                    :, first : first + depth, second : second + height, third : third + length
                ]
                planes.append(
                    jnp.einsum("sxyzc,sxyzo->co", window, delta, preferred_element_type=jnp.float32)
                )
    stacked = jnp.stack(planes, axis=0)
    return stacked.reshape((3, 3, 3) + stacked.shape[1:])


def flipped(weight):
    return jnp.swapaxes(weight[::-1, ::-1, ::-1], 3, 4)


def pad_dims(field, dims):
    widths = [(1, 1) if place in dims else (0, 0) for place in range(field.ndim)]
    return jnp.pad(field, widths)


def pool_cells(field):
    s, x, y, z, c = field.shape
    return jnp.mean(field.reshape(s, x // 2, 2, y // 2, 2, z // 2, 2, c), axis=(2, 4, 6))


def spread_cells(field):
    s, x, y, z, c = field.shape
    wide = jnp.broadcast_to(field[:, :, None, :, None, :, None, :], (s, x, 2, y, 2, z, 2, c))
    return wide.reshape(s, 2 * x, 2 * y, 2 * z, c) * 0.125


def late_layer(joined, late_weight, cotangent):
    rim = padded_2(joined, (("space", 1),), 1)
    late_pad = pad_dims(rim, (2, 3))
    pre_late = conv_padded(late_pad, late_weight)
    delta_late = jax.vjp(gelu_tanh, pre_late)[1](cotangent.astype(jnp.float32))[0].astype(
        jnp.bfloat16
    )
    late_part = kernel_grad(late_pad, delta_late)
    delta_rim = padded_2(delta_late, (("space", 1),), 1)
    back_partial = conv_padded(pad_dims(delta_rim, (2, 3)), flipped(late_weight))
    return (back_partial, late_part)


def per_device(volume, early_weight, late_weight, cotangent):
    count = (
        cotangent.shape[0]
        * lax.axis_size("rep")
        * cotangent.shape[1]
        * lax.axis_size("space")
        * cotangent.shape[2]
        * cotangent.shape[3]
    )
    scale = 1.0 / math.sqrt(count)
    haloed = padded_2(volume, (("space", 1), ("chan", 2)), 1)
    padded_in = pad_dims(haloed, (3,))
    pre_early = conv_padded(padded_in, early_weight)
    pooled = pool_cells(gelu_tanh(pre_early)).astype(jnp.bfloat16)
    joined = lax.all_gather(pooled, "chan", axis=2, tiled=True)
    back_partial, late_part = late_layer(joined, late_weight, cotangent)
    back_rows = lax.psum_scatter(back_partial, "chan", scatter_dimension=2, tiled=True)
    delta_early = jax.vjp(gelu_tanh, pre_early)[1](spread_cells(back_rows))[0].astype(jnp.bfloat16)
    early_part = kernel_grad(padded_in, delta_early)
    delta_halo = padded_2(delta_early, (("space", 1), ("chan", 2)), 1)
    grad_volume = conv_padded(pad_dims(delta_halo, (3,)), flipped(early_weight)).astype(
        jnp.bfloat16
    )
    early_total = lax.psum(early_part, ("space", "chan", "rep"))
    grad_early = (early_total * scale).astype(jnp.bfloat16)
    late_total = lax.psum(late_part, ("space", "rep"))
    grad_late = (late_total * scale).astype(jnp.bfloat16)
    return (grad_early, grad_late, grad_volume)


NT = (((1,), (1,)), ((), ()))


def gelu_and_slope(v):
    k = 0.7978845608028654
    sq = v * v
    t = jnp.tanh(k * (v + 0.044715 * (v * sq)))
    half = 0.5 * (1.0 + t)
    return v * half, half + 0.5 * v * (1.0 - t * t) * (k * (1.0 + 0.134145 * sq))


def depth_of(rows, period):
    return lax.broadcasted_iota(jnp.int32, (rows, 128), 0) % period


def shifted(ref, lead, start, rows, cell, period, step):
    dy, dz = step
    got = ref[lead + (pl.ds(start + dy * period + dz, rows), slice(None))]
    if dz == 0:
        return got
    lanes = got.shape[1] // 128
    edge = (cell == 0) if dz < 0 else (cell == period - 1)
    edge = jnp.concatenate([edge] * lanes, axis=1) if lanes > 1 else edge
    return jnp.where(edge, 0.0, got)


STEPS = [(b, c) for b in (-1, 0, 1) for c in (-1, 0, 1)]


def fold(parts, rows):
    zero = jnp.zeros((rows, parts[0].shape[1]), F32)
    return (
        parts[1]
        + jnp.concatenate([zero, parts[0][:-rows]], axis=0)
        + jnp.concatenate([parts[2][rows:], zero], axis=0)
    )


def begin_kernel(own_hbm, we_hbm, own_ref, we_ref, wcat_ref, sems):
    own = pltpu.make_async_copy(own_hbm, own_ref, sems.at[3])
    copies = [pltpu.make_async_copy(we_hbm.at[a], we_ref.at[a], sems.at[a]) for a in range(3)]
    for copy in (*copies, own):
        copy.start()
    for a in range(3):
        copies[a].wait()
        for n in range(9):
            b, c = divmod(n, 3)
            wcat_ref[pl.ds(n * 128, 128), pl.ds(a * 128, 128)] = we_ref[a, b, c]
    own.wait()


def early_kernel(*refs, nk, dims):
    gx, gy, gz, lx, ly, lz, bx, by = dims
    blocks, refs = refs[:nk], refs[nk:]
    wcat_ref, half_ref, slope_ref, send_ref, edge_ref = refs[:5]
    vol_ref, col_ref, p_ref, pre_ref, h_ref, row_ref = refs[5:]
    k, j = lax.axis_index("space"), lax.axis_index("chan")
    brows, hl, line = by * gz, by // 2 * lz, gx * gz
    vol_ref[:, pl.ds(0, 16), :] = jnp.zeros((gx, 16, 128), F32)
    vol_ref[:, pl.ds(16 + brows, 16), :] = jnp.zeros((gx, 16, 128), F32)
    for n, dk in enumerate([0, *steps_of(nk)]):
        src = blocks[n]
        kk = partner(k, dk, nk)
        for q in range(bx):
            got = src[pl.ds(q * brows, brows), :]
            vol_ref[kk * bx + q, pl.ds(16, brows), :] = got.astype(F32)
            half_ref[pl.ds(pl.multiple_of((kk * bx + q) * brows, brows), brows), :] = got

    cell = depth_of(brows, gz)
    for x in range(gx):
        for n, step in enumerate(STEPS):
            col_ref[pl.ds(x * brows, brows), pl.ds(n * 128, 128)] = shifted(
                vol_ref, (x,), 16, brows, cell, gz, step
            ).astype(BF)

    p_ref[...] = jnp.dot(col_ref[...], wcat_ref[...], preferred_element_type=F32)

    outer = pl.multiple_of((brows - gz) * (1 - j), gz)
    inner = pl.multiple_of((brows - 2 * gz) * (1 - j) + gz * j, gz)
    for x in range(gx):
        row_ref[pl.ds(x * gz, gz), :] = vol_ref[x, pl.ds(16 + outer, gz), :]
    row = row_ref[...]
    rcell = depth_of(line, gz)
    trio = [
        jnp.where(rcell == 0, 0.0, pltpu.roll(row, 1, 0)),
        row,
        jnp.where(rcell == gz - 1, 0.0, pltpu.roll(row, line - 1, 0)),
    ]
    taps = wcat_ref[pl.ds(pl.multiple_of(j * (6 * 128), 128), 3 * 128), :]
    given = jnp.dot(jnp.concatenate(trio, axis=1).astype(BF), taps, preferred_element_type=F32)
    given = fold([given[:, a * 128 : (a + 1) * 128] for a in range(3)], gz)

    for lq in range(lx):
        pair = None
        for x in (2 * lq, 2 * lq + 1):
            pre = p_ref[pl.ds(x * brows, brows), pl.ds(128, 128)]
            if x > 0:
                pre = pre + p_ref[pl.ds((x - 1) * brows, brows), pl.ds(0, 128)]
            if x < gx - 1:
                pre = pre + p_ref[pl.ds((x + 1) * brows, brows), pl.ds(256, 128)]
            pre_ref[x] = pre
            h, slope = gelu_and_slope(pre)
            slope_ref[pl.ds(x * brows, brows), :] = slope
            pair = h if pair is None else pair + h
        wide = pair.reshape(by // 2, 2, gz, 128)
        h_ref[...] = (wide[:, 0] + wide[:, 1]).reshape(by // 2 * gz, 128)
        pooled = (h_ref[pl.ds(0, hl, stride=2), :] + h_ref[pl.ds(1, hl, stride=2), :]) * 0.125
        send_ref[pl.ds(lq * hl, hl), :] = pooled.astype(BF)
    for x in range(gx):
        edge_ref[pl.ds(x * gz, gz), :] = pre_ref[x, pl.ds(inner, gz), :]
        edge_ref[pl.ds(line + x * gz, gz), :] = pre_ref[x, pl.ds(outer, gz), :]
    edge_ref[pl.ds(2 * line, line), :] = given
    send_ref[pl.ds(lx * hl, 3 * line), :] = edge_ref[...].astype(BF)


def fetch_kernel(far_ref, we_ref, near_ref, back_ref, wt_ref, sems):
    copies = [pltpu.make_async_copy(far_ref.at[a], near_ref.at[a], sems.at[a]) for a in range(3)]
    cl = near_ref.shape[-1]
    for copy in copies:
        copy.start()
    for n in range(9):
        b, c = divmod(n, 3)
        for a in range(3):
            wt_ref[a, pl.ds(n * 128, 128), :] = we_ref[a, b, c].astype(F32).T.astype(BF)
    for a in range(3):
        copies[a].wait()
        for n in range(9):
            b, c = divmod(n, 3)
            back_ref[pl.ds(n * cl, cl), pl.ds(a * 128, 128)] = near_ref[a, b, c].astype(F32).T.astype(BF)


def border_pool(inner, outer, tmp_ref, tile_ref, dims):
    lx, lz, gz = dims
    h, slope = gelu_and_slope(outer)
    h = (h + gelu_and_slope(inner)[0]).reshape(lx, 2, gz, 128)
    tmp_ref[...] = (h[:, 0] + h[:, 1]).reshape(lx * gz, 128)
    got = (tmp_ref[pl.ds(0, lx * lz, stride=2), :] + tmp_ref[pl.ds(1, lx * lz, stride=2), :]) * 0.125
    got = got.astype(BF).astype(F32)
    for x in range(lx):
        for copy in range(2):
            tile_ref[pl.ds((2 * x + copy) * lz, lz), :] = got[x * lz : (x + 1) * lz]
    return slope


def late_kernel(
    sent_ref, got_ref, edge_ref, wl_ref, pooled_ref, slope_ref, patch_ref,
    pool_ref, lcol_ref, tmp_ref, tile_ref, *, dims
):
    gx, gz, lx, ly, lz = dims
    lplane, hl, line = ly * lz, ly // 2 * lz, gx * gz
    cl = wl_ref.shape[-1]
    j = lax.axis_index("chan")
    edges = got_ref[pl.ds(lx * hl, 3 * line), :].astype(F32)
    lrow = lax.broadcasted_iota(jnp.int32, (hl, 128), 0)
    for x in range(lx):
        pool_ref[x, pl.ds(0, 8), :] = jnp.zeros((8, 128), F32)
        pool_ref[x, pl.ds(8 + lplane, 8), :] = jnp.zeros((8, 128), F32)
    sides = (
        (j, sent_ref, edge_ref[pl.ds(0, line), :], edge_ref[pl.ds(line, line), :] + edges[2 * line :]),
        (1 - j, got_ref, edges[:line], edges[line : 2 * line] + edge_ref[pl.ds(2 * line, line), :]),
    )
    for n, (side, ref, inner, outer) in enumerate(sides):
        slope = border_pool(inner, outer, tmp_ref, tile_ref, (lx, lz, gz))
        if n == 0:
            patch_ref[...] = slope
        first = (hl - lz) * (1 - side)
        border = (lrow >= first) & (lrow < first + lz)
        for x in range(lx):
            tiles = jnp.concatenate([tile_ref[pl.ds(x * 2 * lz, 2 * lz), :]] * (hl // (2 * lz)), axis=0)
            start = pl.multiple_of(8 + side * hl, 8)
            pool_ref[x, pl.ds(start, hl), :] = jnp.where(
                border, tiles, ref[pl.ds(x * hl, hl), :].astype(F32)
            )
    for x in range(lx):
        pooled_ref[pl.ds(x * lplane, lplane), :] = pool_ref[x, pl.ds(8, lplane), :].astype(BF)

    lcell = depth_of(lplane, lz)
    for x in range(lx):
        for n, step in enumerate(STEPS):
            lcol_ref[pl.ds(x * lplane, lplane), pl.ds(n * 128, 128)] = shifted(
                pool_ref, (x,), 8, lplane, lcell, lz, step
            ).astype(BF)
    lcol = lcol_ref[...]
    parts = [
        jnp.dot(lcol, wl_ref[a].reshape(9 * 128, cl), preferred_element_type=F32) for a in range(3)
    ]
    pre = fold(parts, lplane)
    slope_ref[...] = gelu_and_slope(pre)[1]


def late_back_kernel(*refs, nk, dims):
    lx, ly, lz, cx = dims
    cots, refs = refs[:nk], refs[nk:]
    pooled_ref, slope_ref, wback_ref, pd_ref, back_ref, mine_ref, dl_ref, dcol_ref, cot_ref = refs
    lplane = ly * lz
    cl = slope_ref.shape[1]
    crow = cx * lplane
    k = lax.axis_index("space")
    for n, dk in enumerate([0, *steps_of(nk)]):
        start = pl.multiple_of(partner(k, dk, nk) * crow, 8)
        cot_ref[pl.ds(start, crow), :] = cots[n][...].astype(F32).reshape(crow, cl)
    pd_ref[:, pl.ds(0, 128)] = pooled_ref[...]
    pd_ref[:, pl.ds(128, cl)] = (cot_ref[...] * slope_ref[...]).astype(BF)
    lcell = depth_of(lplane, lz)
    for x in range(lx):
        dl_ref[x, pl.ds(0, 8), :] = jnp.zeros((8, cl), F32)
        dl_ref[x, pl.ds(8 + lplane, 8), :] = jnp.zeros((8, cl), F32)
        dl_ref[x, pl.ds(8, lplane), :] = pd_ref[pl.ds(x * lplane, lplane), pl.ds(128, cl)].astype(F32)
    for n, (b, c) in enumerate(STEPS):
        for x in range(lx):
            dcol_ref[pl.ds(x * lplane, lplane), pl.ds(n * cl, cl)] = shifted(
                dl_ref, (x,), 8, lplane, lcell, lz, (-b, -c)
            ).astype(BF)
    total = jnp.dot(dcol_ref[...], wback_ref[...], preferred_element_type=F32)
    back = fold([total[:, (2 - a) * 128 : (3 - a) * 128] for a in range(3)], lplane)
    back_ref[...] = back.astype(BF)
    mine_ref[...] = back


def late_grad_kernel(mine_ref, other_ref, out_ref, pool_ref, lcol_ref, wide_ref, *, dims, scale):
    lx, ly, lz = dims
    lplane = ly * lz
    rows = lx * lplane
    cl = mine_ref.shape[1] - 128
    lcell = depth_of(lplane, lz)
    for x in range(lx):
        pool_ref[x, pl.ds(0, 8), :] = jnp.zeros((8, 128), F32)
        pool_ref[x, pl.ds(8 + lplane, 8), :] = jnp.zeros((8, 128), F32)
    for s, ref in enumerate((mine_ref, other_ref)):
        for x in range(lx):
            pool_ref[x, pl.ds(8, lplane), :] = ref[pl.ds(x * lplane, lplane), pl.ds(0, 128)].astype(F32)
        for x in range(lx):
            for n, step in enumerate(STEPS):
                lcol_ref[pl.ds(s * rows + x * lplane, lplane), pl.ds(n * 128, 128)] = shifted(
                    pool_ref, (x,), 8, lplane, lcell, lz, step
                ).astype(BF)
        zero = jnp.zeros((lplane, cl), BF)
        wide_ref[pl.ds(s * rows + rows - lplane, lplane), pl.ds(0, cl)] = zero
        wide_ref[pl.ds(s * rows, rows - lplane), pl.ds(0, cl)] = ref[pl.ds(lplane, rows - lplane), pl.ds(128, cl)]
        wide_ref[pl.ds(s * rows, rows), pl.ds(cl, cl)] = ref[:, pl.ds(128, cl)]
        wide_ref[pl.ds(s * rows, lplane), pl.ds(2 * cl, cl)] = zero
        wide_ref[pl.ds(s * rows + lplane, rows - lplane), pl.ds(2 * cl, cl)] = ref[
            pl.ds(0, rows - lplane), pl.ds(128, cl)
        ]
    got = lax.dot_general(
        lcol_ref[...], wide_ref[...], (((0,), (0,)), ((), ())), preferred_element_type=F32
    )
    for a in range(3):
        out_ref[pl.ds(a * 9 * 128, 9 * 128), :] = (got[:, a * cl : (a + 1) * cl] * scale).astype(BF)


def other_kernel(
    half_ref, got_ref, wcat_ref, col_ref, slope_ref, vol_ref, p_ref, *, dims
):
    gx, gy, gz, lx, ly, lz, bx, by = dims
    brows = by * gz
    j = lax.axis_index("chan")
    vol_ref[:, :, pl.ds(0, 16), :] = jnp.zeros((2, gx, 16, 128), F32)
    vol_ref[:, :, pl.ds(16 + brows, 16), :] = jnp.zeros((2, gx, 16, 128), F32)
    for h, src in enumerate((half_ref, got_ref)):
        for x in range(gx):
            vol_ref[h, x, pl.ds(16, brows), :] = src[pl.ds(x * brows, brows), :].astype(F32)
    for h, side in enumerate((j, 1 - j)):
        into = pl.multiple_of((16 + brows) * (1 - side) + (16 - gz) * side, 8)
        start = pl.multiple_of(16 + (brows - gz) * side, 8)
        for x in range(gx):
            vol_ref[h, x, pl.ds(into, gz), :] = vol_ref[1 - h, x, pl.ds(start, gz), :]
    cell = depth_of(brows, gz)
    for h in (1, 0):
        for x in range(gx):
            for n, step in enumerate(STEPS):
                col_ref[pl.ds((h * gx + x) * brows, brows), pl.ds(n * 128, 128)] = shifted(
                    vol_ref, (h, x), 16, brows, cell, gz, step
                ).astype(BF)
    p_ref[...] = jnp.dot(
        col_ref[pl.ds(gx * brows, gx * brows), :], wcat_ref[...], preferred_element_type=F32
    )
    for x in range(gx):
        pre = p_ref[pl.ds(x * brows, brows), pl.ds(128, 128)]
        if x > 0:
            pre = pre + p_ref[pl.ds((x - 1) * brows, brows), pl.ds(0, 128)]
        if x < gx - 1:
            pre = pre + p_ref[pl.ds((x + 1) * brows, brows), pl.ds(256, 128)]
        slope_ref[pl.ds(x * brows, brows), :] = gelu_and_slope(pre)[1]


def tap_terms(left_ref, col_ref, part_ref, first, count):
    got = jnp.dot(left_ref[...], col_ref[:, pl.ds(first * 128, count * 128)], preferred_element_type=F32)
    for a in range(3):
        for n in range(count):
            part_ref[pl.ds((a * count + n) * 128, 128), :] = got[
                a * 128 : (a + 1) * 128, n * 128 : (n + 1) * 128
            ].T.astype(part_ref.dtype)


def more_kernel(left_ref, col_ref, part_ref):
    tap_terms(left_ref, col_ref, part_ref, EARLY_TAPS, 9 - EARLY_TAPS)


def finish_kernel(one_ref, one_got_ref, two_ref, two_got_ref, out_ref, sum_ref, sems, *, scale):
    copies = []
    for a in range(3):
        at = a * 9 * 128
        for mine_ref, got_ref, count in (
            (one_ref, one_got_ref, EARLY_TAPS), (two_ref, two_got_ref, 9 - EARLY_TAPS)
        ):
            rows = pl.ds(a * count * 128, count * 128)
            total = mine_ref[rows, :].astype(F32) + got_ref[rows, :].astype(F32)
            sum_ref[pl.ds(at, count * 128), :] = (total * scale).astype(BF)
            at += count * 128
        rows = pl.ds(a * 9 * 128, 9 * 128)
        copies.append(pltpu.make_async_copy(sum_ref.at[rows], out_ref.at[rows], sems.at[a]))
        copies[-1].start()
    for copy in copies:
        copy.wait()


def early_grad_kernel(
    mine_ref, other_ref, slope_ref, far_ref, patch_ref, col_ref, late_ref,
    part_ref, win_ref, out_ref, left_ref, wide_ref, d_ref, sem, *, dims
):
    leave = pltpu.make_async_copy(late_ref, out_ref, sem)
    leave.start()
    gx, gy, gz, lx, ly, lz, bx, by = dims
    plane, lplane = gy * gz, ly * lz
    k, j = lax.axis_index("space"), lax.axis_index("chan")
    brows = by * gz
    half = gx * brows
    for q in (0, gx + 1):
        d_ref[q] = jnp.zeros(d_ref.shape[1:], F32)
    d_ref[:, pl.ds(0, 16), :] = jnp.zeros((gx + 2, 16, 128), F32)
    d_ref[:, pl.ds(16 + plane, 16), :] = jnp.zeros((gx + 2, 16, 128), F32)
    for h in (0, 1):
        left_ref[pl.ds(0, 128), pl.ds((h + 1) * half - brows, brows)] = jnp.zeros((128, brows), BF)
        left_ref[pl.ds(2 * 128, 128), pl.ds(h * half, brows)] = jnp.zeros((128, brows), BF)
    back = (mine_ref[...] + other_ref[...].astype(F32)) * 0.125
    wide_ref[pl.ds(0, lx * lplane, stride=2), :] = back
    wide_ref[pl.ds(1, lx * lplane, stride=2), :] = back
    first = (brows - gz) * (1 - j)
    row = lax.broadcasted_iota(jnp.int32, (brows, 128), 0)
    border = (row >= first) & (row < first + gz)
    for lq in range(lx):
        for h, side in enumerate((j, 1 - j)):
            start = pl.multiple_of(lq * ly * gz + side * (by // 2 * gz), 8)
            rows = wide_ref[pl.ds(start, by // 2 * gz), :].reshape(by // 2, 1, gz, 128)
            rows = jnp.broadcast_to(rows, (by // 2, 2, gz, 128)).reshape(brows, 128)
            for x in (2 * lq, 2 * lq + 1):
                slope = (far_ref if h else slope_ref)[pl.ds(x * brows, brows), :]
                if h == 0:
                    tiles = jnp.concatenate([patch_ref[pl.ds(x * gz, gz), :]] * by, axis=0)
                    slope = jnp.where(border, tiles, slope)
                delta = (rows * slope).astype(BF).astype(F32)
                d_ref[x + 1, pl.ds(pl.multiple_of(16 + side * brows, 8), brows), :] = delta
                tile = delta.T.astype(BF)
                for a in range(3):
                    if 0 <= x + a - 1 < gx:
                        left_ref[pl.ds(a * 128, 128), pl.ds(h * half + (x + a - 1) * brows, brows)] = tile
    tap_terms(left_ref, col_ref, part_ref, 0, EARLY_TAPS)
    row = pl.multiple_of(j * brows, 8)
    for q in range(bx + 2):
        win_ref[q] = d_ref[k * bx + q, pl.ds(row, brows + 32), :]
    leave.wait()


def grad_volume_kernel(win_ref, wt_ref, gv_ref, vcol_ref, *, bx, brows, gz):
    cell = depth_of(brows, gz)
    for q in range(bx + 2):
        for n, (b, c) in enumerate(STEPS):
            vcol_ref[pl.ds(q * brows, brows), pl.ds(n * 128, 128)] = shifted(
                win_ref, (q,), 16, brows, cell, gz, (-b, -c)
            ).astype(BF)
    total = None
    for a in range(3):
        term = jnp.dot(vcol_ref[pl.ds((2 - a) * brows, bx * brows), :], wt_ref[a], preferred_element_type=F32)
        total = term if total is None else total + term
    gv_ref[...] = total.astype(BF)


def steps_of(count):
    return range(1, count)


def partner(index, by, count):
    if count & (count - 1) == 0:
        return index ^ by
    return lax.rem(index + count - by, count)


def turned(value, axis, by):
    count = lax.axis_size(axis)
    pairs = count & (count - 1) == 0
    return lax.ppermute(value, axis, [(i, i ^ by if pairs else (i + by) % count) for i in range(count)])


def call(kernel, outs, scratch, args, name, far=(), raw=(), away=()):
    args = [
        pltpu.with_memory_space_constraint(arg, pltpu.HBM if n in raw else pltpu.VMEM)
        for n, arg in enumerate(args)
    ]
    outs = [out if n in (*far, *away) else pltpu.VMEM(out.shape, out.dtype) for n, out in enumerate(outs)]
    return pl.pallas_call(
        kernel,
        out_shape=outs,
        in_specs=[
            pl.BlockSpec(memory_space=pltpu.HBM if n in raw else pltpu.VMEM) for n in range(len(args))
        ],
        out_specs=[
            pl.BlockSpec(memory_space=pltpu.HBM if n in away else pltpu.VMEM) for n in range(len(outs))
        ],
        scratch_shapes=scratch,
        compiler_params=pltpu.CompilerParams(vmem_limit_bytes=VMEM_BYTES),
        name=name,
    )(*args)


def whole_sample(volume, early_weight, late_weight, cotangent):
    nk, nj, nr = (lax.axis_size(axis) for axis in ("space", "chan", "rep"))
    _, bx, by, gz, _ = volume.shape
    _, cx, ly, lz, cl = cotangent.shape
    gx, gy, lx = bx * nk, by * nj, cx * nk
    plane, lplane, brows = gy * gz, ly * lz, by * gz
    rows, lrows = gx * plane, lx * lplane
    scale = 1.0 / math.sqrt(nr * lrows)
    sds = jax.ShapeDtypeStruct

    mine = volume.reshape(bx * brows, 128)
    line = [mine] + [turned(mine, "space", dk) for dk in steps_of(nk)]
    cot = cotangent.reshape(cx * ly, lz, cl)
    own, we, wcat = call(
        begin_kernel,
        [sds(mine.shape, BF), sds(early_weight.shape, BF), sds((9 * 128, 3 * 128), BF)],
        [pltpu.SemaphoreType.DMA((4,))],
        [mine, early_weight],
        "begin",
        raw=(0, 1),
    )
    line[0] = own
    late_steps = [dk for dk in range(1, nk) if nk & (nk - 1) == 0 and dk & (dk - 1)]
    cots = {dk: turned(cot, "space", dk) for dk in steps_of(nk) if dk not in late_steps}

    dims = (gx, gy, gz, lx, ly, lz, bx, by)
    hrows, edge = gx * brows, 3 * gx * gz
    half, slope, send, edges = call(
        functools.partial(early_kernel, nk=nk, dims=dims),
        [
            sds((hrows, 128), BF),
            sds((hrows, 128), F32),
            sds((lrows // 2 + edge, 128), BF),
            sds((edge, 128), F32),
        ],
        [
            pltpu.VMEM((gx, brows + 32, 128), F32),
            pltpu.VMEM((hrows, 9 * 128), BF),
            pltpu.VMEM((hrows, 3 * 128), F32),
            pltpu.VMEM((gx, brows, 128), F32),
            pltpu.VMEM((by // 2 * gz, 128), F32),
            pltpu.VMEM((gx * gz, 128), F32),
        ],
        line + [wcat],
        "early",
    )
    ready, cots = lax.optimization_barrier((send, cots))
    send_other = turned(ready, "chan", 1)
    half_other = turned(half, "chan", 1)
    for dk in late_steps:
        low = dk & -dk
        cots[dk] = turned(cots[dk ^ low], "space", low)
    cots = [cot] + [cots[dk] for dk in steps_of(nk)]
    held, _ = lax.optimization_barrier((late_weight, send))
    wl, wback, wt = call(
        fetch_kernel,
        [sds(late_weight.shape, BF), sds((9 * cl, 3 * 128), BF), sds((3, 9 * 128, 128), BF)],
        [pltpu.SemaphoreType.DMA((3,))],
        [held, we],
        "fetch",
        raw=(0,),
    )
    pooled, late_slope, patch = call(
        functools.partial(late_kernel, dims=(gx, gz, lx, ly, lz)),
        [sds((lrows, 128), BF), sds((lrows, cl), F32), sds((gx * gz, 128), F32)],
        [
            pltpu.VMEM((lx, lplane + 16, 128), F32),
            pltpu.VMEM((lrows, 9 * 128), BF),
            pltpu.VMEM((lx * gz, 128), F32),
            pltpu.VMEM((lx * 2 * lz, 128), F32),
        ],
        [send, send_other, edges, wl],
        "late",
    )
    pooled_delta, back, back_mine = call(
        functools.partial(late_back_kernel, nk=nk, dims=(lx, ly, lz, cx)),
        [sds((lrows, 128 + cl), BF), sds((lrows, 128), BF), sds((lrows, 128), F32)],
        [
            pltpu.VMEM((lx, lplane + 16, cl), F32),
            pltpu.VMEM((lrows, 9 * cl), BF),
            pltpu.VMEM((lrows, cl), F32),
        ],
        cots + [pooled, late_slope, wback],
        "late_back",
    )
    pd_other = turned(pooled_delta, "rep", 1)
    back_other = turned(back, "chan", 1)
    (late,) = call(
        functools.partial(late_grad_kernel, dims=(lx, ly, lz), scale=scale),
        [sds((27 * 128, cl), BF)],
        [
            pltpu.VMEM((lx, lplane + 16, 128), F32),
            pltpu.VMEM((2 * lrows, 9 * 128), BF),
            pltpu.VMEM((2 * lrows, 3 * cl), BF),
        ],
        [pooled_delta, pd_other],
        "late_grad",
    )
    half_other, wcat, _, late = lax.optimization_barrier((half_other, wcat, back, late))
    col, far_slope = call(
        functools.partial(other_kernel, dims=dims),
        [sds((rows, 9 * 128), BF), sds((hrows, 128), F32)],
        [pltpu.VMEM((2, gx, brows + 32, 128), F32), pltpu.VMEM((hrows, 3 * 128), F32)],
        [half, half_other, wcat],
        "other",
    )
    back_mine, late = lax.optimization_barrier((back_mine, late))
    part, win, late, left = call(
        functools.partial(early_grad_kernel, dims=dims),
        [
            sds((3 * EARLY_TAPS * 128, 128), BF),
            sds((bx + 2, brows + 32, 128), F32),
            sds(late.shape, BF),
            sds((3 * 128, rows), BF),
        ],
        [
            pltpu.VMEM((lx * ly * gz, 128), F32),
            pltpu.VMEM((gx + 2, plane + 32, 128), F32),
            pltpu.SemaphoreType.DMA(()),
        ],
        [back_mine, back_other, slope, far_slope, patch, col, late],
        "early_grad",
        away=(2,),
    )
    part_other = turned(part, "rep", 1)
    (more,) = call(more_kernel, [sds((3 * (9 - EARLY_TAPS) * 128, 128), BF)], [], [left, col], "more")
    more_other = turned(more, "rep", 1)
    win, _ = lax.optimization_barrier((win, more))
    (gv,) = call(
        functools.partial(grad_volume_kernel, bx=bx, brows=brows, gz=gz),
        [sds((bx * brows, 128), BF)],
        [pltpu.VMEM(((bx + 2) * brows, 9 * 128), BF)],
        [win, wt],
        "grad_volume",
        far=(0,),
    )
    (early,) = call(
        functools.partial(finish_kernel, scale=scale),
        [sds((27 * 128, 128), BF)],
        [pltpu.VMEM((27 * 128, 128), BF), pltpu.SemaphoreType.DMA((3,))],
        [part, part_other, more, more_other],
        "finish",
        away=(0,),
    )
    return (
        early.reshape(3, 3, 3, 128, 128),
        late.reshape(3, 3, 3, 128, cl),
        gv.reshape(1, bx, by, gz, 128),
    )


def solution(mesh):
    few = mesh.shape["space"] * mesh.shape["chan"] <= GATHER_BLOCKS
    alone = mesh.shape["rep"] == 2 and mesh.shape["chan"] == 2
    return jax.shard_map(
        whole_sample if few and alone else per_device,
        mesh=mesh,
        in_specs=(
            P(("groups", "rep"), "space", "chan", None, None),
            P(),
            P(None, None, None, None, "chan"),
            P(("groups", "rep"), "space", None, None, "chan"),
        ),
        out_specs=(
            P("groups", None, None, None, None),
            P("groups", None, None, None, "chan"),
            P(("groups", "rep"), "space", "chan", None, None),
        ),
        check_vma=False,
    )
```

```python
import functools
import math

import jax
import jax.numpy as jnp
from jax import lax
from jax.experimental import pallas as pl
from jax.experimental.pallas import tpu as pltpu
from jax.sharding import PartitionSpec as P

BF = jnp.bfloat16
F32 = jnp.float32
VMEM_BYTES = 14 * 2**20
GATHER_BLOCKS = 8
EARLY_TAPS = 6


def padded_2(block, sides, width):
    for axis, dim in sides:
        count = lax.axis_size(axis)
        forward = [(i, i + 1) for i in range(count - 1)]
        backward = [(target, source) for source, target in forward]
        low = lax.ppermute(
            lax.slice_in_dim(block, block.shape[dim] - width, None, axis=dim), axis, forward
        )
        high = lax.ppermute(lax.slice_in_dim(block, 0, width, axis=dim), axis, backward)
        block = jnp.concatenate([low, block, high], axis=dim)
    return block


def gelu_tanh(value):
    return jax.nn.gelu(value, approximate=True)


def conv_padded(padded, weight):
    depth = padded.shape[1] - 2
    height = padded.shape[2] - 2
    length = padded.shape[3] - 2
    total = None
    for first in range(3):
        for second in range(3):
            for third in range(3):
                window = padded[
                    :, first : first + depth, second : second + height, third : third + length
                ]
                term = jnp.einsum(
                    "sxyzc,co->sxyzo",
                    window,
                    weight[first, second, third],
                    preferred_element_type=jnp.float32,
                )
                total = term if total is None else total + term
    return total


def kernel_grad(padded, delta):
    depth = delta.shape[1]
    height = delta.shape[2]
    length = delta.shape[3]
    planes = []
    for first in range(3):
        for second in range(3):
            for third in range(3):
                window = padded[
                    :, first : first + depth, second : second + height, third : third + length
                ]
                planes.append(
                    jnp.einsum("sxyzc,sxyzo->co", window, delta, preferred_element_type=jnp.float32)
                )
    stacked = jnp.stack(planes, axis=0)
    return stacked.reshape((3, 3, 3) + stacked.shape[1:])


def flipped(weight):
    return jnp.swapaxes(weight[::-1, ::-1, ::-1], 3, 4)


def pad_dims(field, dims):
    widths = [(1, 1) if place in dims else (0, 0) for place in range(field.ndim)]
    return jnp.pad(field, widths)


def pool_cells(field):
    s, x, y, z, c = field.shape
    return jnp.mean(field.reshape(s, x // 2, 2, y // 2, 2, z // 2, 2, c), axis=(2, 4, 6))


def spread_cells(field):
    s, x, y, z, c = field.shape
    wide = jnp.broadcast_to(field[:, :, None, :, None, :, None, :], (s, x, 2, y, 2, z, 2, c))
    return wide.reshape(s, 2 * x, 2 * y, 2 * z, c) * 0.125


def late_layer(joined, late_weight, cotangent):
    rim = padded_2(joined, (("space", 1),), 1)
    late_pad = pad_dims(rim, (2, 3))
    pre_late = conv_padded(late_pad, late_weight)
    delta_late = jax.vjp(gelu_tanh, pre_late)[1](cotangent.astype(jnp.float32))[0].astype(
        jnp.bfloat16
    )
    late_part = kernel_grad(late_pad, delta_late)
    delta_rim = padded_2(delta_late, (("space", 1),), 1)
    back_partial = conv_padded(pad_dims(delta_rim, (2, 3)), flipped(late_weight))
    return (back_partial, late_part)


def per_device(volume, early_weight, late_weight, cotangent):
    count = (
        cotangent.shape[0]
        * lax.axis_size("rep")
        * cotangent.shape[1]
        * lax.axis_size("space")
        * cotangent.shape[2]
        * cotangent.shape[3]
    )
    scale = 1.0 / math.sqrt(count)
    haloed = padded_2(volume, (("space", 1), ("chan", 2)), 1)
    padded_in = pad_dims(haloed, (3,))
    pre_early = conv_padded(padded_in, early_weight)
    pooled = pool_cells(gelu_tanh(pre_early)).astype(jnp.bfloat16)
    joined = lax.all_gather(pooled, "chan", axis=2, tiled=True)
    back_partial, late_part = late_layer(joined, late_weight, cotangent)
    back_rows = lax.psum_scatter(back_partial, "chan", scatter_dimension=2, tiled=True)
    delta_early = jax.vjp(gelu_tanh, pre_early)[1](spread_cells(back_rows))[0].astype(jnp.bfloat16)
    early_part = kernel_grad(padded_in, delta_early)
    delta_halo = padded_2(delta_early, (("space", 1), ("chan", 2)), 1)
    grad_volume = conv_padded(pad_dims(delta_halo, (3,)), flipped(early_weight)).astype(
        jnp.bfloat16
    )
    early_total = lax.psum(early_part, ("space", "chan", "rep"))
    grad_early = (early_total * scale).astype(jnp.bfloat16)
    late_total = lax.psum(late_part, ("space", "rep"))
    grad_late = (late_total * scale).astype(jnp.bfloat16)
    return (grad_early, grad_late, grad_volume)


NT = (((1,), (1,)), ((), ()))


def gelu_and_slope(v):
    k = 0.7978845608028654
    sq = v * v
    t = jnp.tanh(k * (v + 0.044715 * (v * sq)))
    half = 0.5 * (1.0 + t)
    return v * half, half + 0.5 * v * (1.0 - t * t) * (k * (1.0 + 0.134145 * sq))


def depth_of(rows, period):
    return lax.broadcasted_iota(jnp.int32, (rows, 128), 0) % period


def shifted(ref, lead, start, rows, cell, period, step):
    dy, dz = step
    got = ref[lead + (pl.ds(start + dy * period + dz, rows), slice(None))]
    if dz == 0:
        return got
    lanes = got.shape[1] // 128
    edge = (cell == 0) if dz < 0 else (cell == period - 1)
    edge = jnp.concatenate([edge] * lanes, axis=1) if lanes > 1 else edge
    return jnp.where(edge, 0.0, got)


STEPS = [(b, c) for b in (-1, 0, 1) for c in (-1, 0, 1)]


def fold(parts, rows):
    zero = jnp.zeros((rows, parts[0].shape[1]), F32)
    return (
        parts[1]
        + jnp.concatenate([zero, parts[0][:-rows]], axis=0)
        + jnp.concatenate([parts[2][rows:], zero], axis=0)
    )


def begin_kernel(own_hbm, we_hbm, own_ref, we_ref, wcat_ref, sems):
    own = pltpu.make_async_copy(own_hbm, own_ref, sems.at[3])
    copies = [pltpu.make_async_copy(we_hbm.at[a], we_ref.at[a], sems.at[a]) for a in range(3)]
    for copy in (*copies, own):
        copy.start()
    for a in range(3):
        copies[a].wait()
        for n in range(9):
            b, c = divmod(n, 3)
            wcat_ref[pl.ds(n * 128, 128), pl.ds(a * 128, 128)] = we_ref[a, b, c]
    own.wait()


def early_kernel(*refs, nk, dims):
    gx, gy, gz, lx, ly, lz, bx, by = dims
    blocks, refs = refs[:nk], refs[nk:]
    wcat_ref, half_ref, slope_ref, send_ref, edge_ref = refs[:5]
    vol_ref, col_ref, p_ref, pre_ref, h_ref, row_ref = refs[5:]
    k, j = lax.axis_index("space"), lax.axis_index("chan")
    brows, hl, line = by * gz, by // 2 * lz, gx * gz
    vol_ref[:, pl.ds(0, 16), :] = jnp.zeros((gx, 16, 128), F32)
    vol_ref[:, pl.ds(16 + brows, 16), :] = jnp.zeros((gx, 16, 128), F32)
    for n, dk in enumerate([0, *steps_of(nk)]):
        src = blocks[n]
        kk = partner(k, dk, nk)
        for q in range(bx):
            got = src[pl.ds(q * brows, brows), :]
            vol_ref[kk * bx + q, pl.ds(16, brows), :] = got.astype(F32)
            half_ref[pl.ds(pl.multiple_of((kk * bx + q) * brows, brows), brows), :] = got

    cell = depth_of(brows, gz)
    for x in range(gx):
        for n, step in enumerate(STEPS):
            col_ref[pl.ds(x * brows, brows), pl.ds(n * 128, 128)] = shifted(
                vol_ref, (x,), 16, brows, cell, gz, step
            ).astype(BF)

    p_ref[...] = jnp.dot(col_ref[...], wcat_ref[...], preferred_element_type=F32)

    outer = pl.multiple_of((brows - gz) * (1 - j), gz)
    inner = pl.multiple_of((brows - 2 * gz) * (1 - j) + gz * j, gz)
    for x in range(gx):
        row_ref[pl.ds(x * gz, gz), :] = vol_ref[x, pl.ds(16 + outer, gz), :]
    row = row_ref[...]
    rcell = depth_of(line, gz)
    trio = [
        jnp.where(rcell == 0, 0.0, pltpu.roll(row, 1, 0)),
        row,
        jnp.where(rcell == gz - 1, 0.0, pltpu.roll(row, line - 1, 0)),
    ]
    taps = wcat_ref[pl.ds(pl.multiple_of(j * (6 * 128), 128), 3 * 128), :]
    given = jnp.dot(jnp.concatenate(trio, axis=1).astype(BF), taps, preferred_element_type=F32)
    given = fold([given[:, a * 128 : (a + 1) * 128] for a in range(3)], gz)

    for lq in range(lx):
        pair = None
        for x in (2 * lq, 2 * lq + 1):
            pre = p_ref[pl.ds(x * brows, brows), pl.ds(128, 128)]
            if x > 0:
                pre = pre + p_ref[pl.ds((x - 1) * brows, brows), pl.ds(0, 128)]
            if x < gx - 1:
                pre = pre + p_ref[pl.ds((x + 1) * brows, brows), pl.ds(256, 128)]
            pre_ref[x] = pre
            h, slope = gelu_and_slope(pre)
            slope_ref[pl.ds(x * brows, brows), :] = slope
            pair = h if pair is None else pair + h
        wide = pair.reshape(by // 2, 2, gz, 128)
        h_ref[...] = (wide[:, 0] + wide[:, 1]).reshape(by // 2 * gz, 128)
        pooled = (h_ref[pl.ds(0, hl, stride=2), :] + h_ref[pl.ds(1, hl, stride=2), :]) * 0.125
        send_ref[pl.ds(lq * hl, hl), :] = pooled.astype(BF)
    for x in range(gx):
        edge_ref[pl.ds(x * gz, gz), :] = pre_ref[x, pl.ds(inner, gz), :]
        edge_ref[pl.ds(line + x * gz, gz), :] = pre_ref[x, pl.ds(outer, gz), :]
    edge_ref[pl.ds(2 * line, line), :] = given
    send_ref[pl.ds(lx * hl, 3 * line), :] = edge_ref[...].astype(BF)


def fetch_kernel(far_ref, we_ref, near_ref, back_ref, wt_ref, sems):
    copies = [pltpu.make_async_copy(far_ref.at[a], near_ref.at[a], sems.at[a]) for a in range(3)]
    cl = near_ref.shape[-1]
    for copy in copies:
        copy.start()
    for n in range(9):
        b, c = divmod(n, 3)
        for a in range(3):
            wt_ref[a, pl.ds(n * 128, 128), :] = we_ref[a, b, c].astype(F32).T.astype(BF)
    for a in range(3):
        copies[a].wait()
        for n in range(9):
            b, c = divmod(n, 3)
            back_ref[pl.ds(n * cl, cl), pl.ds(a * 128, 128)] = near_ref[a, b, c].astype(F32).T.astype(BF)


def border_pool(inner, outer, tmp_ref, tile_ref, dims):
    lx, lz, gz = dims
    h, slope = gelu_and_slope(outer)
    h = (h + gelu_and_slope(inner)[0]).reshape(lx, 2, gz, 128)
    tmp_ref[...] = (h[:, 0] + h[:, 1]).reshape(lx * gz, 128)
    got = (tmp_ref[pl.ds(0, lx * lz, stride=2), :] + tmp_ref[pl.ds(1, lx * lz, stride=2), :]) * 0.125
    got = got.astype(BF).astype(F32)
    for x in range(lx):
        for copy in range(2):
            tile_ref[pl.ds((2 * x + copy) * lz, lz), :] = got[x * lz : (x + 1) * lz]
    return slope


def late_kernel(
    sent_ref, got_ref, edge_ref, wl_ref, pooled_ref, slope_ref, patch_ref,
    pool_ref, lcol_ref, tmp_ref, tile_ref, *, dims
):
    gx, gz, lx, ly, lz = dims
    lplane, hl, line = ly * lz, ly // 2 * lz, gx * gz
    cl = wl_ref.shape[-1]
    j = lax.axis_index("chan")
    edges = got_ref[pl.ds(lx * hl, 3 * line), :].astype(F32)
    lrow = lax.broadcasted_iota(jnp.int32, (hl, 128), 0)
    for x in range(lx):
        pool_ref[x, pl.ds(0, 8), :] = jnp.zeros((8, 128), F32)
        pool_ref[x, pl.ds(8 + lplane, 8), :] = jnp.zeros((8, 128), F32)
    sides = (
        (j, sent_ref, edge_ref[pl.ds(0, line), :], edge_ref[pl.ds(line, line), :] + edges[2 * line :]),
        (1 - j, got_ref, edges[:line], edges[line : 2 * line] + edge_ref[pl.ds(2 * line, line), :]),
    )
    for n, (side, ref, inner, outer) in enumerate(sides):
        slope = border_pool(inner, outer, tmp_ref, tile_ref, (lx, lz, gz))
        if n == 0:
            patch_ref[...] = slope
        first = (hl - lz) * (1 - side)
        border = (lrow >= first) & (lrow < first + lz)
        for x in range(lx):
            tiles = jnp.concatenate([tile_ref[pl.ds(x * 2 * lz, 2 * lz), :]] * (hl // (2 * lz)), axis=0)
            start = pl.multiple_of(8 + side * hl, 8)
            pool_ref[x, pl.ds(start, hl), :] = jnp.where(
                border, tiles, ref[pl.ds(x * hl, hl), :].astype(F32)
            )
    for x in range(lx):
        pooled_ref[pl.ds(x * lplane, lplane), :] = pool_ref[x, pl.ds(8, lplane), :].astype(BF)

    lcell = depth_of(lplane, lz)
    for x in range(lx):
        for n, step in enumerate(STEPS):
            lcol_ref[pl.ds(x * lplane, lplane), pl.ds(n * 128, 128)] = shifted(
                pool_ref, (x,), 8, lplane, lcell, lz, step
            ).astype(BF)
    lcol = lcol_ref[...]
    parts = [
        jnp.dot(lcol, wl_ref[a].reshape(9 * 128, cl), preferred_element_type=F32) for a in range(3)
    ]
    pre = fold(parts, lplane)
    slope_ref[...] = gelu_and_slope(pre)[1]


def late_back_kernel(*refs, nk, dims):
    lx, ly, lz, cx = dims
    cots, refs = refs[:nk], refs[nk:]
    pooled_ref, slope_ref, wback_ref, pd_ref, back_ref, mine_ref, dl_ref, dcol_ref, cot_ref = refs
    lplane = ly * lz
    cl = slope_ref.shape[1]
    crow = cx * lplane
    k = lax.axis_index("space")
    for n, dk in enumerate([0, *steps_of(nk)]):
        start = pl.multiple_of(partner(k, dk, nk) * crow, 8)
        cot_ref[pl.ds(start, crow), :] = cots[n][...].astype(F32).reshape(crow, cl)
    pd_ref[:, pl.ds(0, 128)] = pooled_ref[...]
    pd_ref[:, pl.ds(128, cl)] = (cot_ref[...] * slope_ref[...]).astype(BF)
    lcell = depth_of(lplane, lz)
    for x in range(lx):
        dl_ref[x, pl.ds(0, 8), :] = jnp.zeros((8, cl), F32)
        dl_ref[x, pl.ds(8 + lplane, 8), :] = jnp.zeros((8, cl), F32)
        dl_ref[x, pl.ds(8, lplane), :] = pd_ref[pl.ds(x * lplane, lplane), pl.ds(128, cl)].astype(F32)
    for n, (b, c) in enumerate(STEPS):
        for x in range(lx):
            dcol_ref[pl.ds(x * lplane, lplane), pl.ds(n * cl, cl)] = shifted(
                dl_ref, (x,), 8, lplane, lcell, lz, (-b, -c)
            ).astype(BF)
    total = jnp.dot(dcol_ref[...], wback_ref[...], preferred_element_type=F32)
    back = fold([total[:, (2 - a) * 128 : (3 - a) * 128] for a in range(3)], lplane)
    back_ref[...] = back.astype(BF)
    mine_ref[...] = back


def late_grad_kernel(mine_ref, other_ref, out_ref, pool_ref, lcol_ref, wide_ref, *, dims, scale):
    lx, ly, lz = dims
    lplane = ly * lz
    rows = lx * lplane
    cl = mine_ref.shape[1] - 128
    lcell = depth_of(lplane, lz)
    for x in range(lx):
        pool_ref[x, pl.ds(0, 8), :] = jnp.zeros((8, 128), F32)
        pool_ref[x, pl.ds(8 + lplane, 8), :] = jnp.zeros((8, 128), F32)
    for s, ref in enumerate((mine_ref, other_ref)):
        for x in range(lx):
            pool_ref[x, pl.ds(8, lplane), :] = ref[pl.ds(x * lplane, lplane), pl.ds(0, 128)].astype(F32)
        for x in range(lx):
            for n, step in enumerate(STEPS):
                lcol_ref[pl.ds(s * rows + x * lplane, lplane), pl.ds(n * 128, 128)] = shifted(
                    pool_ref, (x,), 8, lplane, lcell, lz, step
                ).astype(BF)
        zero = jnp.zeros((lplane, cl), BF)
        wide_ref[pl.ds(s * rows + rows - lplane, lplane), pl.ds(0, cl)] = zero
        wide_ref[pl.ds(s * rows, rows - lplane), pl.ds(0, cl)] = ref[pl.ds(lplane, rows - lplane), pl.ds(128, cl)]
        wide_ref[pl.ds(s * rows, rows), pl.ds(cl, cl)] = ref[:, pl.ds(128, cl)]
        wide_ref[pl.ds(s * rows, lplane), pl.ds(2 * cl, cl)] = zero
        wide_ref[pl.ds(s * rows + lplane, rows - lplane), pl.ds(2 * cl, cl)] = ref[
            pl.ds(0, rows - lplane), pl.ds(128, cl)
        ]
    got = lax.dot_general(
        lcol_ref[...], wide_ref[...], (((0,), (0,)), ((), ())), preferred_element_type=F32
    )
    for a in range(3):
        out_ref[pl.ds(a * 9 * 128, 9 * 128), :] = (got[:, a * cl : (a + 1) * cl] * scale).astype(BF)


def other_kernel(
    half_ref, got_ref, wcat_ref, col_ref, slope_ref, vol_ref, p_ref, *, dims
):
    gx, gy, gz, lx, ly, lz, bx, by = dims
    brows = by * gz
    j = lax.axis_index("chan")
    vol_ref[:, :, pl.ds(0, 16), :] = jnp.zeros((2, gx, 16, 128), F32)
    vol_ref[:, :, pl.ds(16 + brows, 16), :] = jnp.zeros((2, gx, 16, 128), F32)
    for h, src in enumerate((half_ref, got_ref)):
        for x in range(gx):
            vol_ref[h, x, pl.ds(16, brows), :] = src[pl.ds(x * brows, brows), :].astype(F32)
    for h, side in enumerate((j, 1 - j)):
        into = pl.multiple_of((16 + brows) * (1 - side) + (16 - gz) * side, 8)
        start = pl.multiple_of(16 + (brows - gz) * side, 8)
        for x in range(gx):
            vol_ref[h, x, pl.ds(into, gz), :] = vol_ref[1 - h, x, pl.ds(start, gz), :]
    cell = depth_of(brows, gz)
    for h in (1, 0):
        for x in range(gx):
            for n, step in enumerate(STEPS):
                col_ref[pl.ds((h * gx + x) * brows, brows), pl.ds(n * 128, 128)] = shifted(
                    vol_ref, (h, x), 16, brows, cell, gz, step
                ).astype(BF)
    p_ref[...] = jnp.dot(
        col_ref[pl.ds(gx * brows, gx * brows), :], wcat_ref[...], preferred_element_type=F32
    )
    for x in range(gx):
        pre = p_ref[pl.ds(x * brows, brows), pl.ds(128, 128)]
        if x > 0:
            pre = pre + p_ref[pl.ds((x - 1) * brows, brows), pl.ds(0, 128)]
        if x < gx - 1:
            pre = pre + p_ref[pl.ds((x + 1) * brows, brows), pl.ds(256, 128)]
        slope_ref[pl.ds(x * brows, brows), :] = gelu_and_slope(pre)[1]


def tap_terms(left_ref, col_ref, part_ref, first, count):
    got = jnp.dot(left_ref[...], col_ref[:, pl.ds(first * 128, count * 128)], preferred_element_type=F32)
    for a in range(3):
        for n in range(count):
            part_ref[pl.ds((a * count + n) * 128, 128), :] = got[
                a * 128 : (a + 1) * 128, n * 128 : (n + 1) * 128
            ].T.astype(part_ref.dtype)


def more_kernel(left_ref, col_ref, part_ref):
    tap_terms(left_ref, col_ref, part_ref, EARLY_TAPS, 9 - EARLY_TAPS)


def finish_kernel(one_ref, one_got_ref, two_ref, two_got_ref, out_ref, sum_ref, sems, *, scale):
    copies = []
    for a in range(3):
        at = a * 9 * 128
        for mine_ref, got_ref, count in (
            (one_ref, one_got_ref, EARLY_TAPS), (two_ref, two_got_ref, 9 - EARLY_TAPS)
        ):
            rows = pl.ds(a * count * 128, count * 128)
            total = mine_ref[rows, :].astype(F32) + got_ref[rows, :].astype(F32)
            sum_ref[pl.ds(at, count * 128), :] = (total * scale).astype(BF)
            at += count * 128
        rows = pl.ds(a * 9 * 128, 9 * 128)
        copies.append(pltpu.make_async_copy(sum_ref.at[rows], out_ref.at[rows], sems.at[a]))
        copies[-1].start()
    for copy in copies:
        copy.wait()


def early_grad_kernel(
    mine_ref, other_ref, slope_ref, far_ref, patch_ref, col_ref, late_ref,
    part_ref, win_ref, out_ref, left_ref, wide_ref, d_ref, sem, *, dims
):
    leave = pltpu.make_async_copy(late_ref, out_ref, sem)
    leave.start()
    gx, gy, gz, lx, ly, lz, bx, by = dims
    plane, lplane = gy * gz, ly * lz
    k, j = lax.axis_index("space"), lax.axis_index("chan")
    brows = by * gz
    half = gx * brows
    for q in (0, gx + 1):
        d_ref[q] = jnp.zeros(d_ref.shape[1:], F32)
    d_ref[:, pl.ds(0, 16), :] = jnp.zeros((gx + 2, 16, 128), F32)
    d_ref[:, pl.ds(16 + plane, 16), :] = jnp.zeros((gx + 2, 16, 128), F32)
    for h in (0, 1):
        left_ref[pl.ds(0, 128), pl.ds((h + 1) * half - brows, brows)] = jnp.zeros((128, brows), BF)
        left_ref[pl.ds(2 * 128, 128), pl.ds(h * half, brows)] = jnp.zeros((128, brows), BF)
    back = (mine_ref[...] + other_ref[...].astype(F32)) * 0.125
    wide_ref[pl.ds(0, lx * lplane, stride=2), :] = back
    wide_ref[pl.ds(1, lx * lplane, stride=2), :] = back
    first = (brows - gz) * (1 - j)
    row = lax.broadcasted_iota(jnp.int32, (brows, 128), 0)
    border = (row >= first) & (row < first + gz)
    for lq in range(lx):
        for h, side in enumerate((j, 1 - j)):
            start = pl.multiple_of(lq * ly * gz + side * (by // 2 * gz), 8)
            rows = wide_ref[pl.ds(start, by // 2 * gz), :].reshape(by // 2, 1, gz, 128)
            rows = jnp.broadcast_to(rows, (by // 2, 2, gz, 128)).reshape(brows, 128)
            for x in (2 * lq, 2 * lq + 1):
                slope = (far_ref if h else slope_ref)[pl.ds(x * brows, brows), :]
                if h == 0:
                    tiles = jnp.concatenate([patch_ref[pl.ds(x * gz, gz), :]] * by, axis=0)
                    slope = jnp.where(border, tiles, slope)
                delta = (rows * slope).astype(BF).astype(F32)
                d_ref[x + 1, pl.ds(pl.multiple_of(16 + side * brows, 8), brows), :] = delta
                tile = delta.T.astype(BF)
                for a in range(3):
                    if 0 <= x + a - 1 < gx:
                        left_ref[pl.ds(a * 128, 128), pl.ds(h * half + (x + a - 1) * brows, brows)] = tile
    tap_terms(left_ref, col_ref, part_ref, 0, EARLY_TAPS)
    row = pl.multiple_of(j * brows, 8)
    for q in range(bx + 2):
        win_ref[q] = d_ref[k * bx + q, pl.ds(row, brows + 32), :]
    leave.wait()


def grad_volume_kernel(win_ref, wt_ref, gv_ref, vcol_ref, *, bx, brows, gz):
    cell = depth_of(brows, gz)
    for q in range(bx + 2):
        for n, (b, c) in enumerate(STEPS):
            vcol_ref[pl.ds(q * brows, brows), pl.ds(n * 128, 128)] = shifted(
                win_ref, (q,), 16, brows, cell, gz, (-b, -c)
            ).astype(BF)
    total = None
    for a in range(3):
        term = jnp.dot(vcol_ref[pl.ds((2 - a) * brows, bx * brows), :], wt_ref[a], preferred_element_type=F32)
        total = term if total is None else total + term
    gv_ref[...] = total.astype(BF)


def steps_of(count):
    return range(1, count)


def partner(index, by, count):
    if count & (count - 1) == 0:
        return index ^ by
    return lax.rem(index + count - by, count)


def turned(value, axis, by):
    count = lax.axis_size(axis)
    pairs = count & (count - 1) == 0
    return lax.ppermute(value, axis, [(i, i ^ by if pairs else (i + by) % count) for i in range(count)])


def call(kernel, outs, scratch, args, name, far=(), raw=(), away=()):
    args = [
        pltpu.with_memory_space_constraint(arg, pltpu.HBM if n in raw else pltpu.VMEM)
        for n, arg in enumerate(args)
    ]
    outs = [out if n in (*far, *away) else pltpu.VMEM(out.shape, out.dtype) for n, out in enumerate(outs)]
    return pl.pallas_call(
        kernel,
        out_shape=outs,
        in_specs=[
            pl.BlockSpec(memory_space=pltpu.HBM if n in raw else pltpu.VMEM) for n in range(len(args))
        ],
        out_specs=[
            pl.BlockSpec(memory_space=pltpu.HBM if n in away else pltpu.VMEM) for n in range(len(outs))
        ],
        scratch_shapes=scratch,
        compiler_params=pltpu.CompilerParams(vmem_limit_bytes=VMEM_BYTES),
        name=name,
    )(*args)


def whole_sample(volume, early_weight, late_weight, cotangent):
    nk, nj, nr = (lax.axis_size(axis) for axis in ("space", "chan", "rep"))
    _, bx, by, gz, _ = volume.shape
    _, cx, ly, lz, cl = cotangent.shape
    gx, gy, lx = bx * nk, by * nj, cx * nk
    plane, lplane, brows = gy * gz, ly * lz, by * gz
    rows, lrows = gx * plane, lx * lplane
    scale = 1.0 / math.sqrt(nr * lrows)
    sds = jax.ShapeDtypeStruct

    mine = volume.reshape(bx * brows, 128)
    line = [mine] + [turned(mine, "space", dk) for dk in steps_of(nk)]
    cot = cotangent.reshape(cx * ly, lz, cl)
    own, we, wcat = call(
        begin_kernel,
        [sds(mine.shape, BF), sds(early_weight.shape, BF), sds((9 * 128, 3 * 128), BF)],
        [pltpu.SemaphoreType.DMA((4,))],
        [mine, early_weight],
        "begin",
        raw=(0, 1),
    )
    line[0] = own
    late_steps = [dk for dk in range(1, nk) if nk & (nk - 1) == 0 and dk & (dk - 1)]
    cots = {dk: turned(cot, "space", dk) for dk in steps_of(nk) if dk not in late_steps}

    dims = (gx, gy, gz, lx, ly, lz, bx, by)
    hrows, edge = gx * brows, 3 * gx * gz
    half, slope, send, edges = call(
        functools.partial(early_kernel, nk=nk, dims=dims),
        [
            sds((hrows, 128), BF),
            sds((hrows, 128), F32),
            sds((lrows // 2 + edge, 128), BF),
            sds((edge, 128), F32),
        ],
        [
            pltpu.VMEM((gx, brows + 32, 128), F32),
            pltpu.VMEM((hrows, 9 * 128), BF),
            pltpu.VMEM((hrows, 3 * 128), F32),
            pltpu.VMEM((gx, brows, 128), F32),
            pltpu.VMEM((by // 2 * gz, 128), F32),
            pltpu.VMEM((gx * gz, 128), F32),
        ],
        line + [wcat],
        "early",
    )
    ready, cots = lax.optimization_barrier((send, cots))
    send_other = turned(ready, "chan", 1)
    half_other = turned(half, "chan", 1)
    for dk in late_steps:
        low = dk & -dk
        cots[dk] = turned(cots[dk ^ low], "space", low)
    cots = [cot] + [cots[dk] for dk in steps_of(nk)]
    held, _ = lax.optimization_barrier((late_weight, send))
    wl, wback, wt = call(
        fetch_kernel,
        [sds(late_weight.shape, BF), sds((9 * cl, 3 * 128), BF), sds((3, 9 * 128, 128), BF)],
        [pltpu.SemaphoreType.DMA((3,))],
        [held, we],
        "fetch",
        raw=(0,),
    )
    pooled, late_slope, patch = call(
        functools.partial(late_kernel, dims=(gx, gz, lx, ly, lz)),
        [sds((lrows, 128), BF), sds((lrows, cl), F32), sds((gx * gz, 128), F32)],
        [
            pltpu.VMEM((lx, lplane + 16, 128), F32),
            pltpu.VMEM((lrows, 9 * 128), BF),
            pltpu.VMEM((lx * gz, 128), F32),
            pltpu.VMEM((lx * 2 * lz, 128), F32),
        ],
        [send, send_other, edges, wl],
        "late",
    )
    pooled_delta, back, back_mine = call(
        functools.partial(late_back_kernel, nk=nk, dims=(lx, ly, lz, cx)),
        [sds((lrows, 128 + cl), BF), sds((lrows, 128), BF), sds((lrows, 128), F32)],
        [
            pltpu.VMEM((lx, lplane + 16, cl), F32),
            pltpu.VMEM((lrows, 9 * cl), BF),
            pltpu.VMEM((lrows, cl), F32),
        ],
        cots + [pooled, late_slope, wback],
        "late_back",
    )
    pd_other = turned(pooled_delta, "rep", 1)
    back_other = turned(back, "chan", 1)
    (late,) = call(
        functools.partial(late_grad_kernel, dims=(lx, ly, lz), scale=scale),
        [sds((27 * 128, cl), BF)],
        [
            pltpu.VMEM((lx, lplane + 16, 128), F32),
            pltpu.VMEM((2 * lrows, 9 * 128), BF),
            pltpu.VMEM((2 * lrows, 3 * cl), BF),
        ],
        [pooled_delta, pd_other],
        "late_grad",
    )
    half_other, wcat, _, late = lax.optimization_barrier((half_other, wcat, back, late))
    col, far_slope = call(
        functools.partial(other_kernel, dims=dims),
        [sds((rows, 9 * 128), BF), sds((hrows, 128), F32)],
        [pltpu.VMEM((2, gx, brows + 32, 128), F32), pltpu.VMEM((hrows, 3 * 128), F32)],
        [half, half_other, wcat],
        "other",
    )
    back_mine, late = lax.optimization_barrier((back_mine, late))
    part, win, late, left = call(
        functools.partial(early_grad_kernel, dims=dims),
        [
            sds((3 * EARLY_TAPS * 128, 128), BF),
            sds((bx + 2, brows + 32, 128), F32),
            sds(late.shape, BF),
            sds((3 * 128, rows), BF),
        ],
        [
            pltpu.VMEM((lx * ly * gz, 128), F32),
            pltpu.VMEM((gx + 2, plane + 32, 128), F32),
            pltpu.SemaphoreType.DMA(()),
        ],
        [back_mine, back_other, slope, far_slope, patch, col, late],
        "early_grad",
        away=(2,),
    )
    part_other = turned(part, "rep", 1)
    (more,) = call(more_kernel, [sds((3 * (9 - EARLY_TAPS) * 128, 128), BF)], [], [left, col], "more")
    more_other = turned(more, "rep", 1)
    win, _ = lax.optimization_barrier((win, more))
    (gv,) = call(
        functools.partial(grad_volume_kernel, bx=bx, brows=brows, gz=gz),
        [sds((bx * brows, 128), BF)],
        [pltpu.VMEM(((bx + 2) * brows, 9 * 128), BF)],
        [win, wt],
        "grad_volume",
        far=(0,),
    )
    (early,) = call(
        functools.partial(finish_kernel, scale=scale),
        [sds((27 * 128, 128), BF)],
        [pltpu.VMEM((27 * 128, 128), BF), pltpu.SemaphoreType.DMA((3,))],
        [part, part_other, more, more_other],
        "finish",
        away=(0,),
    )
    return (
        early.reshape(3, 3, 3, 128, 128),
        late.reshape(3, 3, 3, 128, cl),
        gv.reshape(1, bx, by, gz, 128),
    )


def solution(mesh):
    few = mesh.shape["space"] * mesh.shape["chan"] <= GATHER_BLOCKS
    alone = mesh.shape["rep"] == 2 and mesh.shape["chan"] == 2
    return jax.shard_map(
        whole_sample if few and alone else per_device,
        mesh=mesh,
        in_specs=(
            P(("groups", "rep"), "space", "chan", None, None),
            P(),
            P(None, None, None, None, "chan"),
            P(("groups", "rep"), "space", None, None, "chan"),
        ),
        out_specs=(
            P("groups", None, None, None, None),
            P("groups", None, None, None, "chan"),
            P(("groups", "rep"), "space", "chan", None, None),
        ),
        check_vma=False,
    )
```

```python
import functools
import math

import jax
import jax.numpy as jnp
from jax import lax
from jax.experimental import pallas as pl
from jax.experimental.pallas import tpu as pltpu
from jax.sharding import PartitionSpec as P

BF = jnp.bfloat16
F32 = jnp.float32
VMEM_BYTES = 14 * 2**20
GATHER_BLOCKS = 8
EARLY_TAPS = 7


def padded_2(block, sides, width):
    for axis, dim in sides:
        count = lax.axis_size(axis)
        forward = [(i, i + 1) for i in range(count - 1)]
        backward = [(target, source) for source, target in forward]
        low = lax.ppermute(
            lax.slice_in_dim(block, block.shape[dim] - width, None, axis=dim), axis, forward
        )
        high = lax.ppermute(lax.slice_in_dim(block, 0, width, axis=dim), axis, backward)
        block = jnp.concatenate([low, block, high], axis=dim)
    return block


def gelu_tanh(value):
    return jax.nn.gelu(value, approximate=True)


def conv_padded(padded, weight):
    depth = padded.shape[1] - 2
    height = padded.shape[2] - 2
    length = padded.shape[3] - 2
    total = None
    for first in range(3):
        for second in range(3):
            for third in range(3):
                window = padded[
                    :, first : first + depth, second : second + height, third : third + length
                ]
                term = jnp.einsum(
                    "sxyzc,co->sxyzo",
                    window,
                    weight[first, second, third],
                    preferred_element_type=jnp.float32,
                )
                total = term if total is None else total + term
    return total


def kernel_grad(padded, delta):
    depth = delta.shape[1]
    height = delta.shape[2]
    length = delta.shape[3]
    planes = []
    for first in range(3):
        for second in range(3):
            for third in range(3):
                window = padded[
                    :, first : first + depth, second : second + height, third : third + length
                ]
                planes.append(
                    jnp.einsum("sxyzc,sxyzo->co", window, delta, preferred_element_type=jnp.float32)
                )
    stacked = jnp.stack(planes, axis=0)
    return stacked.reshape((3, 3, 3) + stacked.shape[1:])


def flipped(weight):
    return jnp.swapaxes(weight[::-1, ::-1, ::-1], 3, 4)


def pad_dims(field, dims):
    widths = [(1, 1) if place in dims else (0, 0) for place in range(field.ndim)]
    return jnp.pad(field, widths)


def pool_cells(field):
    s, x, y, z, c = field.shape
    return jnp.mean(field.reshape(s, x // 2, 2, y // 2, 2, z // 2, 2, c), axis=(2, 4, 6))


def spread_cells(field):
    s, x, y, z, c = field.shape
    wide = jnp.broadcast_to(field[:, :, None, :, None, :, None, :], (s, x, 2, y, 2, z, 2, c))
    return wide.reshape(s, 2 * x, 2 * y, 2 * z, c) * 0.125


def late_layer(joined, late_weight, cotangent):
    rim = padded_2(joined, (("space", 1),), 1)
    late_pad = pad_dims(rim, (2, 3))
    pre_late = conv_padded(late_pad, late_weight)
    delta_late = jax.vjp(gelu_tanh, pre_late)[1](cotangent.astype(jnp.float32))[0].astype(
        jnp.bfloat16
    )
    late_part = kernel_grad(late_pad, delta_late)
    delta_rim = padded_2(delta_late, (("space", 1),), 1)
    back_partial = conv_padded(pad_dims(delta_rim, (2, 3)), flipped(late_weight))
    return (back_partial, late_part)


def per_device(volume, early_weight, late_weight, cotangent):
    count = (
        cotangent.shape[0]
        * lax.axis_size("rep")
        * cotangent.shape[1]
        * lax.axis_size("space")
        * cotangent.shape[2]
        * cotangent.shape[3]
    )
    scale = 1.0 / math.sqrt(count)
    haloed = padded_2(volume, (("space", 1), ("chan", 2)), 1)
    padded_in = pad_dims(haloed, (3,))
    pre_early = conv_padded(padded_in, early_weight)
    pooled = pool_cells(gelu_tanh(pre_early)).astype(jnp.bfloat16)
    joined = lax.all_gather(pooled, "chan", axis=2, tiled=True)
    back_partial, late_part = late_layer(joined, late_weight, cotangent)
    back_rows = lax.psum_scatter(back_partial, "chan", scatter_dimension=2, tiled=True)
    delta_early = jax.vjp(gelu_tanh, pre_early)[1](spread_cells(back_rows))[0].astype(jnp.bfloat16)
    early_part = kernel_grad(padded_in, delta_early)
    delta_halo = padded_2(delta_early, (("space", 1), ("chan", 2)), 1)
    grad_volume = conv_padded(pad_dims(delta_halo, (3,)), flipped(early_weight)).astype(
        jnp.bfloat16
    )
    early_total = lax.psum(early_part, ("space", "chan", "rep"))
    grad_early = (early_total * scale).astype(jnp.bfloat16)
    late_total = lax.psum(late_part, ("space", "rep"))
    grad_late = (late_total * scale).astype(jnp.bfloat16)
    return (grad_early, grad_late, grad_volume)


NT = (((1,), (1,)), ((), ()))


def gelu_and_slope(v):
    k = 0.7978845608028654
    sq = v * v
    t = jnp.tanh(k * (v + 0.044715 * (v * sq)))
    half = 0.5 * (1.0 + t)
    return v * half, half + 0.5 * v * (1.0 - t * t) * (k * (1.0 + 0.134145 * sq))


def depth_of(rows, period):
    return lax.broadcasted_iota(jnp.int32, (rows, 128), 0) % period


def shifted(ref, lead, start, rows, cell, period, step):
    dy, dz = step
    got = ref[lead + (pl.ds(start + dy * period + dz, rows), slice(None))]
    if dz == 0:
        return got
    lanes = got.shape[1] // 128
    edge = (cell == 0) if dz < 0 else (cell == period - 1)
    edge = jnp.concatenate([edge] * lanes, axis=1) if lanes > 1 else edge
    return jnp.where(edge, 0.0, got)


STEPS = [(b, c) for b in (-1, 0, 1) for c in (-1, 0, 1)]


def fold(parts, rows):
    zero = jnp.zeros((rows, parts[0].shape[1]), F32)
    return (
        parts[1]
        + jnp.concatenate([zero, parts[0][:-rows]], axis=0)
        + jnp.concatenate([parts[2][rows:], zero], axis=0)
    )


def begin_kernel(own_hbm, we_hbm, own_ref, we_ref, wcat_ref, sems):
    own = pltpu.make_async_copy(own_hbm, own_ref, sems.at[3])
    copies = [pltpu.make_async_copy(we_hbm.at[a], we_ref.at[a], sems.at[a]) for a in range(3)]
    for copy in (*copies, own):
        copy.start()
    for a in range(3):
        copies[a].wait()
        for n in range(9):
            b, c = divmod(n, 3)
            wcat_ref[pl.ds(n * 128, 128), pl.ds(a * 128, 128)] = we_ref[a, b, c]
    own.wait()


def early_kernel(*refs, nk, dims):
    gx, gy, gz, lx, ly, lz, bx, by = dims
    blocks, refs = refs[:nk], refs[nk:]
    wcat_ref, half_ref, slope_ref, send_ref, edge_ref = refs[:5]
    vol_ref, col_ref, p_ref, pre_ref, h_ref, row_ref = refs[5:]
    k, j = lax.axis_index("space"), lax.axis_index("chan")
    brows, hl, line = by * gz, by // 2 * lz, gx * gz
    vol_ref[:, pl.ds(0, 16), :] = jnp.zeros((gx, 16, 128), F32)
    vol_ref[:, pl.ds(16 + brows, 16), :] = jnp.zeros((gx, 16, 128), F32)
    for n, dk in enumerate([0, *steps_of(nk)]):
        src = blocks[n]
        kk = partner(k, dk, nk)
        for q in range(bx):
            got = src[pl.ds(q * brows, brows), :]
            vol_ref[kk * bx + q, pl.ds(16, brows), :] = got.astype(F32)
            half_ref[pl.ds(pl.multiple_of((kk * bx + q) * brows, brows), brows), :] = got

    cell = depth_of(brows, gz)
    for x in range(gx):
        for n, step in enumerate(STEPS):
            col_ref[pl.ds(x * brows, brows), pl.ds(n * 128, 128)] = shifted(
                vol_ref, (x,), 16, brows, cell, gz, step
            ).astype(BF)

    p_ref[...] = jnp.dot(col_ref[...], wcat_ref[...], preferred_element_type=F32)

    outer = pl.multiple_of((brows - gz) * (1 - j), gz)
    inner = pl.multiple_of((brows - 2 * gz) * (1 - j) + gz * j, gz)
    for x in range(gx):
        row_ref[pl.ds(x * gz, gz), :] = vol_ref[x, pl.ds(16 + outer, gz), :]
    row = row_ref[...]
    rcell = depth_of(line, gz)
    trio = [
        jnp.where(rcell == 0, 0.0, pltpu.roll(row, 1, 0)),
        row,
        jnp.where(rcell == gz - 1, 0.0, pltpu.roll(row, line - 1, 0)),
    ]
    taps = wcat_ref[pl.ds(pl.multiple_of(j * (6 * 128), 128), 3 * 128), :]
    given = jnp.dot(jnp.concatenate(trio, axis=1).astype(BF), taps, preferred_element_type=F32)
    given = fold([given[:, a * 128 : (a + 1) * 128] for a in range(3)], gz)

    for lq in range(lx):
        pair = None
        for x in (2 * lq, 2 * lq + 1):
            pre = p_ref[pl.ds(x * brows, brows), pl.ds(128, 128)]
            if x > 0:
                pre = pre + p_ref[pl.ds((x - 1) * brows, brows), pl.ds(0, 128)]
            if x < gx - 1:
                pre = pre + p_ref[pl.ds((x + 1) * brows, brows), pl.ds(256, 128)]
            pre_ref[x] = pre
            h, slope = gelu_and_slope(pre)
            slope_ref[pl.ds(x * brows, brows), :] = slope
            pair = h if pair is None else pair + h
        wide = pair.reshape(by // 2, 2, gz, 128)
        h_ref[...] = (wide[:, 0] + wide[:, 1]).reshape(by // 2 * gz, 128)
        pooled = (h_ref[pl.ds(0, hl, stride=2), :] + h_ref[pl.ds(1, hl, stride=2), :]) * 0.125
        send_ref[pl.ds(lq * hl, hl), :] = pooled.astype(BF)
    for x in range(gx):
        edge_ref[pl.ds(x * gz, gz), :] = pre_ref[x, pl.ds(inner, gz), :]
        edge_ref[pl.ds(line + x * gz, gz), :] = pre_ref[x, pl.ds(outer, gz), :]
    edge_ref[pl.ds(2 * line, line), :] = given
    send_ref[pl.ds(lx * hl, 3 * line), :] = edge_ref[...].astype(BF)


def fetch_kernel(far_ref, we_ref, near_ref, back_ref, wt_ref, sems):
    copies = [pltpu.make_async_copy(far_ref.at[a], near_ref.at[a], sems.at[a]) for a in range(3)]
    cl = near_ref.shape[-1]
    for copy in copies:
        copy.start()
    for n in range(9):
        b, c = divmod(n, 3)
        for a in range(3):
            wt_ref[a, pl.ds(n * 128, 128), :] = we_ref[a, b, c].astype(F32).T.astype(BF)
    for a in range(3):
        copies[a].wait()
        for n in range(9):
            b, c = divmod(n, 3)
            back_ref[pl.ds(n * cl, cl), pl.ds(a * 128, 128)] = near_ref[a, b, c].astype(F32).T.astype(BF)


def border_pool(inner, outer, tmp_ref, tile_ref, dims):
    lx, lz, gz = dims
    h, slope = gelu_and_slope(outer)
    h = (h + gelu_and_slope(inner)[0]).reshape(lx, 2, gz, 128)
    tmp_ref[...] = (h[:, 0] + h[:, 1]).reshape(lx * gz, 128)
    got = (tmp_ref[pl.ds(0, lx * lz, stride=2), :] + tmp_ref[pl.ds(1, lx * lz, stride=2), :]) * 0.125
    got = got.astype(BF).astype(F32)
    for x in range(lx):
        for copy in range(2):
            tile_ref[pl.ds((2 * x + copy) * lz, lz), :] = got[x * lz : (x + 1) * lz]
    return slope


def late_kernel(
    sent_ref, got_ref, edge_ref, wl_ref, pooled_ref, slope_ref, patch_ref,
    pool_ref, lcol_ref, tmp_ref, tile_ref, *, dims
):
    gx, gz, lx, ly, lz = dims
    lplane, hl, line = ly * lz, ly // 2 * lz, gx * gz
    cl = wl_ref.shape[-1]
    j = lax.axis_index("chan")
    edges = got_ref[pl.ds(lx * hl, 3 * line), :].astype(F32)
    lrow = lax.broadcasted_iota(jnp.int32, (hl, 128), 0)
    for x in range(lx):
        pool_ref[x, pl.ds(0, 8), :] = jnp.zeros((8, 128), F32)
        pool_ref[x, pl.ds(8 + lplane, 8), :] = jnp.zeros((8, 128), F32)
    sides = (
        (j, sent_ref, edge_ref[pl.ds(0, line), :], edge_ref[pl.ds(line, line), :] + edges[2 * line :]),
        (1 - j, got_ref, edges[:line], edges[line : 2 * line] + edge_ref[pl.ds(2 * line, line), :]),
    )
    for n, (side, ref, inner, outer) in enumerate(sides):
        slope = border_pool(inner, outer, tmp_ref, tile_ref, (lx, lz, gz))
        if n == 0:
            patch_ref[...] = slope
        first = (hl - lz) * (1 - side)
        border = (lrow >= first) & (lrow < first + lz)
        for x in range(lx):
            tiles = jnp.concatenate([tile_ref[pl.ds(x * 2 * lz, 2 * lz), :]] * (hl // (2 * lz)), axis=0)
            start = pl.multiple_of(8 + side * hl, 8)
            pool_ref[x, pl.ds(start, hl), :] = jnp.where(
                border, tiles, ref[pl.ds(x * hl, hl), :].astype(F32)
            )
    for x in range(lx):
        pooled_ref[pl.ds(x * lplane, lplane), :] = pool_ref[x, pl.ds(8, lplane), :].astype(BF)

    lcell = depth_of(lplane, lz)
    for x in range(lx):
        for n, step in enumerate(STEPS):
            lcol_ref[pl.ds(x * lplane, lplane), pl.ds(n * 128, 128)] = shifted(
                pool_ref, (x,), 8, lplane, lcell, lz, step
            ).astype(BF)
    lcol = lcol_ref[...]
    parts = [
        jnp.dot(lcol, wl_ref[a].reshape(9 * 128, cl), preferred_element_type=F32) for a in range(3)
    ]
    pre = fold(parts, lplane)
    slope_ref[...] = gelu_and_slope(pre)[1]


def late_back_kernel(*refs, nk, dims):
    lx, ly, lz, cx = dims
    cots, refs = refs[:nk], refs[nk:]
    pooled_ref, slope_ref, wback_ref, pd_ref, back_ref, mine_ref, dl_ref, dcol_ref, cot_ref = refs
    lplane = ly * lz
    cl = slope_ref.shape[1]
    crow = cx * lplane
    k = lax.axis_index("space")
    for n, dk in enumerate([0, *steps_of(nk)]):
        start = pl.multiple_of(partner(k, dk, nk) * crow, 8)
        cot_ref[pl.ds(start, crow), :] = cots[n][...].astype(F32).reshape(crow, cl)
    pd_ref[:, pl.ds(0, 128)] = pooled_ref[...]
    pd_ref[:, pl.ds(128, cl)] = (cot_ref[...] * slope_ref[...]).astype(BF)
    lcell = depth_of(lplane, lz)
    for x in range(lx):
        dl_ref[x, pl.ds(0, 8), :] = jnp.zeros((8, cl), F32)
        dl_ref[x, pl.ds(8 + lplane, 8), :] = jnp.zeros((8, cl), F32)
        dl_ref[x, pl.ds(8, lplane), :] = pd_ref[pl.ds(x * lplane, lplane), pl.ds(128, cl)].astype(F32)
    for n, (b, c) in enumerate(STEPS):
        for x in range(lx):
            dcol_ref[pl.ds(x * lplane, lplane), pl.ds(n * cl, cl)] = shifted(
                dl_ref, (x,), 8, lplane, lcell, lz, (-b, -c)
            ).astype(BF)
    total = jnp.dot(dcol_ref[...], wback_ref[...], preferred_element_type=F32)
    back = fold([total[:, (2 - a) * 128 : (3 - a) * 128] for a in range(3)], lplane)
    back_ref[...] = back.astype(BF)
    mine_ref[...] = back


def late_grad_kernel(mine_ref, other_ref, out_ref, pool_ref, lcol_ref, wide_ref, *, dims, scale):
    lx, ly, lz = dims
    lplane = ly * lz
    rows = lx * lplane
    cl = mine_ref.shape[1] - 128
    lcell = depth_of(lplane, lz)
    for x in range(lx):
        pool_ref[x, pl.ds(0, 8), :] = jnp.zeros((8, 128), F32)
        pool_ref[x, pl.ds(8 + lplane, 8), :] = jnp.zeros((8, 128), F32)
    for s, ref in enumerate((mine_ref, other_ref)):
        for x in range(lx):
            pool_ref[x, pl.ds(8, lplane), :] = ref[pl.ds(x * lplane, lplane), pl.ds(0, 128)].astype(F32)
        for x in range(lx):
            for n, step in enumerate(STEPS):
                lcol_ref[pl.ds(s * rows + x * lplane, lplane), pl.ds(n * 128, 128)] = shifted(
                    pool_ref, (x,), 8, lplane, lcell, lz, step
                ).astype(BF)
        zero = jnp.zeros((lplane, cl), BF)
        wide_ref[pl.ds(s * rows + rows - lplane, lplane), pl.ds(0, cl)] = zero
        wide_ref[pl.ds(s * rows, rows - lplane), pl.ds(0, cl)] = ref[pl.ds(lplane, rows - lplane), pl.ds(128, cl)]
        wide_ref[pl.ds(s * rows, rows), pl.ds(cl, cl)] = ref[:, pl.ds(128, cl)]
        wide_ref[pl.ds(s * rows, lplane), pl.ds(2 * cl, cl)] = zero
        wide_ref[pl.ds(s * rows + lplane, rows - lplane), pl.ds(2 * cl, cl)] = ref[
            pl.ds(0, rows - lplane), pl.ds(128, cl)
        ]
    got = lax.dot_general(
        lcol_ref[...], wide_ref[...], (((0,), (0,)), ((), ())), preferred_element_type=F32
    )
    for a in range(3):
        out_ref[pl.ds(a * 9 * 128, 9 * 128), :] = (got[:, a * cl : (a + 1) * cl] * scale).astype(BF)


def other_kernel(
    half_ref, got_ref, wcat_ref, col_ref, slope_ref, vol_ref, p_ref, *, dims
):
    gx, gy, gz, lx, ly, lz, bx, by = dims
    brows = by * gz
    j = lax.axis_index("chan")
    vol_ref[:, :, pl.ds(0, 16), :] = jnp.zeros((2, gx, 16, 128), F32)
    vol_ref[:, :, pl.ds(16 + brows, 16), :] = jnp.zeros((2, gx, 16, 128), F32)
    for h, src in enumerate((half_ref, got_ref)):
        for x in range(gx):
            vol_ref[h, x, pl.ds(16, brows), :] = src[pl.ds(x * brows, brows), :].astype(F32)
    for h, side in enumerate((j, 1 - j)):
        into = pl.multiple_of((16 + brows) * (1 - side) + (16 - gz) * side, 8)
        start = pl.multiple_of(16 + (brows - gz) * side, 8)
        for x in range(gx):
            vol_ref[h, x, pl.ds(into, gz), :] = vol_ref[1 - h, x, pl.ds(start, gz), :]
    cell = depth_of(brows, gz)
    for h in (1, 0):
        for x in range(gx):
            for n, step in enumerate(STEPS):
                col_ref[pl.ds((h * gx + x) * brows, brows), pl.ds(n * 128, 128)] = shifted(
                    vol_ref, (h, x), 16, brows, cell, gz, step
                ).astype(BF)
    p_ref[...] = jnp.dot(
        col_ref[pl.ds(gx * brows, gx * brows), :], wcat_ref[...], preferred_element_type=F32
    )
    for x in range(gx):
        pre = p_ref[pl.ds(x * brows, brows), pl.ds(128, 128)]
        if x > 0:
            pre = pre + p_ref[pl.ds((x - 1) * brows, brows), pl.ds(0, 128)]
        if x < gx - 1:
            pre = pre + p_ref[pl.ds((x + 1) * brows, brows), pl.ds(256, 128)]
        slope_ref[pl.ds(x * brows, brows), :] = gelu_and_slope(pre)[1]


def tap_terms(left_ref, col_ref, part_ref, first, count):
    got = jnp.dot(left_ref[...], col_ref[:, pl.ds(first * 128, count * 128)], preferred_element_type=F32)
    for a in range(3):
        for n in range(count):
            part_ref[pl.ds((a * count + n) * 128, 128), :] = got[
                a * 128 : (a + 1) * 128, n * 128 : (n + 1) * 128
            ].T.astype(part_ref.dtype)


def more_kernel(left_ref, col_ref, part_ref):
    tap_terms(left_ref, col_ref, part_ref, EARLY_TAPS, 9 - EARLY_TAPS)


def finish_kernel(one_ref, one_got_ref, two_ref, two_got_ref, out_ref, sum_ref, sems, *, scale):
    copies = []
    for a in range(3):
        at = a * 9 * 128
        for mine_ref, got_ref, count in (
            (one_ref, one_got_ref, EARLY_TAPS), (two_ref, two_got_ref, 9 - EARLY_TAPS)
        ):
            rows = pl.ds(a * count * 128, count * 128)
            total = mine_ref[rows, :].astype(F32) + got_ref[rows, :].astype(F32)
            sum_ref[pl.ds(at, count * 128), :] = (total * scale).astype(BF)
            at += count * 128
        rows = pl.ds(a * 9 * 128, 9 * 128)
        copies.append(pltpu.make_async_copy(sum_ref.at[rows], out_ref.at[rows], sems.at[a]))
        copies[-1].start()
    for copy in copies:
        copy.wait()


def early_grad_kernel(
    mine_ref, other_ref, slope_ref, far_ref, patch_ref, col_ref, late_ref,
    part_ref, win_ref, out_ref, left_ref, wide_ref, d_ref, sem, *, dims
):
    leave = pltpu.make_async_copy(late_ref, out_ref, sem)
    leave.start()
    gx, gy, gz, lx, ly, lz, bx, by = dims
    plane, lplane = gy * gz, ly * lz
    k, j = lax.axis_index("space"), lax.axis_index("chan")
    brows = by * gz
    half = gx * brows
    for q in (0, gx + 1):
        d_ref[q] = jnp.zeros(d_ref.shape[1:], F32)
    d_ref[:, pl.ds(0, 16), :] = jnp.zeros((gx + 2, 16, 128), F32)
    d_ref[:, pl.ds(16 + plane, 16), :] = jnp.zeros((gx + 2, 16, 128), F32)
    for h in (0, 1):
        left_ref[pl.ds(0, 128), pl.ds((h + 1) * half - brows, brows)] = jnp.zeros((128, brows), BF)
        left_ref[pl.ds(2 * 128, 128), pl.ds(h * half, brows)] = jnp.zeros((128, brows), BF)
    back = (mine_ref[...] + other_ref[...].astype(F32)) * 0.125
    wide_ref[pl.ds(0, lx * lplane, stride=2), :] = back
    wide_ref[pl.ds(1, lx * lplane, stride=2), :] = back
    first = (brows - gz) * (1 - j)
    row = lax.broadcasted_iota(jnp.int32, (brows, 128), 0)
    border = (row >= first) & (row < first + gz)
    for lq in range(lx):
        for h, side in enumerate((j, 1 - j)):
            start = pl.multiple_of(lq * ly * gz + side * (by // 2 * gz), 8)
            rows = wide_ref[pl.ds(start, by // 2 * gz), :].reshape(by // 2, 1, gz, 128)
            rows = jnp.broadcast_to(rows, (by // 2, 2, gz, 128)).reshape(brows, 128)
            for x in (2 * lq, 2 * lq + 1):
                slope = (far_ref if h else slope_ref)[pl.ds(x * brows, brows), :]
                if h == 0:
                    tiles = jnp.concatenate([patch_ref[pl.ds(x * gz, gz), :]] * by, axis=0)
                    slope = jnp.where(border, tiles, slope)
                delta = (rows * slope).astype(BF).astype(F32)
                d_ref[x + 1, pl.ds(pl.multiple_of(16 + side * brows, 8), brows), :] = delta
                tile = delta.T.astype(BF)
                for a in range(3):
                    if 0 <= x + a - 1 < gx:
                        left_ref[pl.ds(a * 128, 128), pl.ds(h * half + (x + a - 1) * brows, brows)] = tile
    tap_terms(left_ref, col_ref, part_ref, 0, EARLY_TAPS)
    row = pl.multiple_of(j * brows, 8)
    for q in range(bx + 2):
        win_ref[q] = d_ref[k * bx + q, pl.ds(row, brows + 32), :]
    leave.wait()


def grad_volume_kernel(win_ref, wt_ref, gv_ref, vcol_ref, *, bx, brows, gz):
    cell = depth_of(brows, gz)
    for q in range(bx + 2):
        for n, (b, c) in enumerate(STEPS):
            vcol_ref[pl.ds(q * brows, brows), pl.ds(n * 128, 128)] = shifted(
                win_ref, (q,), 16, brows, cell, gz, (-b, -c)
            ).astype(BF)
    total = None
    for a in range(3):
        term = jnp.dot(vcol_ref[pl.ds((2 - a) * brows, bx * brows), :], wt_ref[a], preferred_element_type=F32)
        total = term if total is None else total + term
    gv_ref[...] = total.astype(BF)


def steps_of(count):
    return range(1, count)


def partner(index, by, count):
    if count & (count - 1) == 0:
        return index ^ by
    return lax.rem(index + count - by, count)


def turned(value, axis, by):
    count = lax.axis_size(axis)
    pairs = count & (count - 1) == 0
    return lax.ppermute(value, axis, [(i, i ^ by if pairs else (i + by) % count) for i in range(count)])


def call(kernel, outs, scratch, args, name, far=(), raw=(), away=()):
    args = [
        pltpu.with_memory_space_constraint(arg, pltpu.HBM if n in raw else pltpu.VMEM)
        for n, arg in enumerate(args)
    ]
    outs = [out if n in (*far, *away) else pltpu.VMEM(out.shape, out.dtype) for n, out in enumerate(outs)]
    return pl.pallas_call(
        kernel,
        out_shape=outs,
        in_specs=[
            pl.BlockSpec(memory_space=pltpu.HBM if n in raw else pltpu.VMEM) for n in range(len(args))
        ],
        out_specs=[
            pl.BlockSpec(memory_space=pltpu.HBM if n in away else pltpu.VMEM) for n in range(len(outs))
        ],
        scratch_shapes=scratch,
        compiler_params=pltpu.CompilerParams(vmem_limit_bytes=VMEM_BYTES),
        name=name,
    )(*args)


def whole_sample(volume, early_weight, late_weight, cotangent):
    nk, nj, nr = (lax.axis_size(axis) for axis in ("space", "chan", "rep"))
    _, bx, by, gz, _ = volume.shape
    _, cx, ly, lz, cl = cotangent.shape
    gx, gy, lx = bx * nk, by * nj, cx * nk
    plane, lplane, brows = gy * gz, ly * lz, by * gz
    rows, lrows = gx * plane, lx * lplane
    scale = 1.0 / math.sqrt(nr * lrows)
    sds = jax.ShapeDtypeStruct

    mine = volume.reshape(bx * brows, 128)
    line = [mine] + [turned(mine, "space", dk) for dk in steps_of(nk)]
    cot = cotangent.reshape(cx * ly, lz, cl)
    own, we, wcat = call(
        begin_kernel,
        [sds(mine.shape, BF), sds(early_weight.shape, BF), sds((9 * 128, 3 * 128), BF)],
        [pltpu.SemaphoreType.DMA((4,))],
        [mine, early_weight],
        "begin",
        raw=(0, 1),
    )
    line[0] = own
    late_steps = [dk for dk in range(1, nk) if nk & (nk - 1) == 0 and dk & (dk - 1)]
    cots = {dk: turned(cot, "space", dk) for dk in steps_of(nk) if dk not in late_steps}

    dims = (gx, gy, gz, lx, ly, lz, bx, by)
    hrows, edge = gx * brows, 3 * gx * gz
    half, slope, send, edges = call(
        functools.partial(early_kernel, nk=nk, dims=dims),
        [
            sds((hrows, 128), BF),
            sds((hrows, 128), F32),
            sds((lrows // 2 + edge, 128), BF),
            sds((edge, 128), F32),
        ],
        [
            pltpu.VMEM((gx, brows + 32, 128), F32),
            pltpu.VMEM((hrows, 9 * 128), BF),
            pltpu.VMEM((hrows, 3 * 128), F32),
            pltpu.VMEM((gx, brows, 128), F32),
            pltpu.VMEM((by // 2 * gz, 128), F32),
            pltpu.VMEM((gx * gz, 128), F32),
        ],
        line + [wcat],
        "early",
    )
    ready, cots = lax.optimization_barrier((send, cots))
    send_other = turned(ready, "chan", 1)
    half_other = turned(half, "chan", 1)
    for dk in late_steps:
        low = dk & -dk
        cots[dk] = turned(cots[dk ^ low], "space", low)
    cots = [cot] + [cots[dk] for dk in steps_of(nk)]
    held, _ = lax.optimization_barrier((late_weight, send))
    wl, wback, wt = call(
        fetch_kernel,
        [sds(late_weight.shape, BF), sds((9 * cl, 3 * 128), BF), sds((3, 9 * 128, 128), BF)],
        [pltpu.SemaphoreType.DMA((3,))],
        [held, we],
        "fetch",
        raw=(0,),
    )
    pooled, late_slope, patch = call(
        functools.partial(late_kernel, dims=(gx, gz, lx, ly, lz)),
        [sds((lrows, 128), BF), sds((lrows, cl), F32), sds((gx * gz, 128), F32)],
        [
            pltpu.VMEM((lx, lplane + 16, 128), F32),
            pltpu.VMEM((lrows, 9 * 128), BF),
            pltpu.VMEM((lx * gz, 128), F32),
            pltpu.VMEM((lx * 2 * lz, 128), F32),
        ],
        [send, send_other, edges, wl],
        "late",
    )
    pooled_delta, back, back_mine = call(
        functools.partial(late_back_kernel, nk=nk, dims=(lx, ly, lz, cx)),
        [sds((lrows, 128 + cl), BF), sds((lrows, 128), BF), sds((lrows, 128), F32)],
        [
            pltpu.VMEM((lx, lplane + 16, cl), F32),
            pltpu.VMEM((lrows, 9 * cl), BF),
            pltpu.VMEM((lrows, cl), F32),
        ],
        cots + [pooled, late_slope, wback],
        "late_back",
    )
    pd_other = turned(pooled_delta, "rep", 1)
    back_other = turned(back, "chan", 1)
    (late,) = call(
        functools.partial(late_grad_kernel, dims=(lx, ly, lz), scale=scale),
        [sds((27 * 128, cl), BF)],
        [
            pltpu.VMEM((lx, lplane + 16, 128), F32),
            pltpu.VMEM((2 * lrows, 9 * 128), BF),
            pltpu.VMEM((2 * lrows, 3 * cl), BF),
        ],
        [pooled_delta, pd_other],
        "late_grad",
    )
    half_other, wcat, _, late = lax.optimization_barrier((half_other, wcat, back, late))
    col, far_slope = call(
        functools.partial(other_kernel, dims=dims),
        [sds((rows, 9 * 128), BF), sds((hrows, 128), F32)],
        [pltpu.VMEM((2, gx, brows + 32, 128), F32), pltpu.VMEM((hrows, 3 * 128), F32)],
        [half, half_other, wcat],
        "other",
    )
    back_mine, late = lax.optimization_barrier((back_mine, late))
    part, win, late, left = call(
        functools.partial(early_grad_kernel, dims=dims),
        [
            sds((3 * EARLY_TAPS * 128, 128), BF),
            sds((bx + 2, brows + 32, 128), F32),
            sds(late.shape, BF),
            sds((3 * 128, rows), BF),
        ],
        [
            pltpu.VMEM((lx * ly * gz, 128), F32),
            pltpu.VMEM((gx + 2, plane + 32, 128), F32),
            pltpu.SemaphoreType.DMA(()),
        ],
        [back_mine, back_other, slope, far_slope, patch, col, late],
        "early_grad",
        away=(2,),
    )
    part_other = turned(part, "rep", 1)
    (more,) = call(more_kernel, [sds((3 * (9 - EARLY_TAPS) * 128, 128), BF)], [], [left, col], "more")
    more_other = turned(more, "rep", 1)
    win, _ = lax.optimization_barrier((win, more))
    (gv,) = call(
        functools.partial(grad_volume_kernel, bx=bx, brows=brows, gz=gz),
        [sds((bx * brows, 128), BF)],
        [pltpu.VMEM(((bx + 2) * brows, 9 * 128), BF)],
        [win, wt],
        "grad_volume",
        far=(0,),
    )
    (early,) = call(
        functools.partial(finish_kernel, scale=scale),
        [sds((27 * 128, 128), BF)],
        [pltpu.VMEM((27 * 128, 128), BF), pltpu.SemaphoreType.DMA((3,))],
        [part, part_other, more, more_other],
        "finish",
        away=(0,),
    )
    return (
        early.reshape(3, 3, 3, 128, 128),
        late.reshape(3, 3, 3, 128, cl),
        gv.reshape(1, bx, by, gz, 128),
    )


def solution(mesh):
    few = mesh.shape["space"] * mesh.shape["chan"] <= GATHER_BLOCKS
    alone = mesh.shape["rep"] == 2 and mesh.shape["chan"] == 2
    return jax.shard_map(
        whole_sample if few and alone else per_device,
        mesh=mesh,
        in_specs=(
            P(("groups", "rep"), "space", "chan", None, None),
            P(),
            P(None, None, None, None, "chan"),
            P(("groups", "rep"), "space", None, None, "chan"),
        ),
        out_specs=(
            P("groups", None, None, None, None),
            P("groups", None, None, None, "chan"),
            P(("groups", "rep"), "space", "chan", None, None),
        ),
        check_vma=False,
    )
```
